128 devices in a mesh: com: 32 (over x, y, core), arc: 4 (over z).
Axes of the slice: x: 4, y: 4, z: 4, core: 2. Of those that a mesh axis runs over, the one named last changes fastest.
Arguments:
- flow_start: float32 [1024, 65536], P('com', 'arc'), may hold values from 0 to 1
- price_start: float32 [1024, 16384], P('com'), may hold values from -3 to 3
- cost: float32 [1024, 65536], P('com', 'arc'), may hold values from -6 to 6
- demand: float32 [1024, 16384], P('com'), may hold values from -6 to 6
- head_block: int32 [512], P('arc'), may hold values from 0 to 127
- tail_block: int32 [512], P('arc'), may hold values from 0 to 127
- head_local: int32 [65536], P('arc'), may hold values from 0 to 127
- tail_local: int32 [65536], P('arc'), may hold values from 0 to 127
- cap_class: int32 [65536], P('arc'), may hold values from 0 to 7
- cap_levels: float32 [8], replicated, may hold values from 102 to 512
Outputs:
- flow: float32 [1024, 65536], P('com', 'arc')
- price: float32 [1024, 16384], P('com')
The draws below stay inside these ranges and needn't reach their ends.
Inputs may be any that keep to these rules, and one draw needn't show every extreme that they name: `head_block`: node block indices. `tail_block`: node block indices. `head_local`: positions within a node block. `tail_local`: positions within a node block.
All inputs are finite; a program needn't handle non-finite values.
Results may differ from the reference program's by a relative error of at most 0.00016.
Values sent between devices are 32-bit elements; how exact they have to be, the bound alone decides.
No kernel may reach another device: no remote copies, remote signals or barrier semaphores. Data moves between devices by JAX's collectives and lax.ppermute only.
A program may use at most 128 MiB of HBM per device.

```python
import math
import jax
import jax.numpy as jnp

NODES = 16384
BLOCK = 128
CLASSES = 8
ITERS = 4
NEWTON = 3
COMMODITIES = 1024
ARCS = 65536
ARC_BLOCKS = 512
NODE_BLOCKS = 128


def set_ends(result, key, low, largest):
    longest = result.shape.index(max(result.shape))
    spots = []
    for shift in (0, 1):
        where = [jax.random.randint(jax.random.fold_in(key, axis), (), 0, length) for axis, length in enumerate(result.shape)]
        where[longest] = (where[longest] + shift) % result.shape[longest]
        spots.append(tuple(where))
    return result.at[spots[0]].set(low).at[spots[1]].set(largest)


def shard_levels(key, extent, shards, low, largest):
    def one(dim, blocks):
        heights = jax.random.uniform(jax.random.fold_in(jax.random.fold_in(key, 6), dim), (blocks,), jnp.float32, low / len(shards), largest / len(shards))
        return jnp.repeat(jnp.exp(heights), extent[dim] // blocks).reshape((-1,) + (1,) * (len(extent) - dim - 1))

    factor_of = one(*shards[0])
    for cut in shards[1:]:
        factor_of = factor_of * one(*cut)
    return factor_of


def noise(own_key, shape, width, reach, cuts=(), held_as=jnp.bfloat16):
    result = jax.random.normal(own_key, shape, jnp.float32) * width
    if len(cuts) > 0:
        result = shard_levels(own_key, shape, cuts, -0.22, 0.18) * result
    return jnp.clip(result, min=-reach, max=reach).astype(held_as)


def setup_inputs(seed: int = 0) -> dict:
    keys = jax.random.split(jax.random.key(seed), 11)
    return {
        "flow_start": jnp.clip(1.0 * jax.random.uniform(keys[0], (COMMODITIES, ARCS), jnp.float32) ** shard_levels(keys[0], (COMMODITIES, ARCS), ((0, 32), (1, 4)), -0.2, 0.2), 0.0, 1.0),
        "price_start": noise(keys[1], (COMMODITIES, NODES), 0.5, 3.0, ((0, 32),), jnp.float32),
        "cost": noise(keys[2], (COMMODITIES, ARCS), 1.0, 6.0, ((0, 32), (1, 4)), jnp.float32),
        "demand": noise(keys[3], (COMMODITIES, NODES), 1.0, 6.0, ((0, 32),), jnp.float32),
        "head_block": set_ends(jax.random.randint(keys[4], (ARC_BLOCKS,), 0, NODE_BLOCKS), jax.random.fold_in(keys[4], 1), 0, NODE_BLOCKS - 1).astype(jnp.int32),
        "tail_block": set_ends(jax.random.randint(keys[5], (ARC_BLOCKS,), 0, NODE_BLOCKS), jax.random.fold_in(keys[5], 1), 0, NODE_BLOCKS - 1).astype(jnp.int32),
        "head_local": set_ends(jax.random.randint(keys[6], (ARCS,), 0, BLOCK), jax.random.fold_in(keys[6], 1), 0, BLOCK - 1).astype(jnp.int32),
        "tail_local": set_ends(jax.random.randint(keys[7], (ARCS,), 0, BLOCK), jax.random.fold_in(keys[7], 1), 0, BLOCK - 1).astype(jnp.int32),
        "cap_class": set_ends(jax.random.randint(keys[8], (ARCS,), 0, CLASSES), jax.random.fold_in(keys[8], 1), 0, CLASSES - 1).astype(jnp.int32),
        "cap_levels": jnp.clip(jnp.exp(jax.random.uniform(keys[9], (CLASSES,), jnp.float32, math.log(102.0), math.log(512.0))), 102.0, 512.0),
    }


step_primal = 0.25
step_dual = 0.1
soft_width = 0.05


def reference(flow_start, price_start, cost, demand, head_block, tail_block, head_local, tail_local, cap_class, cap_levels):
    heads = (jnp.repeat(head_block, BLOCK) * BLOCK + head_local).astype(jnp.int32)
    tails = (jnp.repeat(tail_block, BLOCK) * BLOCK + tail_local).astype(jnp.int32)
    capacity = cap_levels[cap_class]
    flow = flow_start
    price = price_start
    for step in range(ITERS):
        trial = flow - step_primal * (cost - (price[:, heads] - price[:, tails]))
        theta = jnp.zeros((trial.shape[1],), jnp.float32)
        for inner in range(NEWTON):
            excess = jnp.maximum(trial - theta, 0.0)
            total = jnp.sum(excess, axis=0)
            active = jnp.sum(jnp.minimum(excess / soft_width, 1.0), axis=0)
            theta = theta + jnp.maximum(total - capacity, 0.0) / jnp.maximum(active, 1.0)
        fresh = jnp.maximum(trial - theta, 0.0)
        extra = (2.0 * fresh - flow).T
        balance = jax.ops.segment_sum(extra, heads, NODES) - jax.ops.segment_sum(extra, tails, NODES)
        price = price + step_dual * (demand - balance.T)
        flow = fresh
    return flow, price
```

```python
import functools

import jax
import jax.numpy as jnp
from jax import lax
from jax.experimental import pallas as pl
from jax.experimental.pallas import tpu as pltpu
from jax.sharding import PartitionSpec as P

NODES = 16384
BLOCK = 128
ITERS = 4
NEWTON = 3

step_primal = 0.25
step_dual = 0.1
soft_width = 0.05

SHARDS = 4
OWNERS = 32
OWN = 512
QUADS = OWN // BLOCK
UNROLL = 2
LIMIT = 48 << 20

f32 = jnp.float32
bf16 = jnp.bfloat16
vmem = pl.BlockSpec(memory_space=pltpu.VMEM)
smem = pl.BlockSpec(memory_space=pltpu.SMEM)
params = pltpu.CompilerParams(vmem_limit_bytes=LIMIT)


def node_slice(block):
    return pl.ds(pl.multiple_of(block * BLOCK, BLOCK), BLOCK)


def arc_slice(start, piece):
    return pl.ds(pl.multiple_of(start + piece * BLOCK, BLOCK), BLOCK)


def gather_kernel(head_block, tail_block, head_local, tail_local, price, flow, cost, trial):
    for shard in range(SHARDS):

        def step(o, carry):
            for u in range(UNROLL):
                owner = o * UNROLL + u
                start = owner * OWN
                for q in range(QUADS):
                    j = (shard * OWNERS + owner) * QUADS + q
                    head = jnp.broadcast_to(head_local[pl.ds(j, 1), :], (8, BLOCK))
                    tail = jnp.broadcast_to(tail_local[pl.ds(j, 1), :], (8, BLOCK))
                    at_head = jnp.take_along_axis(price[:, node_slice(head_block[j])], head, axis=1)
                    at_tail = jnp.take_along_axis(price[:, node_slice(tail_block[j])], tail, axis=1)
                    where = arc_slice(start, q)
                    trial[shard * OWNERS + owner, :, q * BLOCK : (q + 1) * BLOCK] = flow[
                        shard, :, where
                    ] - step_primal * (cost[shard, :, where] - (at_head - at_tail))
            return carry

        lax.fori_loop(0, OWNERS // UNROLL, step, 0)


def project_kernel(levels, classes, values, theta_out):
    cls = classes[...]
    capacity = jnp.zeros((QUADS, BLOCK), f32)
    for k in range(8):
        capacity = jnp.where(cls == k, levels[k], capacity)
    caps = [capacity[q : q + 1] for q in range(QUADS)]
    thetas = [jnp.zeros((1, BLOCK), f32) for q in range(QUADS)]
    groups = values.shape[0]
    for inner in range(NEWTON):
        wide = [jnp.broadcast_to(t, (8, BLOCK)) for t in thetas]

        def step(o, carry):
            out = list(carry)
            for u in range(8):
                for q in range(QUADS):
                    excess = jnp.maximum(values[o * 8 + u, :, q * BLOCK : (q + 1) * BLOCK] - wide[q], 0.0)
                    out[2 * q] = out[2 * q] + excess
                    out[2 * q + 1] = out[2 * q + 1] + jnp.minimum(excess * (1.0 / soft_width), 1.0)
            return tuple(out)

        sums = lax.fori_loop(0, groups // 8, step, tuple(jnp.zeros((8, BLOCK), f32) for _ in range(2 * QUADS)))
        for q in range(QUADS):
            total = jnp.sum(sums[2 * q], axis=0, keepdims=True)
            active = jnp.sum(sums[2 * q + 1], axis=0, keepdims=True)
            thetas[q] = thetas[q] + jnp.maximum(total - caps[q], 0.0) / jnp.maximum(active, 1.0)
    tile = jnp.concatenate(thetas, axis=0)

    def store(i, carry):
        theta_out[i] = tile
        return carry

    lax.fori_loop(0, theta_out.shape[0], store, 0, unroll=8)


def scatter_kernel(
    head_block, tail_block, head_local, tail_local, trial, theta, flow, price, demand, fresh_out, price_out, balance
):
    balance[...] = jnp.zeros_like(balance)
    lanes = lax.broadcasted_iota(jnp.int32, (BLOCK, BLOCK), 0).astype(jnp.int16)
    one = jnp.ones((), bf16)
    zero = jnp.zeros((), bf16)

    def table(local):
        return jnp.where(lanes == jnp.broadcast_to(local.astype(jnp.int16), (BLOCK, BLOCK)), one, zero)

    for shard in range(SHARDS):

        def step(o, carry):
            found = []
            for u in range(UNROLL):
                owner = o * UNROLL + u
                start = owner * OWN
                for q in range(QUADS):
                    j = (shard * OWNERS + owner) * QUADS + q
                    where = arc_slice(start, q)
                    limit = theta[shard * OWNERS + owner, q : q + 1, :]
                    fresh = jnp.maximum(
                        trial[shard * OWNERS + owner, :, q * BLOCK : (q + 1) * BLOCK] - limit, 0.0
                    )
                    fresh_out[shard, :, where] = fresh
                    extra = 2.0 * fresh - flow[shard, :, where]
                    high = extra.astype(bf16)
                    low = (extra - high.astype(f32)).astype(bf16)
                    both = jnp.concatenate([high, low], axis=0)
                    tables = jnp.concatenate(
                        [table(head_local[pl.ds(j, 1), :]), table(tail_local[pl.ds(j, 1), :])], axis=0
                    )
                    sums = lax.dot_general(both, tables, (((1,), (1,)), ((), ())), preferred_element_type=f32)
                    found.append((j, sums[:8] + sums[8:]))
            for j, sums in found:
                balance[:, node_slice(head_block[j])] += sums[:, :BLOCK]
                balance[:, node_slice(tail_block[j])] -= sums[:, BLOCK:]
            return carry

        lax.fori_loop(0, OWNERS // UNROLL, step, 0)
    price_out[...] = price[...] + step_dual * (demand[...] - balance[...])


def gather(tables, price, flow, cost):
    return pl.pallas_call(
        gather_kernel,
        in_specs=[smem, smem] + [vmem] * 5,
        out_specs=vmem,
        out_shape=jax.ShapeDtypeStruct((SHARDS * OWNERS, 8, OWN), f32),
        compiler_params=params,
        name="arc_trial",
    )(*tables, price, flow, cost)


def project(levels, classes, values, receivers):
    return pl.pallas_call(
        project_kernel,
        in_specs=[smem, vmem, vmem],
        out_specs=vmem,
        out_shape=jax.ShapeDtypeStruct((receivers, QUADS, BLOCK), f32),
        compiler_params=params,
        name="project",
    )(levels, classes, values)


def scatter(tables, trial, theta, flow, price, demand):
    return pl.pallas_call(
        scatter_kernel,
        in_specs=[smem, smem] + [vmem] * 7,
        out_specs=[vmem, vmem],
        out_shape=[
            jax.ShapeDtypeStruct((SHARDS, 8, OWNERS * OWN), f32),
            jax.ShapeDtypeStruct((8, NODES), f32),
        ],
        scratch_shapes=[pltpu.VMEM((8, NODES), f32)],
        compiler_params=params,
        name="balance",
    )(*tables, trial, theta, flow, price, demand)


def on_device(
    flow_start,
    price_start,
    cost,
    demand,
    head_block,
    tail_block,
    head_local,
    tail_local,
    cap_class,
    cap_levels,
):
    com_rows, arc_cols = flow_start.shape
    part = lax.axis_index("arc")
    place = lax.axis_index("com")
    blocks = arc_cols // BLOCK

    packed = jnp.concatenate(
        [
            head_local.reshape(blocks, BLOCK),
            tail_local.reshape(blocks, BLOCK),
            head_block.reshape(1, BLOCK),
            tail_block.reshape(1, BLOCK),
            jnp.zeros((6, BLOCK), jnp.int32),
        ],
        axis=0,
    )
    every = lax.all_gather(packed, "arc", axis=0)
    tables = (
        every[:, 2 * blocks].reshape(SHARDS * blocks),
        every[:, 2 * blocks + 1].reshape(SHARDS * blocks),
        every[:, :blocks].reshape(SHARDS * blocks, BLOCK),
        every[:, blocks : 2 * blocks].reshape(SHARDS * blocks, BLOCK),
    )
    classes = lax.dynamic_slice(cap_class.reshape(blocks, BLOCK), (place * QUADS, 0), (QUADS, BLOCK))

    def spread(values):
        return lax.all_to_all(values.reshape(SHARDS, 8, arc_cols), "arc", split_axis=0, concat_axis=0, tiled=True)

    flow = spread(flow_start)
    unit_cost = spread(cost)
    price = lax.dynamic_slice(price_start, (part * 8, 0), (8, NODES))
    wanted = lax.dynamic_slice(demand, (part * 8, 0), (8, NODES))
    both = ("arc", "com")
    for step in range(ITERS):
        trial = gather(tables, price, flow, unit_cost)
        values = lax.all_to_all(trial, both, split_axis=0, concat_axis=0, tiled=True)
        theta = project(cap_levels, classes, values, SHARDS * OWNERS)
        theta = lax.all_to_all(theta, both, split_axis=0, concat_axis=0, tiled=True)
        flow, price = scatter(tables, trial, theta, flow, price, wanted)
    out = spread(flow).reshape(com_rows, arc_cols)
    return out, lax.all_gather(price, "arc", axis=0, tiled=True)


def solution(mesh):
    return jax.shard_map(
        on_device,
        mesh=mesh,
        in_specs=(
            P("com", "arc"),
            P("com", None),
            P("com", "arc"),
            P("com", None),
            P("arc"),
            P("arc"),
            P("arc"),
            P("arc"),
            P("arc"),
            P(),
        ),
        out_specs=(P("com", "arc"), P("com", None)),
        check_vma=False,
    )
```

```python
import functools

import jax
import jax.numpy as jnp
from jax import lax
from jax.experimental import pallas as pl
from jax.experimental.pallas import tpu as pltpu
from jax.sharding import PartitionSpec as P

NODES = 16384
BLOCK = 128
ITERS = 4
NEWTON = 3

step_primal = 0.25
step_dual = 0.1
soft_width = 0.05

SHARDS = 4
OWNERS = 32
OWN = 512
QUADS = OWN // BLOCK
CHUNK = 4096
UNROLL = 8
LIMIT = 48 << 20

f32 = jnp.float32
bf16 = jnp.bfloat16
vmem = pl.BlockSpec(memory_space=pltpu.VMEM)
smem = pl.BlockSpec(memory_space=pltpu.SMEM)
params = pltpu.CompilerParams(vmem_limit_bytes=LIMIT)


def node_slice(block):
    return pl.ds(pl.multiple_of(block * BLOCK, BLOCK), BLOCK)


def arc_slice(start, piece):
    return pl.ds(pl.multiple_of(start + piece * BLOCK, BLOCK), BLOCK)


def own_trial_kernel(head_block, tail_block, head_local, tail_local, price, flow, cost, trial):
    first = pl.program_id(1) * (CHUNK // BLOCK)
    for i in range(CHUNK // BLOCK):
        j = first + i
        head = jnp.broadcast_to(head_local[pl.ds(j, 1), :], (8, BLOCK))
        tail = jnp.broadcast_to(tail_local[pl.ds(j, 1), :], (8, BLOCK))
        at_head = jnp.take_along_axis(price[:, node_slice(head_block[j])], head, axis=1)
        at_tail = jnp.take_along_axis(price[:, node_slice(tail_block[j])], tail, axis=1)
        q = i % QUADS
        where = slice(i * BLOCK, (i + 1) * BLOCK)
        trial[i // QUADS, :, q * BLOCK : (q + 1) * BLOCK] = flow[:, where] - step_primal * (
            cost[:, where] - (at_head - at_tail)
        )


def gather_kernel(part, blocks, *refs):
    locals_, price, flow, cost, trial = refs[:4], refs[4], refs[5:9], refs[9:13], refs[13]
    for k in range(SHARDS):
        shard = (part[0] - k) & (SHARDS - 1)

        def step(o, carry):
            for u in range(UNROLL):
                owner = o * UNROLL + u
                start = owner * OWN
                for q in range(QUADS):
                    j = owner * QUADS + q
                    head = jnp.broadcast_to(locals_[k][pl.ds(j, 1), :], (8, BLOCK))
                    tail = jnp.broadcast_to(locals_[k][pl.ds(BLOCK + j, 1), :], (8, BLOCK))
                    at_head = jnp.take_along_axis(price[:, node_slice(blocks[2 * k, j])], head, axis=1)
                    at_tail = jnp.take_along_axis(price[:, node_slice(blocks[2 * k + 1, j])], tail, axis=1)
                    where = arc_slice(start, q)
                    trial[owner * SHARDS + shard, :, q * BLOCK : (q + 1) * BLOCK] = flow[k][
                        :, where
                    ] - step_primal * (cost[k][:, where] - (at_head - at_tail))
            return carry

        lax.fori_loop(0, OWNERS // UNROLL, step, 0)


def project_kernel(levels, classes, values, theta_out, *fresh_out):
    cls = classes[...]
    capacity = jnp.zeros((QUADS, BLOCK), f32)
    for k in range(8):
        capacity = jnp.where(cls == k, levels[k], capacity)
    caps = [capacity[q : q + 1] for q in range(QUADS)]
    thetas = [jnp.zeros((1, BLOCK), f32) for q in range(QUADS)]
    groups = values.shape[0]
    for inner in range(NEWTON):
        wide = [jnp.broadcast_to(t, (8, BLOCK)) for t in thetas]

        def step(o, carry):
            out = list(carry)
            for u in range(8):
                for q in range(QUADS):
                    excess = jnp.maximum(values[o * 8 + u, :, q * BLOCK : (q + 1) * BLOCK] - wide[q], 0.0)
                    out[2 * q] = out[2 * q] + excess
                    out[2 * q + 1] = out[2 * q + 1] + jnp.minimum(excess * (1.0 / soft_width), 1.0)
            return tuple(out)

        sums = lax.fori_loop(0, groups // 8, step, tuple(jnp.zeros((8, BLOCK), f32) for _ in range(2 * QUADS)))
        for q in range(QUADS):
            total = jnp.sum(sums[2 * q], axis=0, keepdims=True)
            active = jnp.sum(sums[2 * q + 1], axis=0, keepdims=True)
            thetas[q] = thetas[q] + jnp.maximum(total - caps[q], 0.0) / jnp.maximum(active, 1.0)
    tile = jnp.concatenate(thetas, axis=0)

    def store(i, carry):
        theta_out[i] = tile
        return carry

    lax.fori_loop(0, theta_out.shape[0], store, 0, unroll=8)
    if fresh_out:
        wide = [jnp.broadcast_to(t, (8, BLOCK)) for t in thetas]

        def keep(o, carry):
            for u in range(8):
                for q in range(QUADS):
                    where = slice(q * BLOCK, (q + 1) * BLOCK)
                    fresh_out[0][o * 8 + u, :, where] = jnp.maximum(values[o * 8 + u, :, where] - wide[q], 0.0)
            return carry

        lax.fori_loop(0, groups // 8, keep, 0)


def scatter_kernel(part, blocks, *refs, last):
    locals_, trial, theta, flow, price, demand = refs[:4], refs[4], refs[5], refs[6:10], refs[10], refs[11]
    fresh_out, price_out, balance = refs[12:-2], refs[-2], refs[-1]
    balance[...] = jnp.zeros_like(balance)
    lanes = lax.broadcasted_iota(jnp.int32, (BLOCK, BLOCK), 0).astype(jnp.int16)
    one = jnp.ones((), bf16)
    zero = jnp.zeros((), bf16)

    def table(local):
        return jnp.where(lanes == jnp.broadcast_to(local.astype(jnp.int16), (BLOCK, BLOCK)), one, zero)

    for k in range(SHARDS):
        shard = (part[0] - k) & (SHARDS - 1)

        def step(o, carry):
            found = []
            for u in range(UNROLL):
                owner = o * UNROLL + u
                start = owner * OWN
                for q in range(QUADS):
                    j = owner * QUADS + q
                    where = arc_slice(start, q)
                    limit = theta[owner * SHARDS + shard, q : q + 1, :]
                    fresh = jnp.maximum(
                        trial[owner * SHARDS + shard, :, q * BLOCK : (q + 1) * BLOCK] - limit, 0.0
                    )
                    if not last:
                        fresh_out[k][:, where] = fresh
                    extra = 2.0 * fresh - flow[k][:, where]
                    high = extra.astype(bf16)
                    low = (extra - high.astype(f32)).astype(bf16)
                    both = jnp.concatenate([high, low], axis=0)
                    tables = jnp.concatenate(
                        [table(locals_[k][pl.ds(j, 1), :]), table(locals_[k][pl.ds(BLOCK + j, 1), :])], axis=0
                    )
                    sums = lax.dot_general(both, tables, (((1,), (1,)), ((), ())), preferred_element_type=f32)
                    found.append((j, sums[:8] + sums[8:]))
            for j, sums in found:
                balance[:, node_slice(blocks[2 * k, j])] += sums[:, :BLOCK]
                balance[:, node_slice(blocks[2 * k + 1, j])] -= sums[:, BLOCK:]
            return carry

        lax.fori_loop(0, OWNERS // UNROLL, step, 0)
    price_out[...] = price[...] + step_dual * (demand[...] - balance[...])


def own_trial(head_block, tail_block, head_local, tail_local, price, flow, cost):
    whole = pl.BlockSpec((BLOCK, BLOCK), lambda r, c: (0, 0))
    return pl.pallas_call(
        own_trial_kernel,
        grid=(SHARDS, OWNERS * OWN // CHUNK),
        in_specs=[
            smem,
            smem,
            whole,
            whole,
            pl.BlockSpec((8, NODES), lambda r, c: (r, 0)),
            pl.BlockSpec((8, CHUNK), lambda r, c: (r, c)),
            pl.BlockSpec((8, CHUNK), lambda r, c: (r, c)),
        ],
        out_specs=pl.BlockSpec((CHUNK // OWN, 8, OWN), lambda r, c: (c, r, 0)),
        out_shape=jax.ShapeDtypeStruct((OWNERS, SHARDS * 8, OWN), f32),
        compiler_params=params,
        name="own_trial",
    )(head_block, tail_block, head_local, tail_local, price, flow, cost)


def gather(part, blocks, locals_, price, flow, cost):
    return pl.pallas_call(
        gather_kernel,
        in_specs=[smem, smem] + [vmem] * 13,
        out_specs=vmem,
        out_shape=jax.ShapeDtypeStruct((OWNERS * SHARDS, 8, OWN), f32),
        compiler_params=params,
        name="trial",
    )(part, blocks, *locals_, price, *flow, *cost)


def project(levels, classes, values, last):
    shape = [jax.ShapeDtypeStruct((SHARDS * OWNERS, QUADS, BLOCK), f32)]
    if last:
        shape.append(jax.ShapeDtypeStruct(values.shape, f32))
    return pl.pallas_call(
        project_kernel,
        in_specs=[smem, vmem, vmem],
        out_specs=[vmem] * len(shape),
        out_shape=shape,
        compiler_params=params,
        name="project",
    )(levels, classes, values)


def scatter(part, blocks, locals_, trial, theta, flow, price, demand, last):
    shape = [] if last else [jax.ShapeDtypeStruct((8, OWNERS * OWN), f32)] * SHARDS
    shape = shape + [jax.ShapeDtypeStruct((8, NODES), f32)]
    out = pl.pallas_call(
        functools.partial(scatter_kernel, last=last),
        in_specs=[smem, smem] + [vmem] * 12,
        out_specs=[vmem] * len(shape),
        out_shape=shape,
        scratch_shapes=[pltpu.VMEM((8, NODES), f32)],
        compiler_params=params,
        name="balance",
    )(part, blocks, *locals_, trial, theta, *flow, price, demand)
    return list(out[:-1]), out[-1]


def on_device(
    flow_start,
    price_start,
    cost,
    demand,
    head_block,
    tail_block,
    head_local,
    tail_local,
    cap_class,
    cap_levels,
):
    com_rows, arc_cols = flow_start.shape
    part = lax.axis_index("arc")
    place = lax.axis_index("com")
    blocks = arc_cols // BLOCK
    head_rows = head_local.reshape(blocks, BLOCK)
    tail_rows = tail_local.reshape(blocks, BLOCK)
    everyone = ("com", "arc")

    def exchange(values, axes):
        return lax.all_to_all(values, axes, split_axis=0, concat_axis=0, tiled=True)

    def around(values, k):
        return lax.ppermute(values, "arc", [(i, (i + k) % SHARDS) for i in range(SHARDS)])

    def rows_of(values, k):
        return lax.dynamic_slice(values, (((part + k) & (SHARDS - 1)) * 8, 0), (8, values.shape[1]))

    def slots(values):
        return [rows_of(values, 0)] + [around(rows_of(values, k), k) for k in range(1, SHARDS)]

    first = own_trial(head_block, tail_block, head_rows, tail_rows, price_start, flow_start, cost)
    values = exchange(first, "com").reshape(OWNERS * SHARDS, 8, OWN)

    packed = jnp.concatenate(
        [
            head_rows,
            tail_rows,
            head_block.reshape(1, BLOCK),
            tail_block.reshape(1, BLOCK),
            jnp.zeros((6, BLOCK), jnp.int32),
        ],
        axis=0,
    )
    locals_ = [packed] + [around(packed, k) for k in range(1, SHARDS)]
    block_ids = jnp.concatenate([x[2 * blocks : 2 * blocks + 2] for x in locals_], axis=0)
    flow = slots(flow_start)
    unit_cost = slots(cost)
    price = rows_of(price_start, 0)
    wanted = rows_of(demand, 0)
    classes = lax.dynamic_slice(cap_class.reshape(blocks, BLOCK), (place * QUADS, 0), (QUADS, BLOCK))
    own = part.astype(jnp.int32).reshape(1)

    for step in range(ITERS):
        last = step == ITERS - 1
        trial = gather(own, block_ids, locals_, price, flow, unit_cost)
        if step > 0:
            values = exchange(trial, everyone)
        theta, *kept = project(cap_levels, classes, values, last)
        theta = exchange(theta, everyone)
        flow, price = scatter(own, block_ids, locals_, trial, theta, flow, price, wanted, last)
    back = exchange(kept[0].reshape(OWNERS, com_rows, OWN), "com")
    out = back.transpose(1, 0, 2).reshape(com_rows, arc_cols)
    return out, lax.all_gather(price, "arc", axis=0, tiled=True)


def solution(mesh):
    return jax.shard_map(
        on_device,
        mesh=mesh,
        in_specs=(
            P("com", "arc"),
            P("com", None),
            P("com", "arc"),
            P("com", None),
            P("arc"),
            P("arc"),
            P("arc"),
            P("arc"),
            P("arc"),
            P(),
        ),
        out_specs=(P("com", "arc"), P("com", None)),
        check_vma=False,
    )
```

```python
import functools

import jax
import jax.numpy as jnp
from jax import lax
from jax.experimental import pallas as pl
from jax.experimental.pallas import tpu as pltpu
from jax.sharding import PartitionSpec as P

NODES = 16384
BLOCK = 128
ITERS = 4
NEWTON = 3

step_primal = 0.25
step_dual = 0.1
soft_width = 0.05

SHARDS = 4
OWNERS = 32
OWN = 512
QUADS = OWN // BLOCK
CHUNK = 8192
UNROLL = 8
COVER = 40_000_000

f32 = jnp.float32
bf16 = jnp.bfloat16
vmem = pl.BlockSpec(memory_space=pltpu.VMEM)
smem = pl.BlockSpec(memory_space=pltpu.SMEM)


def params(mib):
    return pltpu.CompilerParams(vmem_limit_bytes=mib << 20)


def node_slice(block):
    return pl.ds(pl.multiple_of(block * BLOCK, BLOCK), BLOCK)


def arc_slice(start, piece):
    return pl.ds(pl.multiple_of(start + piece * BLOCK, BLOCK), BLOCK)


def own_trial_kernel(head_block, tail_block, head_local, tail_local, price, flow, cost, trial):
    first = pl.program_id(1) * (CHUNK // BLOCK)

    def step(o, carry):
        for i in range(UNROLL * QUADS):
            owner = o * UNROLL + i // QUADS
            q = i % QUADS
            j = first + owner * QUADS + q
            head = jnp.broadcast_to(head_local[pl.ds(j, 1), :], (8, BLOCK))
            tail = jnp.broadcast_to(tail_local[pl.ds(j, 1), :], (8, BLOCK))
            at_head = jnp.take_along_axis(price[:, node_slice(head_block[j])], head, axis=1)
            at_tail = jnp.take_along_axis(price[:, node_slice(tail_block[j])], tail, axis=1)
            where = arc_slice(owner * OWN, q)
            trial[owner, :, q * BLOCK : (q + 1) * BLOCK] = flow[:, where] - step_primal * (
                cost[:, where] - (at_head - at_tail)
            )
        return carry

    lax.fori_loop(0, CHUNK // OWN // UNROLL, step, 0)


def gather_kernel(part, blocks, *refs):
    fill_trial(part, blocks, refs[:4], refs[4], refs[5:9], refs[9:13], refs[13])


def fill_trial(part, blocks, locals_, price, flow, cost, trial):
    for k in range(SHARDS):
        shard = (part[0] - k) & (SHARDS - 1)

        def step(o, carry):
            for u in range(UNROLL):
                owner = o * UNROLL + u
                start = owner * OWN
                for q in range(QUADS):
                    j = owner * QUADS + q
                    head = jnp.broadcast_to(locals_[k][pl.ds(j, 1), :], (8, BLOCK))
                    tail = jnp.broadcast_to(locals_[k][pl.ds(BLOCK + j, 1), :], (8, BLOCK))
                    at_head = jnp.take_along_axis(price[:, node_slice(blocks[2 * k, j])], head, axis=1)
                    at_tail = jnp.take_along_axis(price[:, node_slice(blocks[2 * k + 1, j])], tail, axis=1)
                    where = arc_slice(start, q)
                    trial[owner * SHARDS + shard, :, q * BLOCK : (q + 1) * BLOCK] = flow[k][
                        :, where
                    ] - step_primal * (cost[k][:, where] - (at_head - at_tail))
            return carry

        lax.fori_loop(0, OWNERS // UNROLL, step, 0)


def project_kernel(levels, classes, values, theta_out, *fresh_out):
    cls = classes[...]
    capacity = jnp.zeros((QUADS, BLOCK), f32)
    for k in range(8):
        capacity = jnp.where(cls == k, levels[k], capacity)
    caps = [capacity[q : q + 1] for q in range(QUADS)]
    thetas = [jnp.zeros((1, BLOCK), f32) for q in range(QUADS)]
    groups = values.shape[0]
    for inner in range(NEWTON):
        wide = [jnp.broadcast_to(t, (8, BLOCK)) for t in thetas]

        def step(o, carry):
            out = list(carry)
            for u in range(8):
                for q in range(QUADS):
                    excess = jnp.maximum(values[o * 8 + u, :, q * BLOCK : (q + 1) * BLOCK] - wide[q], 0.0)
                    out[2 * q] = out[2 * q] + excess
                    out[2 * q + 1] = out[2 * q + 1] + jnp.minimum(excess * (1.0 / soft_width), 1.0)
            return tuple(out)

        sums = lax.fori_loop(0, groups // 8, step, tuple(jnp.zeros((8, BLOCK), f32) for _ in range(2 * QUADS)))
        for q in range(QUADS):
            total = jnp.sum(sums[2 * q], axis=0, keepdims=True)
            active = jnp.sum(sums[2 * q + 1], axis=0, keepdims=True)
            thetas[q] = thetas[q] + jnp.maximum(total - caps[q], 0.0) / jnp.maximum(active, 1.0)
    tile = jnp.concatenate(thetas, axis=0)

    def store(i, carry):
        theta_out[i] = tile
        return carry

    lax.fori_loop(0, theta_out.shape[0], store, 0, unroll=8)
    if fresh_out:
        wide = [jnp.broadcast_to(t, (8, BLOCK)) for t in thetas]

        def keep(o, carry):
            for u in range(8):
                for q in range(QUADS):
                    where = slice(q * BLOCK, (q + 1) * BLOCK)
                    fresh_out[0][o * 8 + u, :, where] = jnp.maximum(values[o * 8 + u, :, where] - wide[q], 0.0)
            return carry

        lax.fori_loop(0, groups // 8, keep, 0)


def step_kernel(part, blocks, *refs, last):
    locals_, trial, theta, flow, price, demand = refs[:4], refs[4], refs[5], refs[6:10], refs[10], refs[11]
    balance = refs[-1]
    if last:
        (price_out,) = refs[12:-1]
        fresh_out = cost = following = None
    else:
        cost, following, price_out, fresh_out = refs[12:16], refs[16], refs[17], refs[18:22]
    balance[...] = jnp.zeros_like(balance)
    lanes = lax.broadcasted_iota(jnp.int32, (BLOCK, BLOCK), 0).astype(jnp.int16)
    one = jnp.ones((), bf16)
    zero = jnp.zeros((), bf16)

    def table(local):
        return jnp.where(lanes == jnp.broadcast_to(local.astype(jnp.int16), (BLOCK, BLOCK)), one, zero)

    for k in range(SHARDS):
        shard = (part[0] - k) & (SHARDS - 1)

        def step(o, carry):
            found = []
            for u in range(UNROLL):
                owner = o * UNROLL + u
                start = owner * OWN
                for q in range(QUADS):
                    j = owner * QUADS + q
                    where = arc_slice(start, q)
                    limit = theta[owner * SHARDS + shard, q : q + 1, :]
                    fresh = jnp.maximum(
                        trial[owner * SHARDS + shard, :, q * BLOCK : (q + 1) * BLOCK] - limit, 0.0
                    )
                    if not last:
                        fresh_out[k][:, where] = fresh
                    extra = 2.0 * fresh - flow[k][:, where]
                    high = extra.astype(bf16)
                    low = (extra - high.astype(f32)).astype(bf16)
                    both = jnp.concatenate([high, low], axis=0)
                    tables = jnp.concatenate(
                        [table(locals_[k][pl.ds(j, 1), :]), table(locals_[k][pl.ds(BLOCK + j, 1), :])], axis=0
                    )
                    sums = lax.dot_general(both, tables, (((1,), (1,)), ((), ())), preferred_element_type=f32)
                    found.append((j, sums[:8] + sums[8:]))
            for j, sums in found:
                balance[:, node_slice(blocks[2 * k, j])] += sums[:, :BLOCK]
                balance[:, node_slice(blocks[2 * k + 1, j])] -= sums[:, BLOCK:]
            return carry

        lax.fori_loop(0, OWNERS // UNROLL, step, 0)
    price_out[...] = price[...] + step_dual * (demand[...] - balance[...])
    if not last:
        fill_trial(part, blocks, locals_, price_out, fresh_out, cost, following)


def own_trial(head_block, tail_block, head_local, tail_local, price, flow, cost):
    whole = pl.BlockSpec((BLOCK, BLOCK), lambda r, c: (0, 0))
    return pl.pallas_call(
        own_trial_kernel,
        grid=(SHARDS, OWNERS * OWN // CHUNK),
        in_specs=[
            smem,
            smem,
            whole,
            whole,
            pl.BlockSpec((8, NODES), lambda r, c: (r, 0)),
            pl.BlockSpec((8, CHUNK), lambda r, c: (r, c)),
            pl.BlockSpec((8, CHUNK), lambda r, c: (r, c)),
        ],
        out_specs=pl.BlockSpec((CHUNK // OWN, 8, OWN), lambda r, c: (c, r, 0)),
        out_shape=jax.ShapeDtypeStruct((OWNERS, SHARDS * 8, OWN), f32),
        compiler_params=params(8),
        name="own_trial",
    )(
        head_block,
        tail_block,
        head_local,
        tail_local,
        *in_hbm([price, flow, cost]),
    )


def gather(part, blocks, locals_, price, flow, cost):
    return pl.pallas_call(
        gather_kernel,
        in_specs=[smem, smem] + [vmem] * 13,
        out_specs=vmem,
        out_shape=jax.ShapeDtypeStruct((OWNERS * SHARDS, 8, OWN), f32),
        compiler_params=params(12),
        name="trial",
    )(part, blocks, *locals_, price, *flow, *cost)


def project(levels, classes, values, last):
    shape = [jax.ShapeDtypeStruct((SHARDS * OWNERS, QUADS, BLOCK), f32)]
    if last:
        shape.append(jax.ShapeDtypeStruct(values.shape, f32))
    return pl.pallas_call(
        project_kernel,
        in_specs=[smem, vmem, vmem],
        out_specs=[vmem] * len(shape),
        out_shape=shape,
        compiler_params=params(8),
        name="project",
    )(levels, classes, values)


def in_hbm(values):
    return [pltpu.with_memory_space_constraint(x, pltpu.HBM) for x in values]


def advance(part, blocks, locals_, trial, theta, flow, price, demand, cost, first, last):
    if first or last:
        trial, price, demand, *flow = in_hbm([trial, price, demand, *flow])
    shape = [jax.ShapeDtypeStruct((8, NODES), f32)]
    if not last:
        shape = [jax.ShapeDtypeStruct(trial.shape, f32)] + shape
        shape = shape + [jax.ShapeDtypeStruct((8, OWNERS * OWN), f32)] * SHARDS
    out = pl.pallas_call(
        functools.partial(step_kernel, last=last),
        in_specs=[smem, smem] + [vmem] * (12 if last else 16),
        out_specs=[vmem] * len(shape),
        out_shape=shape,
        scratch_shapes=[pltpu.VMEM((8, NODES), f32)],
        compiler_params=params(14),
        cost_estimate=pl.CostEstimate(flops=2 * 16 * 256 * OWNERS * OWN * SHARDS, transcendentals=0, bytes_accessed=COVER),
        name="step",
    )(part, blocks, *locals_, trial, theta, *flow, price, demand, *([] if last else cost))
    return (None, out[0], None) if last else (out[0], out[1], out[2:])


def assemble_kernel(part, *refs):
    near, left, right, far_left, far_right, out = refs
    half = NODES // 2

    def rows(k):
        return pl.ds(pl.multiple_of(((part[0] - k) & (SHARDS - 1)) * 8, 8), 8)

    out[rows(0), :] = near[...]
    out[rows(1), :] = left[...]
    out[rows(3), :] = right[...]
    out[rows(2), :half] = far_left[...]
    out[rows(2), half:] = far_right[...]


def assemble(part, *pieces):
    return pl.pallas_call(
        assemble_kernel,
        in_specs=[smem] + [vmem] * 5,
        out_specs=vmem,
        out_shape=jax.ShapeDtypeStruct((SHARDS * 8, NODES), f32),
        compiler_params=params(8),
        name="assemble",
    )(part, *pieces)


def on_device(
    flow_start,
    price_start,
    cost,
    demand,
    head_block,
    tail_block,
    head_local,
    tail_local,
    cap_class,
    cap_levels,
):
    com_rows, arc_cols = flow_start.shape
    part = lax.axis_index("arc")
    place = lax.axis_index("com")
    blocks = arc_cols // BLOCK
    head_rows = head_local.reshape(blocks, BLOCK)
    tail_rows = tail_local.reshape(blocks, BLOCK)
    everyone = ("com", "arc")

    def exchange(values, axes):
        return lax.all_to_all(values, axes, split_axis=0, concat_axis=0, tiled=True)

    def around(values, k):
        return lax.ppermute(values, "arc", [(i, (i + k) % SHARDS) for i in range(SHARDS)])

    def rows_of(values, k):
        return lax.dynamic_slice(values, (((part + k) & (SHARDS - 1)) * 8, 0), (8, values.shape[1]))

    def slots(values):
        return [rows_of(values, 0)] + [around(rows_of(values, k), k) for k in range(1, SHARDS)]

    first = own_trial(head_block, tail_block, head_rows, tail_rows, price_start, flow_start, cost)
    first, flow_start, cost, price_start, head_rows, tail_rows, head_block, tail_block = lax.optimization_barrier(
        (first, flow_start, cost, price_start, head_rows, tail_rows, head_block, tail_block)
    )
    values = exchange(first, "com").reshape(OWNERS * SHARDS, 8, OWN)

    flow = slots(flow_start)
    unit_cost = slots(cost)
    packed = jnp.concatenate(
        [
            head_rows,
            tail_rows,
            head_block.reshape(1, BLOCK),
            tail_block.reshape(1, BLOCK),
            jnp.zeros((6, BLOCK), jnp.int32),
        ],
        axis=0,
    )
    locals_ = [packed] + [around(packed, k) for k in range(1, SHARDS)]
    values, flow, locals_, unit_cost[1] = lax.optimization_barrier((values, flow, locals_, unit_cost[1]))
    block_ids = jnp.concatenate([x[2 * blocks : 2 * blocks + 2] for x in locals_], axis=0)
    price = rows_of(price_start, 0)
    wanted = rows_of(demand, 0)
    classes = lax.dynamic_slice(cap_class.reshape(blocks, BLOCK), (place * QUADS, 0), (QUADS, BLOCK))
    own = part.astype(jnp.int32).reshape(1)

    trial = gather(own, block_ids, locals_, price, flow, unit_cost)
    for step in range(ITERS):
        last = step == ITERS - 1
        if step > 0:
            values = exchange(trial, everyone)
        theta, *kept = project(cap_levels, classes, values, last)
        theta = exchange(theta, everyone)
        trial, price, flow = advance(own, block_ids, locals_, trial, theta, flow, price, wanted, unit_cost, step == 0, last)
    back = exchange(kept[0].reshape(OWNERS, com_rows, OWN), "com")
    out = back.transpose(1, 0, 2).reshape(com_rows, arc_cols)
    left = around(price, 1)
    right = around(price, 3)
    half = NODES // 2
    full = assemble(own, price, left, right, around(left[:, :half], 1), around(right[:, half:], 3))
    return out, full


def solution(mesh):
    return jax.shard_map(
        on_device,
        mesh=mesh,
        in_specs=(
            P("com", "arc"),
            P("com", None),
            P("com", "arc"),
            P("com", None),
            P("arc"),
            P("arc"),
            P("arc"),
            P("arc"),
            P("arc"),
            P(),
        ),
        out_specs=(P("com", "arc"), P("com", None)),
        check_vma=False,
    )
```

```python
import functools

import jax
import jax.numpy as jnp
from jax import lax
from jax.experimental import pallas as pl
from jax.experimental.pallas import tpu as pltpu
from jax.sharding import PartitionSpec as P

NODES = 16384
BLOCK = 128
ITERS = 4
NEWTON = 3

step_primal = 0.25
step_dual = 0.1
soft_width = 0.05

SHARDS = 4
OWNERS = 32
OWN = 512
QUADS = OWN // BLOCK
CHUNK = 8192
UNROLL = 8
COVER = 40_000_000

f32 = jnp.float32
bf16 = jnp.bfloat16
vmem = pl.BlockSpec(memory_space=pltpu.VMEM)
smem = pl.BlockSpec(memory_space=pltpu.SMEM)


def params(mib):
    return pltpu.CompilerParams(vmem_limit_bytes=mib << 20)


def node_slice(block):
    return pl.ds(pl.multiple_of(block * BLOCK, BLOCK), BLOCK)


def arc_slice(start, piece):
    return pl.ds(pl.multiple_of(start + piece * BLOCK, BLOCK), BLOCK)


def own_trial_kernel(head_block, tail_block, head_local, tail_local, price, flow, cost, trial):
    first = pl.program_id(1) * (CHUNK // BLOCK)

    def step(o, carry):
        for i in range(UNROLL * QUADS):
            owner = o * UNROLL + i // QUADS
            q = i % QUADS
            j = first + owner * QUADS + q
            head = jnp.broadcast_to(head_local[pl.ds(j, 1), :], (8, BLOCK))
            tail = jnp.broadcast_to(tail_local[pl.ds(j, 1), :], (8, BLOCK))
            at_head = jnp.take_along_axis(price[:, node_slice(head_block[j])], head, axis=1)
            at_tail = jnp.take_along_axis(price[:, node_slice(tail_block[j])], tail, axis=1)
            where = arc_slice(owner * OWN, q)
            trial[owner, :, q * BLOCK : (q + 1) * BLOCK] = flow[:, where] - step_primal * (
                cost[:, where] - (at_head - at_tail)
            )
        return carry

    lax.fori_loop(0, CHUNK // OWN // UNROLL, step, 0)


def gather_kernel(part, blocks, *refs):
    fill_trial(part, blocks, refs[:4], refs[4], refs[5:9], refs[5:9], refs[9])


def fill_trial(part, blocks, locals_, price, flow, cost, trial):
    for k in range(SHARDS):
        shard = (part[0] - k) & (SHARDS - 1)

        def step(o, carry):
            for u in range(UNROLL):
                owner = o * UNROLL + u
                start = owner * OWN
                for q in range(QUADS):
                    j = owner * QUADS + q
                    head = jnp.broadcast_to(locals_[k][pl.ds(j, 1), :], (8, BLOCK))
                    tail = jnp.broadcast_to(locals_[k][pl.ds(BLOCK + j, 1), :], (8, BLOCK))
                    at_head = jnp.take_along_axis(price[:, node_slice(blocks[2 * k, j])], head, axis=1)
                    at_tail = jnp.take_along_axis(price[:, node_slice(blocks[2 * k + 1, j])], tail, axis=1)
                    where = arc_slice(start, q)
                    trial[owner * SHARDS + shard, :, q * BLOCK : (q + 1) * BLOCK] = flow[k][
                        :8, where
                    ] - step_primal * (cost[k][8:, where] - (at_head - at_tail))
            return carry

        lax.fori_loop(0, OWNERS // UNROLL, step, 0)


def project_kernel(levels, classes, values, theta_out, *fresh_out):
    cls = classes[...]
    capacity = jnp.zeros((QUADS, BLOCK), f32)
    for k in range(8):
        capacity = jnp.where(cls == k, levels[k], capacity)
    caps = [capacity[q : q + 1] for q in range(QUADS)]
    thetas = [jnp.zeros((1, BLOCK), f32) for q in range(QUADS)]
    groups = values.shape[0]
    for inner in range(NEWTON):
        wide = [jnp.broadcast_to(t, (8, BLOCK)) for t in thetas]

        def step(o, carry):
            out = list(carry)
            for u in range(8):
                for q in range(QUADS):
                    excess = jnp.maximum(values[o * 8 + u, :, q * BLOCK : (q + 1) * BLOCK] - wide[q], 0.0)
                    out[2 * q] = out[2 * q] + excess
                    out[2 * q + 1] = out[2 * q + 1] + jnp.minimum(excess * (1.0 / soft_width), 1.0)
            return tuple(out)

        sums = lax.fori_loop(0, groups // 8, step, tuple(jnp.zeros((8, BLOCK), f32) for _ in range(2 * QUADS)))
        for q in range(QUADS):
            total = jnp.sum(sums[2 * q], axis=0, keepdims=True)
            active = jnp.sum(sums[2 * q + 1], axis=0, keepdims=True)
            thetas[q] = thetas[q] + jnp.maximum(total - caps[q], 0.0) / jnp.maximum(active, 1.0)
    tile = jnp.concatenate(thetas, axis=0)

    def store(i, carry):
        theta_out[i] = tile
        return carry

    lax.fori_loop(0, theta_out.shape[0], store, 0, unroll=8)
    if fresh_out:
        wide = [jnp.broadcast_to(t, (8, BLOCK)) for t in thetas]

        def keep(o, carry):
            for u in range(8):
                for q in range(QUADS):
                    where = slice(q * BLOCK, (q + 1) * BLOCK)
                    fresh_out[0][o * 8 + u, :, where] = jnp.maximum(values[o * 8 + u, :, where] - wide[q], 0.0)
            return carry

        lax.fori_loop(0, groups // 8, keep, 0)


def step_kernel(part, blocks, *refs, first, last):
    locals_, trial, theta, price, demand, flow = refs[:4], refs[4], refs[5], refs[6], refs[7], refs[8:12]
    balance = refs[-1]
    if last:
        price_out = refs[12]
        fresh_out = cost = following = None
    else:
        cost, rest = (flow, refs[12:]) if first else (refs[12:16], refs[16:])
        following, price_out, fresh_out = rest[0], rest[1], rest[2:6]
    balance[...] = jnp.zeros_like(balance)
    lanes = lax.broadcasted_iota(jnp.int32, (BLOCK, BLOCK), 0).astype(jnp.int16)
    one = jnp.ones((), bf16)
    zero = jnp.zeros((), bf16)

    def table(local):
        return jnp.where(lanes == jnp.broadcast_to(local.astype(jnp.int16), (BLOCK, BLOCK)), one, zero)

    for k in range(SHARDS):
        shard = (part[0] - k) & (SHARDS - 1)

        def step(o, carry):
            found = []
            for u in range(UNROLL):
                owner = o * UNROLL + u
                start = owner * OWN
                for q in range(QUADS):
                    j = owner * QUADS + q
                    where = arc_slice(start, q)
                    limit = theta[owner * SHARDS + shard, q : q + 1, :]
                    fresh = jnp.maximum(
                        trial[owner * SHARDS + shard, :, q * BLOCK : (q + 1) * BLOCK] - limit, 0.0
                    )
                    if not last:
                        fresh_out[k][:, where] = fresh
                    extra = 2.0 * fresh - flow[k][:8, where]
                    high = extra.astype(bf16)
                    low = (extra - high.astype(f32)).astype(bf16)
                    both = jnp.concatenate([high, low], axis=0)
                    tables = jnp.concatenate(
                        [table(locals_[k][pl.ds(j, 1), :]), table(locals_[k][pl.ds(BLOCK + j, 1), :])], axis=0
                    )
                    sums = lax.dot_general(both, tables, (((1,), (1,)), ((), ())), preferred_element_type=f32)
                    found.append((j, sums[:8] + sums[8:]))
            for j, sums in found:
                balance[:, node_slice(blocks[2 * k, j])] += sums[:, :BLOCK]
                balance[:, node_slice(blocks[2 * k + 1, j])] -= sums[:, BLOCK:]
            return carry

        lax.fori_loop(0, OWNERS // UNROLL, step, 0)
    price_out[...] = price[...] + step_dual * (demand[...] - balance[...])
    if not last:
        fill_trial(part, blocks, locals_, price_out, fresh_out, cost, following)


def pack_kernel(part, *refs):
    for k in range(SHARDS):
        refs[2 * SHARDS + k][:8] = refs[k][...]
        refs[2 * SHARDS + k][8:] = refs[SHARDS + k][...]


def pack(part, flow, cost):
    def rows(k):
        return pl.BlockSpec((8, CHUNK), lambda c, part: ((part[0] + k) & (SHARDS - 1), c))

    width = OWNERS * OWN
    return pl.pallas_call(
        pack_kernel,
        grid_spec=pltpu.PrefetchScalarGridSpec(
            num_scalar_prefetch=1,
            grid=(width // CHUNK,),
            in_specs=[rows(k) for k in range(SHARDS)] * 2,
            out_specs=[pl.BlockSpec((16, CHUNK), lambda c, part: (0, c))] * SHARDS,
        ),
        out_shape=[jax.ShapeDtypeStruct((16, width), f32)] * SHARDS,
        compiler_params=params(12),
        name="pack",
    )(part, *in_hbm([flow] * SHARDS + [cost] * SHARDS))


def own_trial(head_block, tail_block, head_local, tail_local, price, flow, cost):
    whole = pl.BlockSpec((BLOCK, BLOCK), lambda r, c: (0, 0))
    return pl.pallas_call(
        own_trial_kernel,
        grid=(SHARDS, OWNERS * OWN // CHUNK),
        in_specs=[
            smem,
            smem,
            whole,
            whole,
            pl.BlockSpec((8, NODES), lambda r, c: (r, 0)),
            pl.BlockSpec((8, CHUNK), lambda r, c: (r, c)),
            pl.BlockSpec((8, CHUNK), lambda r, c: (r, c)),
        ],
        out_specs=pl.BlockSpec((CHUNK // OWN, 8, OWN), lambda r, c: (c, r, 0)),
        out_shape=jax.ShapeDtypeStruct((OWNERS, SHARDS * 8, OWN), f32),
        compiler_params=params(8),
        name="own_trial",
    )(*in_hbm([head_block, tail_block, head_local, tail_local, price, flow, cost]))


def gather(part, blocks, locals_, price, flow_cost):
    return pl.pallas_call(
        gather_kernel,
        in_specs=[smem, smem] + [vmem] * 9,
        out_specs=vmem,
        out_shape=jax.ShapeDtypeStruct((OWNERS * SHARDS, 8, OWN), f32),
        compiler_params=params(12),
        name="trial",
    )(part, blocks, *locals_, price, *flow_cost)


def project(levels, classes, values, last):
    shape = [jax.ShapeDtypeStruct((SHARDS * OWNERS, QUADS, BLOCK), f32)]
    if last:
        shape.append(jax.ShapeDtypeStruct(values.shape, f32))
    return pl.pallas_call(
        project_kernel,
        in_specs=[smem, vmem, vmem],
        out_specs=[vmem] * len(shape),
        out_shape=shape,
        compiler_params=params(8),
        name="project",
    )(levels, classes, values)


def in_hbm(values):
    return [pltpu.with_memory_space_constraint(x, pltpu.HBM) for x in values]


def advance(part, blocks, locals_, trial, theta, flow, price, demand, flow_cost, first, last):
    if first or last:
        trial, price, demand, *flow = in_hbm([trial, price, demand, *flow])
    operands = [trial, theta, price, demand] + list(flow) + ([] if first or last else list(flow_cost))
    shape = [jax.ShapeDtypeStruct((8, NODES), f32)]
    if not last:
        shape = [jax.ShapeDtypeStruct(trial.shape, f32)] + shape
        shape = shape + [jax.ShapeDtypeStruct((8, OWNERS * OWN), f32)] * SHARDS
    out = pl.pallas_call(
        functools.partial(step_kernel, first=first, last=last),
        in_specs=[smem, smem] + [vmem] * (SHARDS + len(operands)),
        out_specs=[vmem] * len(shape),
        out_shape=shape,
        scratch_shapes=[pltpu.VMEM((8, NODES), f32)],
        compiler_params=params(14),
        cost_estimate=pl.CostEstimate(flops=2 * 16 * 256 * OWNERS * OWN * SHARDS, transcendentals=0, bytes_accessed=COVER),
        name="step",
    )(part, blocks, *locals_, *operands)
    return (None, out[0], None) if last else (out[0], out[1], out[2:])


def assemble_kernel(part, *refs):
    near, left, right, far_left, far_right, out = refs
    half = NODES // 2

    def rows(k):
        return pl.ds(pl.multiple_of(((part[0] - k) & (SHARDS - 1)) * 8, 8), 8)

    out[rows(0), :] = near[...]
    out[rows(1), :] = left[...]
    out[rows(3), :] = right[...]
    out[rows(2), :half] = far_left[...]
    out[rows(2), half:] = far_right[...]


def assemble(part, *pieces):
    return pl.pallas_call(
        assemble_kernel,
        in_specs=[smem] + [vmem] * 5,
        out_specs=vmem,
        out_shape=jax.ShapeDtypeStruct((SHARDS * 8, NODES), f32),
        compiler_params=params(8),
        name="assemble",
    )(part, *pieces)


def on_device(
    flow_start,
    price_start,
    cost,
    demand,
    head_block,
    tail_block,
    head_local,
    tail_local,
    cap_class,
    cap_levels,
):
    com_rows, arc_cols = flow_start.shape
    part = lax.axis_index("arc")
    place = lax.axis_index("com")
    blocks = arc_cols // BLOCK
    head_rows = head_local.reshape(blocks, BLOCK)
    tail_rows = tail_local.reshape(blocks, BLOCK)
    everyone = ("com", "arc")

    def exchange(values, axes):
        return lax.all_to_all(values, axes, split_axis=0, concat_axis=0, tiled=True)

    def around(values, k):
        return lax.ppermute(values, "arc", [(i, (i + k) % SHARDS) for i in range(SHARDS)])

    def rows_of(values, k):
        return lax.dynamic_slice(values, (((part + k) & (SHARDS - 1)) * 8, 0), (8, values.shape[1]))

    own = part.astype(jnp.int32).reshape(1)
    pairs = pack(own, flow_start, cost)
    pairs, flow_start, cost, price_start = lax.optimization_barrier((pairs, flow_start, cost, price_start))
    flow_cost = [pairs[0]] + [around(pairs[k], k) for k in (1, 3, 2)]
    flow_cost = [flow_cost[0], flow_cost[1], flow_cost[3], flow_cost[2]]
    first = own_trial(head_block, tail_block, head_rows, tail_rows, price_start, flow_start, cost)
    values = exchange(first, "com").reshape(OWNERS * SHARDS, 8, OWN)

    packed = jnp.concatenate(
        [
            head_rows,
            tail_rows,
            head_block.reshape(1, BLOCK),
            tail_block.reshape(1, BLOCK),
            jnp.zeros((6, BLOCK), jnp.int32),
        ],
        axis=0,
    )
    flow_cost[1], packed = lax.optimization_barrier((flow_cost[1], packed))
    locals_ = [packed] + [around(packed, k) for k in range(1, SHARDS)]
    values, locals_, flow_cost[1] = lax.optimization_barrier((values, locals_, flow_cost[1]))
    block_ids = jnp.concatenate([x[2 * blocks : 2 * blocks + 2] for x in locals_], axis=0)
    price = rows_of(price_start, 0)
    wanted = rows_of(demand, 0)
    classes = lax.dynamic_slice(cap_class.reshape(blocks, BLOCK), (place * QUADS, 0), (QUADS, BLOCK))

    trial = gather(own, block_ids, locals_, price, flow_cost)
    flow = flow_cost
    for step in range(ITERS):
        last = step == ITERS - 1
        if step > 0:
            values = exchange(trial, everyone)
        theta, *kept = project(cap_levels, classes, values, last)
        theta = exchange(theta, everyone)
        trial, price, flow = advance(own, block_ids, locals_, trial, theta, flow, price, wanted, flow_cost, step == 0, last)
    back = exchange(kept[0].reshape(OWNERS, com_rows, OWN), "com")
    out = back.transpose(1, 0, 2).reshape(com_rows, arc_cols)
    left = around(price, 1)
    right = around(price, 3)
    half = NODES // 2
    far_left = around(left[:, :half], 1)
    far_right = around(right[:, half:], 3)
    out, price = lax.optimization_barrier((out, price))
    return out, assemble(own, price, left, right, far_left, far_right)


def solution(mesh):
    return jax.shard_map(
        on_device,
        mesh=mesh,
        in_specs=(
            P("com", "arc"),
            P("com", None),
            P("com", "arc"),
            P("com", None),
            P("arc"),
            P("arc"),
            P("arc"),
            P("arc"),
            P("arc"),
            P(),
        ),
        out_specs=(P("com", "arc"), P("com", None)),
        check_vma=False,
    )
```

```python
import functools

import jax
import jax.numpy as jnp
from jax import lax
from jax.experimental import pallas as pl
from jax.experimental.pallas import tpu as pltpu
from jax.sharding import PartitionSpec as P

NODES = 16384
BLOCK = 128
ITERS = 4
NEWTON = 3

step_primal = 0.25
step_dual = 0.1
soft_width = 0.05

SHARDS = 4
OWNERS = 32
OWN = 512
QUADS = OWN // BLOCK
CHUNK = 8192
UNROLL = 8
COVER = 40_000_000

f32 = jnp.float32
bf16 = jnp.bfloat16
vmem = pl.BlockSpec(memory_space=pltpu.VMEM)
smem = pl.BlockSpec(memory_space=pltpu.SMEM)


def params(mib):
    return pltpu.CompilerParams(vmem_limit_bytes=mib << 20)


def node_slice(block):
    return pl.ds(pl.multiple_of(block * BLOCK, BLOCK), BLOCK)


def rows_at(view, where):
    ref, start = view
    return ref[start : start + 8, where]


def arc_slice(start, piece):
    return pl.ds(pl.multiple_of(start + piece * BLOCK, BLOCK), BLOCK)


def own_trial_kernel(head_block, tail_block, head_local, tail_local, price, flow, cost, trial):
    first = pl.program_id(1) * (CHUNK // BLOCK)

    def step(o, carry):
        for i in range(UNROLL * QUADS):
            owner = o * UNROLL + i // QUADS
            q = i % QUADS
            j = first + owner * QUADS + q
            head = jnp.broadcast_to(head_local[pl.ds(j, 1), :], (8, BLOCK))
            tail = jnp.broadcast_to(tail_local[pl.ds(j, 1), :], (8, BLOCK))
            at_head = jnp.take_along_axis(price[:, node_slice(head_block[j])], head, axis=1)
            at_tail = jnp.take_along_axis(price[:, node_slice(tail_block[j])], tail, axis=1)
            where = arc_slice(owner * OWN, q)
            trial[owner, :, q * BLOCK : (q + 1) * BLOCK] = flow[:, where] - step_primal * (
                cost[:, where] - (at_head - at_tail)
            )
        return carry

    lax.fori_loop(0, CHUNK // OWN // UNROLL, step, 0)


def gather_kernel(part, blocks, *refs):
    fill_trial(part, blocks, refs[:4], refs[4], flow_views(refs[5:10]), cost_views(refs[5:10]), refs[10])


def flow_views(pairs):
    return [(pairs[0], 0), (pairs[1], 0), (pairs[2], 0), (pairs[4], 0)]


def cost_views(pairs):
    return [(pairs[0], 8), (pairs[1], 8), (pairs[3], 0), (pairs[4], 8)]


def fill_trial(part, blocks, locals_, price, flow, cost, trial):
    for k in range(SHARDS):
        shard = (part[0] - k) & (SHARDS - 1)

        def step(o, carry):
            for u in range(UNROLL):
                owner = o * UNROLL + u
                start = owner * OWN
                for q in range(QUADS):
                    j = owner * QUADS + q
                    head = jnp.broadcast_to(locals_[k][pl.ds(j, 1), :], (8, BLOCK))
                    tail = jnp.broadcast_to(locals_[k][pl.ds(BLOCK + j, 1), :], (8, BLOCK))
                    at_head = jnp.take_along_axis(price[:, node_slice(blocks[2 * k, j])], head, axis=1)
                    at_tail = jnp.take_along_axis(price[:, node_slice(blocks[2 * k + 1, j])], tail, axis=1)
                    where = arc_slice(start, q)
                    trial[owner * SHARDS + shard, :, q * BLOCK : (q + 1) * BLOCK] = rows_at(
                        flow[k], where
                    ) - step_primal * (rows_at(cost[k], where) - (at_head - at_tail))
            return carry

        lax.fori_loop(0, OWNERS // UNROLL, step, 0)


def project_kernel(levels, classes, values, theta_out, *fresh_out):
    cls = classes[...]
    capacity = jnp.zeros((QUADS, BLOCK), f32)
    for k in range(8):
        capacity = jnp.where(cls == k, levels[k], capacity)
    caps = [capacity[q : q + 1] for q in range(QUADS)]
    thetas = [jnp.zeros((1, BLOCK), f32) for q in range(QUADS)]
    groups = values.shape[0]
    for inner in range(NEWTON):
        wide = [jnp.broadcast_to(t, (8, BLOCK)) for t in thetas]

        def step(o, carry):
            out = list(carry)
            for u in range(8):
                for q in range(QUADS):
                    excess = jnp.maximum(values[o * 8 + u, :, q * BLOCK : (q + 1) * BLOCK] - wide[q], 0.0)
                    out[2 * q] = out[2 * q] + excess
                    out[2 * q + 1] = out[2 * q + 1] + jnp.minimum(excess * (1.0 / soft_width), 1.0)
            return tuple(out)

        sums = lax.fori_loop(0, groups // 8, step, tuple(jnp.zeros((8, BLOCK), f32) for _ in range(2 * QUADS)))
        for q in range(QUADS):
            total = jnp.sum(sums[2 * q], axis=0, keepdims=True)
            active = jnp.sum(sums[2 * q + 1], axis=0, keepdims=True)
            thetas[q] = thetas[q] + jnp.maximum(total - caps[q], 0.0) / jnp.maximum(active, 1.0)
    tile = jnp.concatenate(thetas, axis=0)

    def store(i, carry):
        theta_out[i] = tile
        return carry

    lax.fori_loop(0, theta_out.shape[0], store, 0, unroll=8)
    if fresh_out:
        wide = [jnp.broadcast_to(t, (8, BLOCK)) for t in thetas]

        def keep(o, carry):
            for u in range(8):
                for q in range(QUADS):
                    where = slice(q * BLOCK, (q + 1) * BLOCK)
                    fresh_out[0][o * 8 + u, :, where] = jnp.maximum(values[o * 8 + u, :, where] - wide[q], 0.0)
            return carry

        lax.fori_loop(0, groups // 8, keep, 0)


def step_kernel(part, blocks, *refs, first, last):
    locals_, trial, theta, price, demand = refs[:4], refs[4], refs[5], refs[6], refs[7]
    balance, rest = refs[-1], refs[8:-1]
    if first:
        flow, cost, rest = flow_views(rest[:5]), cost_views(rest[:5]), rest[5:]
    else:
        flow, rest = [(ref, 0) for ref in rest[:SHARDS]], rest[SHARDS:]
        if not last:
            cost, rest = cost_views(rest[:5]), rest[5:]
    if last:
        price_out = rest[0]
    else:
        following, price_out, fresh_out = rest[0], rest[1], rest[2:6]
    balance[...] = jnp.zeros_like(balance)
    lanes = lax.broadcasted_iota(jnp.int32, (BLOCK, BLOCK), 0).astype(jnp.int16)
    one = jnp.ones((), bf16)
    zero = jnp.zeros((), bf16)

    def table(local):
        return jnp.where(lanes == jnp.broadcast_to(local.astype(jnp.int16), (BLOCK, BLOCK)), one, zero)

    for k in range(SHARDS):
        shard = (part[0] - k) & (SHARDS - 1)

        def step(o, carry):
            found = []
            for u in range(UNROLL):
                owner = o * UNROLL + u
                start = owner * OWN
                for q in range(QUADS):
                    j = owner * QUADS + q
                    where = arc_slice(start, q)
                    limit = theta[owner * SHARDS + shard, q : q + 1, :]
                    fresh = jnp.maximum(
                        trial[owner * SHARDS + shard, :, q * BLOCK : (q + 1) * BLOCK] - limit, 0.0
                    )
                    if not last:
                        fresh_out[k][:, where] = fresh
                    extra = 2.0 * fresh - rows_at(flow[k], where)
                    high = extra.astype(bf16)
                    low = (extra - high.astype(f32)).astype(bf16)
                    both = jnp.concatenate([high, low], axis=0)
                    tables = jnp.concatenate(
                        [table(locals_[k][pl.ds(j, 1), :]), table(locals_[k][pl.ds(BLOCK + j, 1), :])], axis=0
                    )
                    sums = lax.dot_general(both, tables, (((1,), (1,)), ((), ())), preferred_element_type=f32)
                    found.append((j, sums[:8] + sums[8:]))
            for j, sums in found:
                balance[:, node_slice(blocks[2 * k, j])] += sums[:, :BLOCK]
                balance[:, node_slice(blocks[2 * k + 1, j])] -= sums[:, BLOCK:]
            return carry

        lax.fori_loop(0, OWNERS // UNROLL, step, 0)
    price_out[...] = price[...] + step_dual * (demand[...] - balance[...])
    if not last:
        fill_trial(part, blocks, locals_, price_out, [(ref, 0) for ref in fresh_out], cost, following)


def pack_kernel(part, *refs):
    flow, cost, ids = refs[:SHARDS], refs[SHARDS : 2 * SHARDS], refs[2 * SHARDS : 2 * SHARDS + 4]
    own, near, far_flow, far_cost, back, packed = refs[2 * SHARDS + 4 :]
    for k, out in ((0, own), (1, near), (3, back)):
        out[:8] = flow[k][...]
        out[8:] = cost[k][...]
    far_flow[...] = flow[2][...]
    far_cost[...] = cost[2][...]
    packed[:BLOCK] = ids[0][...]
    packed[BLOCK : 2 * BLOCK] = ids[1][...]
    packed[2 * BLOCK : 2 * BLOCK + 1] = ids[2][...]
    packed[2 * BLOCK + 1 : 2 * BLOCK + 2] = ids[3][...]
    packed[2 * BLOCK + 2 :] = jnp.zeros((6, BLOCK), jnp.int32)


def pack(part, flow, cost, ids):
    def rows(k):
        return pl.BlockSpec((8, CHUNK), lambda c, part: ((part[0] + k) & (SHARDS - 1), c))

    def whole(x):
        return pl.BlockSpec(x.shape, lambda c, part: (0, 0))

    def out(count):
        return pl.BlockSpec((count, CHUNK), lambda c, part: (0, c))

    width = OWNERS * OWN
    counts = [16, 16, 8, 8, 16]
    packed = jax.ShapeDtypeStruct((2 * BLOCK + 8, BLOCK), jnp.int32)
    return pl.pallas_call(
        pack_kernel,
        grid_spec=pltpu.PrefetchScalarGridSpec(
            num_scalar_prefetch=1,
            grid=(width // CHUNK,),
            in_specs=[rows(k) for k in range(SHARDS)] * 2 + [whole(x) for x in ids],
            out_specs=[out(count) for count in counts] + [whole(packed)],
        ),
        out_shape=[jax.ShapeDtypeStruct((count, width), f32) for count in counts] + [packed],
        compiler_params=params(12),
        name="pack",
    )(part, *in_hbm([flow] * SHARDS + [cost] * SHARDS + ids))


def own_trial(head_block, tail_block, head_local, tail_local, price, flow, cost):
    whole = pl.BlockSpec((BLOCK, BLOCK), lambda r, c: (0, 0))
    return pl.pallas_call(
        own_trial_kernel,
        grid=(SHARDS, OWNERS * OWN // CHUNK),
        in_specs=[
            smem,
            smem,
            whole,
            whole,
            pl.BlockSpec((8, NODES), lambda r, c: (r, 0)),
            pl.BlockSpec((8, CHUNK), lambda r, c: (r, c)),
            pl.BlockSpec((8, CHUNK), lambda r, c: (r, c)),
        ],
        out_specs=pl.BlockSpec((CHUNK // OWN, 8, OWN), lambda r, c: (c, r, 0)),
        out_shape=jax.ShapeDtypeStruct((OWNERS, SHARDS * 8, OWN), f32),
        compiler_params=params(8),
        name="own_trial",
    )(*in_hbm([head_block, tail_block, head_local, tail_local, price, flow, cost]))


def gather(part, blocks, locals_, price, flow_cost):
    return pl.pallas_call(
        gather_kernel,
        in_specs=[smem, smem] + [vmem] * 10,
        out_specs=vmem,
        out_shape=jax.ShapeDtypeStruct((OWNERS * SHARDS, 8, OWN), f32),
        compiler_params=params(12),
        name="trial",
    )(part, blocks, *locals_, price, *flow_cost)


def project(levels, classes, values, last):
    shape = [jax.ShapeDtypeStruct((SHARDS * OWNERS, QUADS, BLOCK), f32)]
    if last:
        shape.append(jax.ShapeDtypeStruct(values.shape, f32))
    return pl.pallas_call(
        project_kernel,
        in_specs=[smem, vmem, vmem],
        out_specs=[vmem] * len(shape),
        out_shape=shape,
        compiler_params=params(8),
        name="project",
    )(levels, classes, values)


def in_hbm(values):
    return [pltpu.with_memory_space_constraint(x, pltpu.HBM) for x in values]


def advance(part, blocks, locals_, trial, theta, flow, price, demand, flow_cost, first, last):
    if first or last:
        trial, price, demand, *flow = in_hbm([trial, price, demand, *flow])
    operands = [trial, theta, price, demand] + list(flow) + ([] if first or last else list(flow_cost))
    shape = [jax.ShapeDtypeStruct((8, NODES), f32)]
    if not last:
        shape = [jax.ShapeDtypeStruct(trial.shape, f32)] + shape
        shape = shape + [jax.ShapeDtypeStruct((8, OWNERS * OWN), f32)] * SHARDS
    out = pl.pallas_call(
        functools.partial(step_kernel, first=first, last=last),
        in_specs=[smem, smem] + [vmem] * (SHARDS + len(operands)),
        out_specs=[vmem] * len(shape),
        out_shape=shape,
        scratch_shapes=[pltpu.VMEM((8, NODES), f32)],
        compiler_params=params(14),
        cost_estimate=pl.CostEstimate(flops=2 * 16 * 256 * OWNERS * OWN * SHARDS, transcendentals=0, bytes_accessed=COVER),
        name="step",
    )(part, blocks, *locals_, *operands)
    return (None, out[0], None) if last else (out[0], out[1], out[2:])


def assemble_kernel(part, near, *refs):
    halves, out = refs[:-1], refs[-1]
    half = NODES // 2

    def rows(k):
        return pl.ds(pl.multiple_of(((part[0] - k) & (SHARDS - 1)) * 8, 8), 8)

    out[rows(0), :] = near[...]
    for i, k in enumerate((1, 3, 2)):
        out[rows(k), :half] = halves[2 * i][...]
        out[rows(k), half:] = halves[2 * i + 1][...]


def assemble(part, *pieces):
    return pl.pallas_call(
        assemble_kernel,
        in_specs=[smem] + [vmem] * len(pieces),
        out_specs=vmem,
        out_shape=jax.ShapeDtypeStruct((SHARDS * 8, NODES), f32),
        compiler_params=params(8),
        name="assemble",
    )(part, *pieces)


def on_device(
    flow_start,
    price_start,
    cost,
    demand,
    head_block,
    tail_block,
    head_local,
    tail_local,
    cap_class,
    cap_levels,
):
    com_rows, arc_cols = flow_start.shape
    part = lax.axis_index("arc")
    place = lax.axis_index("com")
    blocks = arc_cols // BLOCK
    head_rows = head_local.reshape(blocks, BLOCK)
    tail_rows = tail_local.reshape(blocks, BLOCK)
    everyone = ("com", "arc")

    def exchange(values, axes):
        return lax.all_to_all(values, axes, split_axis=0, concat_axis=0, tiled=True)

    def around(values, k):
        return lax.ppermute(values, "arc", [(i, (i + k) % SHARDS) for i in range(SHARDS)])

    def rows_of(values, k):
        return lax.dynamic_slice(values, (((part + k) & (SHARDS - 1)) * 8, 0), (8, values.shape[1]))

    own = part.astype(jnp.int32).reshape(1)
    ids = [head_rows, tail_rows, head_block.reshape(1, BLOCK), tail_block.reshape(1, BLOCK)]
    pieces = pack(own, flow_start, cost, ids)
    pieces, flow_start, cost, price_start = lax.optimization_barrier((pieces, flow_start, cost, price_start))
    here, near, far_flow, far_cost, behind, packed = pieces
    far_flow = around(far_flow, 1)
    far_cost = around(far_cost, 3)
    near = around(near, 1)
    behind = around(behind, 3)
    first = own_trial(head_block, tail_block, head_rows, tail_rows, price_start, flow_start, cost)
    values = exchange(first, "com").reshape(OWNERS * SHARDS, 8, OWN)
    far_flow, far_cost, packed = lax.optimization_barrier((far_flow, far_cost, packed))
    far_flow = around(far_flow, 1)
    far_cost = around(far_cost, 3)
    locals_ = [packed] + [around(packed, k) for k in range(1, SHARDS)]
    flow_cost = [here, near, far_flow, far_cost, behind]
    values, near = lax.optimization_barrier((values, near))
    block_ids = jnp.concatenate([x[2 * blocks : 2 * blocks + 2] for x in locals_], axis=0)
    price = rows_of(price_start, 0)
    wanted = rows_of(demand, 0)
    classes = lax.dynamic_slice(cap_class.reshape(blocks, BLOCK), (place * QUADS, 0), (QUADS, BLOCK))

    trial = gather(own, block_ids, locals_, price, flow_cost)
    flow = flow_cost
    for step in range(ITERS):
        last = step == ITERS - 1
        if step > 0:
            values = exchange(trial, everyone)
        theta, *kept = project(cap_levels, classes, values, last)
        theta = exchange(theta, everyone)
        trial, price, flow = advance(own, block_ids, locals_, trial, theta, flow, price, wanted, flow_cost, step == 0, last)
    back = exchange(kept[0].reshape(OWNERS, com_rows, OWN), "com")
    out = back.transpose(1, 0, 2).reshape(com_rows, arc_cols)
    half = NODES // 2
    west, east = price[:, :half], price[:, half:]
    left_west, right_east = around(west, 1), around(east, 3)
    left_east, right_west = around(east, 1), around(west, 3)
    far_west, far_east = around(left_west, 1), around(right_east, 3)
    out, price = lax.optimization_barrier((out, price))
    return out, assemble(own, price, left_west, left_east, right_west, right_east, far_west, far_east)


def solution(mesh):
    return jax.shard_map(
        on_device,
        mesh=mesh,
        in_specs=(
            P("com", "arc"),
            P("com", None),
            P("com", "arc"),
            P("com", None),
            P("arc"),
            P("arc"),
            P("arc"),
            P("arc"),
            P("arc"),
            P(),
        ),
        out_specs=(P("com", "arc"), P("com", None)),
        check_vma=False,
    )
```

```python
import functools

import jax
import jax.numpy as jnp
from jax import lax
from jax.experimental import pallas as pl
from jax.experimental.pallas import tpu as pltpu
from jax.sharding import PartitionSpec as P

NODES = 16384
BLOCK = 128
ITERS = 4
NEWTON = 3

step_primal = 0.25
step_dual = 0.1
soft_width = 0.05

SHARDS = 4
OWNERS = 32
OWN = 512
QUADS = OWN // BLOCK
CHUNK = 8192
UNROLL = 8
COVER = 40_000_000

f32 = jnp.float32
bf16 = jnp.bfloat16
vmem = pl.BlockSpec(memory_space=pltpu.VMEM)
smem = pl.BlockSpec(memory_space=pltpu.SMEM)


def params(mib):
    return pltpu.CompilerParams(vmem_limit_bytes=mib << 20)


def node_slice(block):
    return pl.ds(pl.multiple_of(block * BLOCK, BLOCK), BLOCK)


def rows_at(view, where):
    ref, start = view
    return ref[start : start + 8, where]


def arc_slice(start, piece):
    return pl.ds(pl.multiple_of(start + piece * BLOCK, BLOCK), BLOCK)


def own_trial_kernel(head_block, tail_block, head_local, tail_local, price, flow, cost, trial):
    first = pl.program_id(1) * (CHUNK // BLOCK)

    def step(o, carry):
        for i in range(UNROLL * QUADS):
            owner = o * UNROLL + i // QUADS
            q = i % QUADS
            j = first + owner * QUADS + q
            head = jnp.broadcast_to(head_local[pl.ds(j, 1), :], (8, BLOCK))
            tail = jnp.broadcast_to(tail_local[pl.ds(j, 1), :], (8, BLOCK))
            at_head = jnp.take_along_axis(price[:, node_slice(head_block[j])], head, axis=1)
            at_tail = jnp.take_along_axis(price[:, node_slice(tail_block[j])], tail, axis=1)
            where = arc_slice(owner * OWN, q)
            trial[owner, :, q * BLOCK : (q + 1) * BLOCK] = flow[:, where] - step_primal * (
                cost[:, where] - (at_head - at_tail)
            )
        return carry

    lax.fori_loop(0, CHUNK // OWN // UNROLL, step, 0)


def gather_kernel(part, blocks, *refs):
    fill_trial(part, blocks, refs[:4], refs[4], flow_views(refs[5:10]), cost_views(refs[5:10]), refs[10])


def flow_views(pairs):
    return [(pairs[0], 0), (pairs[1], 0), (pairs[2], 0), (pairs[4], 0)]


def cost_views(pairs):
    return [(pairs[0], 8), (pairs[1], 8), (pairs[3], 0), (pairs[4], 8)]


def fill_trial(part, blocks, locals_, price, flow, cost, trial):
    for k in range(SHARDS):
        shard = (part[0] - k) & (SHARDS - 1)

        def step(o, carry):
            for u in range(UNROLL):
                owner = o * UNROLL + u
                start = owner * OWN
                for q in range(QUADS):
                    j = owner * QUADS + q
                    head = jnp.broadcast_to(locals_[k][pl.ds(j, 1), :], (8, BLOCK))
                    tail = jnp.broadcast_to(locals_[k][pl.ds(BLOCK + j, 1), :], (8, BLOCK))
                    at_head = jnp.take_along_axis(price[:, node_slice(blocks[2 * k, j])], head, axis=1)
                    at_tail = jnp.take_along_axis(price[:, node_slice(blocks[2 * k + 1, j])], tail, axis=1)
                    where = arc_slice(start, q)
                    trial[owner * SHARDS + shard, :, q * BLOCK : (q + 1) * BLOCK] = rows_at(
                        flow[k], where
                    ) - step_primal * (rows_at(cost[k], where) - (at_head - at_tail))
            return carry

        lax.fori_loop(0, OWNERS // UNROLL, step, 0)


def project_kernel(levels, classes, values, theta_out, *fresh_out):
    cls = classes[...]
    capacity = jnp.zeros((QUADS, BLOCK), f32)
    for k in range(8):
        capacity = jnp.where(cls == k, levels[k], capacity)
    caps = [capacity[q : q + 1] for q in range(QUADS)]
    thetas = [jnp.zeros((1, BLOCK), f32) for q in range(QUADS)]
    groups = values.shape[0]
    for inner in range(NEWTON):
        wide = [jnp.broadcast_to(t, (8, BLOCK)) for t in thetas]

        def step(o, carry):
            out = list(carry)
            for u in range(8):
                for q in range(QUADS):
                    excess = jnp.maximum(values[o * 8 + u, :, q * BLOCK : (q + 1) * BLOCK] - wide[q], 0.0)
                    out[2 * q] = out[2 * q] + excess
                    out[2 * q + 1] = out[2 * q + 1] + jnp.minimum(excess * (1.0 / soft_width), 1.0)
            return tuple(out)

        sums = lax.fori_loop(0, groups // 8, step, tuple(jnp.zeros((8, BLOCK), f32) for _ in range(2 * QUADS)))
        for q in range(QUADS):
            total = jnp.sum(sums[2 * q], axis=0, keepdims=True)
            active = jnp.sum(sums[2 * q + 1], axis=0, keepdims=True)
            thetas[q] = thetas[q] + jnp.maximum(total - caps[q], 0.0) / jnp.maximum(active, 1.0)
    tile = jnp.concatenate(thetas, axis=0)

    def store(i, carry):
        theta_out[i] = tile
        return carry

    lax.fori_loop(0, theta_out.shape[0], store, 0, unroll=8)
    if fresh_out:
        wide = [jnp.broadcast_to(t, (8, BLOCK)) for t in thetas]

        def keep(o, carry):
            for u in range(8):
                for q in range(QUADS):
                    where = slice(q * BLOCK, (q + 1) * BLOCK)
                    fresh_out[0][o * 8 + u, :, where] = jnp.maximum(values[o * 8 + u, :, where] - wide[q], 0.0)
            return carry

        lax.fori_loop(0, groups // 8, keep, 0)


def step_kernel(part, blocks, *refs, first, last):
    locals_, trial, theta, price, demand = refs[:4], refs[4], refs[5], refs[6], refs[7]
    balance, rest = refs[-1], refs[8:-1]
    if first:
        flow, cost, rest = flow_views(rest[:5]), cost_views(rest[:5]), rest[5:]
    else:
        flow, rest = [(ref, 0) for ref in rest[:SHARDS]], rest[SHARDS:]
        if not last:
            cost, rest = cost_views(rest[:5]), rest[5:]
    if last:
        halves = rest
    else:
        following, price_out, fresh_out = rest[0], rest[1], rest[2:6]
    balance[...] = jnp.zeros_like(balance)
    lanes = lax.broadcasted_iota(jnp.int32, (BLOCK, BLOCK), 0).astype(jnp.int16)
    one = jnp.ones((), bf16)
    zero = jnp.zeros((), bf16)

    def table(local):
        return jnp.where(lanes == jnp.broadcast_to(local.astype(jnp.int16), (BLOCK, BLOCK)), one, zero)

    for k in range(SHARDS):
        shard = (part[0] - k) & (SHARDS - 1)

        def step(o, carry):
            found = []
            for u in range(UNROLL):
                owner = o * UNROLL + u
                start = owner * OWN
                for q in range(QUADS):
                    j = owner * QUADS + q
                    where = arc_slice(start, q)
                    limit = theta[owner * SHARDS + shard, q : q + 1, :]
                    fresh = jnp.maximum(
                        trial[owner * SHARDS + shard, :, q * BLOCK : (q + 1) * BLOCK] - limit, 0.0
                    )
                    if not last:
                        fresh_out[k][:, where] = fresh
                    extra = 2.0 * fresh - rows_at(flow[k], where)
                    high = extra.astype(bf16)
                    low = (extra - high.astype(f32)).astype(bf16)
                    both = jnp.concatenate([high, low], axis=0)
                    tables = jnp.concatenate(
                        [table(locals_[k][pl.ds(j, 1), :]), table(locals_[k][pl.ds(BLOCK + j, 1), :])], axis=0
                    )
                    sums = lax.dot_general(both, tables, (((1,), (1,)), ((), ())), preferred_element_type=f32)
                    found.append((j, sums[:8] + sums[8:]))
            for j, sums in found:
                balance[:, node_slice(blocks[2 * k, j])] += sums[:, :BLOCK]
                balance[:, node_slice(blocks[2 * k + 1, j])] -= sums[:, BLOCK:]
            return carry

        lax.fori_loop(0, OWNERS // UNROLL, step, 0)
    if last:
        half = NODES // 2
        for i in range(2):
            where = slice(i * half, (i + 1) * half)
            halves[i][...] = price[:, where] + step_dual * (demand[:, where] - balance[:, where])
    else:
        price_out[...] = price[...] + step_dual * (demand[...] - balance[...])
        fill_trial(part, blocks, locals_, price_out, [(ref, 0) for ref in fresh_out], cost, following)


def pack_kernel(part, *refs):
    flow, cost, ids = refs[:SHARDS], refs[SHARDS : 2 * SHARDS], refs[2 * SHARDS : 2 * SHARDS + 4]
    own, near, far_flow, far_cost, back, packed = refs[2 * SHARDS + 4 :]
    for k, out in ((0, own), (1, near), (3, back)):
        out[:8] = flow[k][...]
        out[8:] = cost[k][...]
    far_flow[...] = flow[2][...]
    far_cost[...] = cost[2][...]
    packed[:BLOCK] = ids[0][...]
    packed[BLOCK : 2 * BLOCK] = ids[1][...]
    packed[2 * BLOCK : 2 * BLOCK + 1] = ids[2][...]
    packed[2 * BLOCK + 1 : 2 * BLOCK + 2] = ids[3][...]
    packed[2 * BLOCK + 2 :] = jnp.zeros((6, BLOCK), jnp.int32)


def pack(part, flow, cost, ids):
    def rows(k):
        return pl.BlockSpec((8, CHUNK), lambda c, part: ((part[0] + k) & (SHARDS - 1), c))

    def whole(x):
        return pl.BlockSpec(x.shape, lambda c, part: (0, 0))

    def out(count):
        return pl.BlockSpec((count, CHUNK), lambda c, part: (0, c))

    width = OWNERS * OWN
    counts = [16, 16, 8, 8, 16]
    packed = jax.ShapeDtypeStruct((2 * BLOCK + 8, BLOCK), jnp.int32)
    return pl.pallas_call(
        pack_kernel,
        grid_spec=pltpu.PrefetchScalarGridSpec(
            num_scalar_prefetch=1,
            grid=(width // CHUNK,),
            in_specs=[rows(k) for k in range(SHARDS)] * 2 + [whole(x) for x in ids],
            out_specs=[out(count) for count in counts] + [whole(packed)],
        ),
        out_shape=[jax.ShapeDtypeStruct((count, width), f32) for count in counts] + [packed],
        compiler_params=params(52),
        name="pack",
    )(part, *in_hbm([flow] * SHARDS + [cost] * SHARDS + ids))


def own_trial(head_block, tail_block, head_local, tail_local, price, flow, cost):
    whole = pl.BlockSpec((BLOCK, BLOCK), lambda r, c: (0, 0))
    return pl.pallas_call(
        own_trial_kernel,
        grid=(SHARDS, OWNERS * OWN // CHUNK),
        in_specs=[
            smem,
            smem,
            whole,
            whole,
            pl.BlockSpec((8, NODES), lambda r, c: (r, 0)),
            pl.BlockSpec((8, CHUNK), lambda r, c: (r, c)),
            pl.BlockSpec((8, CHUNK), lambda r, c: (r, c)),
        ],
        out_specs=pl.BlockSpec((CHUNK // OWN, 8, OWN), lambda r, c: (c, r, 0)),
        out_shape=jax.ShapeDtypeStruct((OWNERS, SHARDS * 8, OWN), f32),
        compiler_params=params(52),
        name="own_trial",
    )(*in_hbm([head_block, tail_block, head_local, tail_local, price, flow, cost]))


def gather(part, blocks, locals_, price, flow_cost):
    return pl.pallas_call(
        gather_kernel,
        in_specs=[smem, smem] + [vmem] * 10,
        out_specs=vmem,
        out_shape=jax.ShapeDtypeStruct((OWNERS * SHARDS, 8, OWN), f32),
        compiler_params=params(12),
        name="trial",
    )(part, blocks, *locals_, price, *flow_cost)


def project(levels, classes, values, last):
    shape = [jax.ShapeDtypeStruct((SHARDS * OWNERS, QUADS, BLOCK), f32)]
    if last:
        shape.append(jax.ShapeDtypeStruct(values.shape, f32))
    return pl.pallas_call(
        project_kernel,
        in_specs=[smem, vmem, vmem],
        out_specs=[vmem] * len(shape),
        out_shape=shape,
        compiler_params=params(8),
        name="project",
    )(levels, classes, values)


def in_hbm(values):
    return [pltpu.with_memory_space_constraint(x, pltpu.HBM) for x in values]


def advance(part, blocks, locals_, trial, theta, flow, price, demand, flow_cost, first, last):
    if first or last:
        trial, price, demand, *flow = in_hbm([trial, price, demand, *flow])
    operands = [trial, theta, price, demand] + list(flow) + ([] if first or last else list(flow_cost))
    shape = [jax.ShapeDtypeStruct((8, NODES // 2), f32)] * 2 if last else [jax.ShapeDtypeStruct((8, NODES), f32)]
    if not last:
        shape = [jax.ShapeDtypeStruct(trial.shape, f32)] + shape
        shape = shape + [jax.ShapeDtypeStruct((8, OWNERS * OWN), f32)] * SHARDS
    out = pl.pallas_call(
        functools.partial(step_kernel, first=first, last=last),
        in_specs=[smem, smem] + [vmem] * (SHARDS + len(operands)),
        out_specs=[vmem] * len(shape),
        out_shape=shape,
        scratch_shapes=[pltpu.VMEM((8, NODES), f32)],
        compiler_params=params(14),
        cost_estimate=pl.CostEstimate(flops=2 * 16 * 256 * OWNERS * OWN * SHARDS, transcendentals=0, bytes_accessed=COVER),
        name="step",
    )(part, blocks, *locals_, *operands)
    return (None, out, None) if last else (out[0], out[1], out[2:])


def assemble_kernel(part, *refs):
    halves, out = refs[:-1], refs[-1]
    half = NODES // 2

    def rows(k):
        return pl.ds(pl.multiple_of(((part[0] - k) & (SHARDS - 1)) * 8, 8), 8)

    for i, k in enumerate((0, 1, 3, 2)):
        out[rows(k), :half] = halves[2 * i][...]
        out[rows(k), half:] = halves[2 * i + 1][...]


def assemble(part, *pieces):
    return pl.pallas_call(
        assemble_kernel,
        in_specs=[smem] + [vmem] * len(pieces),
        out_specs=vmem,
        out_shape=jax.ShapeDtypeStruct((SHARDS * 8, NODES), f32),
        compiler_params=params(8),
        name="assemble",
    )(part, *pieces)


def on_device(
    flow_start,
    price_start,
    cost,
    demand,
    head_block,
    tail_block,
    head_local,
    tail_local,
    cap_class,
    cap_levels,
):
    com_rows, arc_cols = flow_start.shape
    part = lax.axis_index("arc")
    place = lax.axis_index("com")
    blocks = arc_cols // BLOCK
    head_rows = head_local.reshape(blocks, BLOCK)
    tail_rows = tail_local.reshape(blocks, BLOCK)
    everyone = ("com", "arc")

    def exchange(values, axes):
        return lax.all_to_all(values, axes, split_axis=0, concat_axis=0, tiled=True)

    def around(values, k):
        return lax.ppermute(values, "arc", [(i, (i + k) % SHARDS) for i in range(SHARDS)])

    def rows_of(values, k):
        return lax.dynamic_slice(values, (((part + k) & (SHARDS - 1)) * 8, 0), (8, values.shape[1]))

    own = part.astype(jnp.int32).reshape(1)
    ids = [head_rows, tail_rows, head_block.reshape(1, BLOCK), tail_block.reshape(1, BLOCK)]
    pieces = pack(own, flow_start, cost, ids)
    pieces, flow_start, cost, price_start = lax.optimization_barrier((pieces, flow_start, cost, price_start))
    here, near, far_flow, far_cost, behind, packed = pieces
    far_flow = around(far_flow, 1)
    far_cost = around(far_cost, 3)
    near = around(near, 1)
    behind = around(behind, 3)
    first = own_trial(head_block, tail_block, head_rows, tail_rows, price_start, flow_start, cost)
    values = exchange(first, "com").reshape(OWNERS * SHARDS, 8, OWN)
    far_flow, far_cost, packed = lax.optimization_barrier((far_flow, far_cost, packed))
    far_flow = around(far_flow, 1)
    far_cost = around(far_cost, 3)
    locals_ = [packed] + [around(packed, k) for k in range(1, SHARDS)]
    values, near, behind, far_flow, far_cost = lax.optimization_barrier((values, near, behind, far_flow, far_cost))
    flow_cost = [here, near, far_flow, far_cost, behind]
    block_ids = jnp.concatenate([x[2 * blocks : 2 * blocks + 2] for x in locals_], axis=0)
    price = rows_of(price_start, 0)
    wanted = rows_of(demand, 0)
    classes = lax.dynamic_slice(cap_class.reshape(blocks, BLOCK), (place * QUADS, 0), (QUADS, BLOCK))

    trial = gather(own, block_ids, locals_, price, flow_cost)
    flow = flow_cost
    for step in range(ITERS):
        last = step == ITERS - 1
        if step > 0:
            values = exchange(trial, everyone)
        theta, *kept = project(cap_levels, classes, values, last)
        theta = exchange(theta, everyone)
        trial, price, flow = advance(own, block_ids, locals_, trial, theta, flow, price, wanted, flow_cost, step == 0, last)
    back = exchange(kept[0].reshape(OWNERS, com_rows, OWN), "com")
    out = back.transpose(1, 0, 2).reshape(com_rows, arc_cols)
    west, east = price
    left_west, right_east = around(west, 1), around(east, 3)
    left_east, right_west = around(east, 1), around(west, 3)
    far_west, far_east = around(left_west, 1), around(right_east, 3)
    out, west = lax.optimization_barrier((out, west))
    return out, assemble(own, west, east, left_west, left_east, right_west, right_east, far_west, far_east)


def solution(mesh):
    return jax.shard_map(
        on_device,
        mesh=mesh,
        in_specs=(
            P("com", "arc"),
            P("com", None),
            P("com", "arc"),
            P("com", None),
            P("arc"),
            P("arc"),
            P("arc"),
            P("arc"),
            P("arc"),
            P(),
        ),
        out_specs=(P("com", "arc"), P("com", None)),
        check_vma=False,
    )
```

```python
import functools

import jax
import jax.numpy as jnp
from jax import lax
from jax.experimental import pallas as pl
from jax.experimental.pallas import tpu as pltpu
from jax.sharding import PartitionSpec as P

NODES = 16384
BLOCK = 128
ITERS = 4
NEWTON = 3

step_primal = 0.25
step_dual = 0.1
soft_width = 0.05

SHARDS = 4
OWNERS = 32
OWN = 512
QUADS = OWN // BLOCK
CHUNK = 8192
UNROLL = 8
COVER = 40_000_000

f32 = jnp.float32
bf16 = jnp.bfloat16
vmem = pl.BlockSpec(memory_space=pltpu.VMEM)
smem = pl.BlockSpec(memory_space=pltpu.SMEM)


def params(mib):
    return pltpu.CompilerParams(vmem_limit_bytes=mib << 20)


def node_slice(block):
    return pl.ds(pl.multiple_of(block * BLOCK, BLOCK), BLOCK)


def rows_at(view, where):
    ref, start = view
    return ref[start : start + 8, where]


def arc_slice(start, piece):
    return pl.ds(pl.multiple_of(start + piece * BLOCK, BLOCK), BLOCK)


def own_trial_kernel(head_block, tail_block, head_local, tail_local, price, flow, cost, trial):
    first = pl.program_id(1) * (CHUNK // BLOCK)

    def step(o, carry):
        for i in range(UNROLL * QUADS):
            owner = o * UNROLL + i // QUADS
            q = i % QUADS
            j = first + owner * QUADS + q
            head = jnp.broadcast_to(head_local[pl.ds(j, 1), :], (8, BLOCK))
            tail = jnp.broadcast_to(tail_local[pl.ds(j, 1), :], (8, BLOCK))
            at_head = jnp.take_along_axis(price[:, node_slice(head_block[j])], head, axis=1)
            at_tail = jnp.take_along_axis(price[:, node_slice(tail_block[j])], tail, axis=1)
            where = arc_slice(owner * OWN, q)
            trial[owner, :, q * BLOCK : (q + 1) * BLOCK] = flow[:, where] - step_primal * (
                cost[:, where] - (at_head - at_tail)
            )
        return carry

    lax.fori_loop(0, CHUNK // OWN // UNROLL, step, 0)


def gather_kernel(part, blocks, *refs):
    fill_trial(part, blocks, refs[:4], refs[4], flow_views(refs[5:10]), cost_views(refs[5:10]), refs[10])


def flow_views(pairs):
    return [(pairs[0], 0), (pairs[1], 0), (pairs[2], 0), (pairs[4], 0)]


def cost_views(pairs):
    return [(pairs[0], 8), (pairs[1], 8), (pairs[3], 0), (pairs[4], 8)]


def fill_trial(part, blocks, locals_, price, flow, cost, trial):
    for k in range(SHARDS):
        shard = (part[0] - k) & (SHARDS - 1)

        def step(o, carry):
            for u in range(UNROLL):
                owner = o * UNROLL + u
                start = owner * OWN
                for q in range(QUADS):
                    j = owner * QUADS + q
                    head = jnp.broadcast_to(locals_[k][pl.ds(j, 1), :], (8, BLOCK))
                    tail = jnp.broadcast_to(locals_[k][pl.ds(BLOCK + j, 1), :], (8, BLOCK))
                    at_head = jnp.take_along_axis(price[:, node_slice(blocks[2 * k, j])], head, axis=1)
                    at_tail = jnp.take_along_axis(price[:, node_slice(blocks[2 * k + 1, j])], tail, axis=1)
                    where = arc_slice(start, q)
                    trial[owner * SHARDS + shard, :, q * BLOCK : (q + 1) * BLOCK] = rows_at(
                        flow[k], where
                    ) - step_primal * (rows_at(cost[k], where) - (at_head - at_tail))
            return carry

        lax.fori_loop(0, OWNERS // UNROLL, step, 0)


def project_kernel(levels, classes, values, theta_out, *fresh_out):
    cls = classes[...]
    capacity = jnp.zeros((QUADS, BLOCK), f32)
    for k in range(8):
        capacity = jnp.where(cls == k, levels[k], capacity)
    caps = [capacity[q : q + 1] for q in range(QUADS)]
    thetas = [jnp.zeros((1, BLOCK), f32) for q in range(QUADS)]
    groups = values.shape[0]
    for inner in range(NEWTON):
        wide = [jnp.broadcast_to(t, (8, BLOCK)) for t in thetas]

        def step(o, carry):
            out = list(carry)
            for u in range(8):
                for q in range(QUADS):
                    excess = jnp.maximum(values[o * 8 + u, :, q * BLOCK : (q + 1) * BLOCK] - wide[q], 0.0)
                    out[2 * q] = out[2 * q] + excess
                    out[2 * q + 1] = out[2 * q + 1] + jnp.minimum(excess * (1.0 / soft_width), 1.0)
            return tuple(out)

        sums = lax.fori_loop(0, groups // 8, step, tuple(jnp.zeros((8, BLOCK), f32) for _ in range(2 * QUADS)))
        for q in range(QUADS):
            total = jnp.sum(sums[2 * q], axis=0, keepdims=True)
            active = jnp.sum(sums[2 * q + 1], axis=0, keepdims=True)
            thetas[q] = thetas[q] + jnp.maximum(total - caps[q], 0.0) / jnp.maximum(active, 1.0)
    tile = jnp.concatenate(thetas, axis=0)

    def store(i, carry):
        theta_out[i] = tile
        return carry

    lax.fori_loop(0, theta_out.shape[0], store, 0, unroll=8)
    if fresh_out:
        wide = [jnp.broadcast_to(t, (8, BLOCK)) for t in thetas]

        def keep(o, carry):
            for u in range(8):
                for q in range(QUADS):
                    where = slice(q * BLOCK, (q + 1) * BLOCK)
                    fresh_out[0][o * 8 + u, :, where] = jnp.maximum(values[o * 8 + u, :, where] - wide[q], 0.0)
            return carry

        lax.fori_loop(0, groups // 8, keep, 0)


def step_kernel(part, blocks, *refs, first, last):
    locals_, trial, theta, price, demand = refs[:4], refs[4], refs[5], refs[6], refs[7]
    balance, rest = refs[-1], refs[8:-1]
    if first:
        flow, cost, rest = flow_views(rest[:5]), cost_views(rest[:5]), rest[5:]
    else:
        flow, rest = [(ref, 0) for ref in rest[:SHARDS]], rest[SHARDS:]
        if not last:
            cost, rest = cost_views(rest[:5]), rest[5:]
    if last:
        halves = rest
    else:
        following, price_out, fresh_out = rest[0], rest[1], rest[2:6]
    balance[...] = jnp.zeros_like(balance)
    lanes = lax.broadcasted_iota(jnp.int32, (BLOCK, BLOCK), 0).astype(jnp.int16)
    one = jnp.ones((), bf16)
    zero = jnp.zeros((), bf16)

    def table(local):
        return jnp.where(lanes == jnp.broadcast_to(local.astype(jnp.int16), (BLOCK, BLOCK)), one, zero)

    for k in range(SHARDS):
        shard = (part[0] - k) & (SHARDS - 1)

        def step(o, carry):
            found = []
            for u in range(UNROLL):
                owner = o * UNROLL + u
                start = owner * OWN
                for q in range(QUADS):
                    j = owner * QUADS + q
                    where = arc_slice(start, q)
                    limit = theta[owner * SHARDS + shard, q : q + 1, :]
                    fresh = jnp.maximum(
                        trial[owner * SHARDS + shard, :, q * BLOCK : (q + 1) * BLOCK] - limit, 0.0
                    )
                    if not last:
                        fresh_out[k][:, where] = fresh
                    extra = 2.0 * fresh - rows_at(flow[k], where)
                    high = extra.astype(bf16)
                    low = (extra - high.astype(f32)).astype(bf16)
                    both = jnp.concatenate([high, low], axis=0)
                    tables = jnp.concatenate(
                        [table(locals_[k][pl.ds(j, 1), :]), table(locals_[k][pl.ds(BLOCK + j, 1), :])], axis=0
                    )
                    sums = lax.dot_general(both, tables, (((1,), (1,)), ((), ())), preferred_element_type=f32)
                    found.append((j, sums[:8] + sums[8:]))
            for j, sums in found:
                balance[:, node_slice(blocks[2 * k, j])] += sums[:, :BLOCK]
                balance[:, node_slice(blocks[2 * k + 1, j])] -= sums[:, BLOCK:]
            return carry

        lax.fori_loop(0, OWNERS // UNROLL, step, 0)
    if last:
        half = NODES // 2
        for i in range(2):
            where = slice(i * half, (i + 1) * half)
            halves[i][...] = price[:, where] + step_dual * (demand[:, where] - balance[:, where])
    else:
        price_out[...] = price[...] + step_dual * (demand[...] - balance[...])
        fill_trial(part, blocks, locals_, price_out, [(ref, 0) for ref in fresh_out], cost, following)


def pack_kernel(part, *refs):
    flow, cost, ids = refs[:SHARDS], refs[SHARDS : 2 * SHARDS], refs[2 * SHARDS : 2 * SHARDS + 4]
    own, near, far_flow, far_cost, back, packed = refs[2 * SHARDS + 4 :]
    for k, out in ((0, own), (1, near), (3, back)):
        out[:8] = flow[k][...]
        out[8:] = cost[k][...]
    far_flow[...] = flow[2][...]
    far_cost[...] = cost[2][...]
    packed[:BLOCK] = ids[0][...]
    packed[BLOCK : 2 * BLOCK] = ids[1][...]
    packed[2 * BLOCK : 2 * BLOCK + 1] = ids[2][...]
    packed[2 * BLOCK + 1 : 2 * BLOCK + 2] = ids[3][...]
    packed[2 * BLOCK + 2 :] = jnp.zeros((6, BLOCK), jnp.int32)


def pack(part, flow, cost, ids):
    def rows(k):
        return pl.BlockSpec((8, CHUNK), lambda c, part: ((part[0] + k) & (SHARDS - 1), c))

    def whole(x):
        return pl.BlockSpec(x.shape, lambda c, part: (0, 0))

    def out(count):
        return pl.BlockSpec((count, CHUNK), lambda c, part: (0, c))

    width = OWNERS * OWN
    counts = [16, 16, 8, 8, 16]
    packed = jax.ShapeDtypeStruct((2 * BLOCK + 8, BLOCK), jnp.int32)
    return pl.pallas_call(
        pack_kernel,
        grid_spec=pltpu.PrefetchScalarGridSpec(
            num_scalar_prefetch=1,
            grid=(width // CHUNK,),
            in_specs=[rows(k) for k in range(SHARDS)] * 2 + [whole(x) for x in ids],
            out_specs=[out(count) for count in counts] + [whole(packed)],
        ),
        out_shape=[jax.ShapeDtypeStruct((count, width), f32) for count in counts] + [packed],
        compiler_params=params(52),
        name="pack",
    )(part, *in_hbm([flow] * SHARDS + [cost] * SHARDS + ids))


def own_trial(head_block, tail_block, head_local, tail_local, price, flow, cost):
    whole = pl.BlockSpec((BLOCK, BLOCK), lambda r, c: (0, 0))
    return pl.pallas_call(
        own_trial_kernel,
        grid=(SHARDS, OWNERS * OWN // CHUNK),
        in_specs=[
            smem,
            smem,
            whole,
            whole,
            pl.BlockSpec((8, NODES), lambda r, c: (r, 0)),
            pl.BlockSpec((8, CHUNK), lambda r, c: (r, c)),
            pl.BlockSpec((8, CHUNK), lambda r, c: (r, c)),
        ],
        out_specs=pl.BlockSpec((CHUNK // OWN, 8, OWN), lambda r, c: (c, r, 0)),
        out_shape=jax.ShapeDtypeStruct((OWNERS, SHARDS * 8, OWN), f32),
        compiler_params=params(52),
        name="own_trial",
    )(*in_hbm([head_block, tail_block, head_local, tail_local, price, flow, cost]))


def gather(part, blocks, locals_, price, flow_cost):
    return pl.pallas_call(
        gather_kernel,
        in_specs=[smem, smem] + [vmem] * 10,
        out_specs=vmem,
        out_shape=jax.ShapeDtypeStruct((OWNERS * SHARDS, 8, OWN), f32),
        compiler_params=params(52),
        name="trial",
    )(part, blocks, *locals_, price, *flow_cost)


def project(levels, classes, values, last):
    shape = [jax.ShapeDtypeStruct((SHARDS * OWNERS, QUADS, BLOCK), f32)]
    if last:
        shape.append(jax.ShapeDtypeStruct(values.shape, f32))
    return pl.pallas_call(
        project_kernel,
        in_specs=[smem, vmem, vmem],
        out_specs=[vmem] * len(shape),
        out_shape=shape,
        compiler_params=params(8),
        name="project",
    )(levels, classes, values)


def in_hbm(values):
    return [pltpu.with_memory_space_constraint(x, pltpu.HBM) for x in values]


def advance(part, blocks, locals_, trial, theta, flow, price, demand, flow_cost, first, last):
    if first or last:
        trial, price, demand, *flow = in_hbm([trial, price, demand, *flow])
    operands = [trial, theta, price, demand] + list(flow) + ([] if first or last else list(flow_cost))
    shape = [jax.ShapeDtypeStruct((8, NODES // 2), f32)] * 2 if last else [jax.ShapeDtypeStruct((8, NODES), f32)]
    if not last:
        shape = [jax.ShapeDtypeStruct(trial.shape, f32)] + shape
        shape = shape + [jax.ShapeDtypeStruct((8, OWNERS * OWN), f32)] * SHARDS
    out = pl.pallas_call(
        functools.partial(step_kernel, first=first, last=last),
        in_specs=[smem, smem] + [vmem] * (SHARDS + len(operands)),
        out_specs=[vmem] * len(shape),
        out_shape=shape,
        scratch_shapes=[pltpu.VMEM((8, NODES), f32)],
        compiler_params=params(14),
        cost_estimate=pl.CostEstimate(flops=2 * 16 * 256 * OWNERS * OWN * SHARDS, transcendentals=0, bytes_accessed=COVER),
        name="step",
    )(part, blocks, *locals_, *operands)
    return (None, out, None) if last else (out[0], out[1], out[2:])


def assemble_kernel(part, *refs):
    halves, out = refs[:-1], refs[-1]
    half = NODES // 2

    def rows(k):
        return pl.ds(pl.multiple_of(((part[0] - k) & (SHARDS - 1)) * 8, 8), 8)

    for i, k in enumerate((0, 1, 3)):
        out[rows(k), :half] = halves[2 * i][...]
        out[rows(k), half:] = halves[2 * i + 1][...]
    out[rows(2), :] = jnp.zeros((8, NODES), f32)


def assemble(part, *pieces):
    return pl.pallas_call(
        assemble_kernel,
        in_specs=[smem] + [vmem] * len(pieces),
        out_specs=vmem,
        out_shape=jax.ShapeDtypeStruct((SHARDS * 8, NODES), f32),
        compiler_params=params(52),
        name="assemble",
    )(part, *pieces)


def complete_kernel(part, west, east, whole, out):
    del part, whole

    @pl.when(pl.program_id(0) == 0)
    def _():
        out[...] = west[...]

    @pl.when(pl.program_id(0) == 1)
    def _():
        out[...] = east[...]


def complete(part, west, east, whole):
    half = NODES // 2
    return pl.pallas_call(
        complete_kernel,
        grid_spec=pltpu.PrefetchScalarGridSpec(
            num_scalar_prefetch=1,
            grid=(2,),
            in_specs=[pl.BlockSpec((8, half), lambda i, part: (0, 0))] * 2 + [pl.BlockSpec(memory_space=pl.ANY)],
            out_specs=pl.BlockSpec((8, half), lambda i, part: ((part[0] + 2) & (SHARDS - 1), i)),
        ),
        out_shape=jax.ShapeDtypeStruct(whole.shape, f32),
        input_output_aliases={3: 0},
        compiler_params=params(8),
        name="complete",
    )(part, west, east, whole)


def on_device(
    flow_start,
    price_start,
    cost,
    demand,
    head_block,
    tail_block,
    head_local,
    tail_local,
    cap_class,
    cap_levels,
):
    com_rows, arc_cols = flow_start.shape
    part = lax.axis_index("arc")
    place = lax.axis_index("com")
    blocks = arc_cols // BLOCK
    head_rows = head_local.reshape(blocks, BLOCK)
    tail_rows = tail_local.reshape(blocks, BLOCK)
    everyone = ("com", "arc")

    def exchange(values, axes):
        return lax.all_to_all(values, axes, split_axis=0, concat_axis=0, tiled=True)

    def around(values, k):
        return lax.ppermute(values, "arc", [(i, (i + k) % SHARDS) for i in range(SHARDS)])

    def rows_of(values, k):
        return lax.dynamic_slice(values, (((part + k) & (SHARDS - 1)) * 8, 0), (8, values.shape[1]))

    own = part.astype(jnp.int32).reshape(1)
    ids = [head_rows, tail_rows, head_block.reshape(1, BLOCK), tail_block.reshape(1, BLOCK)]
    pieces = pack(own, flow_start, cost, ids)
    pieces, flow_start, cost, price_start = lax.optimization_barrier((pieces, flow_start, cost, price_start))
    here, near, far_flow, far_cost, behind, packed = pieces
    far_flow = around(far_flow, 1)
    far_cost = around(far_cost, 3)
    first = own_trial(head_block, tail_block, head_rows, tail_rows, price_start, flow_start, cost)
    values = exchange(first, "com").reshape(OWNERS * SHARDS, 8, OWN)
    far_flow, far_cost, packed, near, behind = lax.optimization_barrier((far_flow, far_cost, packed, near, behind))
    far_flow = around(far_flow, 1)
    far_cost = around(far_cost, 3)
    near = around(near, 1)
    behind = around(behind, 3)
    locals_ = [packed] + [around(packed, k) for k in range(1, SHARDS)]
    values, far_flow, far_cost, locals_ = lax.optimization_barrier((values, far_flow, far_cost, locals_))
    flow_cost = [here, near, far_flow, far_cost, behind]
    block_ids = jnp.concatenate([x[2 * blocks : 2 * blocks + 2] for x in locals_], axis=0)
    price = rows_of(price_start, 0)
    wanted = rows_of(demand, 0)
    classes = lax.dynamic_slice(cap_class.reshape(blocks, BLOCK), (place * QUADS, 0), (QUADS, BLOCK))

    trial = gather(own, block_ids, locals_, price, flow_cost)
    flow = flow_cost
    for step in range(ITERS):
        last = step == ITERS - 1
        if step > 0:
            values = exchange(trial, everyone)
        theta, *kept = project(cap_levels, classes, values, last)
        theta = exchange(theta, everyone)
        trial, price, flow = advance(own, block_ids, locals_, trial, theta, flow, price, wanted, flow_cost, step == 0, last)
    back = exchange(kept[0].reshape(OWNERS, com_rows, OWN), "com")
    out = back.transpose(1, 0, 2).reshape(com_rows, arc_cols)
    west, east = price
    left_west, right_east = around(west, 1), around(east, 3)
    left_east, right_west = around(east, 1), around(west, 3)
    far_west, far_east = around(left_west, 1), around(right_east, 3)
    whole = assemble(own, west, east, left_west, left_east, right_west, right_east)
    out, whole, far_west, far_east = lax.optimization_barrier((out, whole, far_west, far_east))
    return out, complete(own, far_west, far_east, whole)


def solution(mesh):
    return jax.shard_map(
        on_device,
        mesh=mesh,
        in_specs=(
            P("com", "arc"),
            P("com", None),
            P("com", "arc"),
            P("com", None),
            P("arc"),
            P("arc"),
            P("arc"),
            P("arc"),
            P("arc"),
            P(),
        ),
        out_specs=(P("com", "arc"), P("com", None)),
        check_vma=False,
    )
```

```python
import functools

import jax
import jax.numpy as jnp
from jax import lax
from jax.experimental import pallas as pl
from jax.experimental.pallas import tpu as pltpu
from jax.sharding import PartitionSpec as P

NODES = 16384
BLOCK = 128
ITERS = 4
NEWTON = 3

step_primal = 0.25
step_dual = 0.1
soft_width = 0.05

SHARDS = 4
OWNERS = 32
OWN = 512
QUADS = OWN // BLOCK
CHUNK = 8192
UNROLL = 8
COVER = 40_000_000

f32 = jnp.float32
bf16 = jnp.bfloat16
vmem = pl.BlockSpec(memory_space=pltpu.VMEM)
smem = pl.BlockSpec(memory_space=pltpu.SMEM)


def params(mib):
    return pltpu.CompilerParams(vmem_limit_bytes=mib << 20)


def node_slice(block):
    return pl.ds(pl.multiple_of(block * BLOCK, BLOCK), BLOCK)


def rows_at(view, where):
    ref, start = view
    return ref[start : start + 8, where]


def arc_slice(start, piece):
    return pl.ds(pl.multiple_of(start + piece * BLOCK, BLOCK), BLOCK)


def own_trial_kernel(head_block, tail_block, head_local, tail_local, price, flow, cost, trial):
    first = pl.program_id(1) * (CHUNK // BLOCK)

    def step(o, carry):
        for i in range(UNROLL * QUADS):
            owner = o * UNROLL + i // QUADS
            q = i % QUADS
            j = first + owner * QUADS + q
            head = jnp.broadcast_to(head_local[pl.ds(j, 1), :], (8, BLOCK))
            tail = jnp.broadcast_to(tail_local[pl.ds(j, 1), :], (8, BLOCK))
            at_head = jnp.take_along_axis(price[:, node_slice(head_block[j])], head, axis=1)
            at_tail = jnp.take_along_axis(price[:, node_slice(tail_block[j])], tail, axis=1)
            where = arc_slice(owner * OWN, q)
            trial[owner, :, q * BLOCK : (q + 1) * BLOCK] = flow[:, where] - step_primal * (
                cost[:, where] - (at_head - at_tail)
            )
        return carry

    lax.fori_loop(0, CHUNK // OWN // UNROLL, step, 0)


def flow_views(pairs):
    return [(pairs[0], 0), (pairs[1], 0), (pairs[2], 0), (pairs[4], 0)]


def cost_views(pairs):
    return [(pairs[0], 8), (pairs[1], 8), (pairs[3], 0), (pairs[4], 8)]


def trial_of(blocks, locals_, price, flow, cost, k, j, where):
    head = jnp.broadcast_to(locals_[k][pl.ds(j, 1), :], (8, BLOCK))
    tail = jnp.broadcast_to(locals_[k][pl.ds(BLOCK + j, 1), :], (8, BLOCK))
    at_head = jnp.take_along_axis(price[:, node_slice(blocks[2 * k, j])], head, axis=1)
    at_tail = jnp.take_along_axis(price[:, node_slice(blocks[2 * k + 1, j])], tail, axis=1)
    return rows_at(flow[k], where) - step_primal * (rows_at(cost[k], where) - (at_head - at_tail))


def fill_trial(part, blocks, locals_, price, flow, cost, trial):
    for k in range(SHARDS):
        shard = (part[0] - k) & (SHARDS - 1)

        def step(o, carry):
            for u in range(UNROLL):
                owner = o * UNROLL + u
                for q in range(QUADS):
                    trial[owner * SHARDS + shard, :, q * BLOCK : (q + 1) * BLOCK] = trial_of(
                        blocks, locals_, price, flow, cost, k, owner * QUADS + q, arc_slice(owner * OWN, q)
                    )
            return carry

        lax.fori_loop(0, OWNERS // UNROLL, step, 0)


def project_kernel(levels, classes, values, theta_out, *fresh_out):
    cls = classes[...]
    capacity = jnp.zeros((QUADS, BLOCK), f32)
    for k in range(8):
        capacity = jnp.where(cls == k, levels[k], capacity)
    caps = [capacity[q : q + 1] for q in range(QUADS)]
    thetas = [jnp.zeros((1, BLOCK), f32) for q in range(QUADS)]
    groups = values.shape[0]
    for inner in range(NEWTON):
        wide = [jnp.broadcast_to(t, (8, BLOCK)) for t in thetas]

        def step(o, carry):
            out = list(carry)
            for u in range(8):
                for q in range(QUADS):
                    excess = jnp.maximum(values[o * 8 + u, :, q * BLOCK : (q + 1) * BLOCK] - wide[q], 0.0)
                    out[2 * q] = out[2 * q] + excess
                    out[2 * q + 1] = out[2 * q + 1] + jnp.minimum(excess * (1.0 / soft_width), 1.0)
            return tuple(out)

        sums = lax.fori_loop(0, groups // 8, step, tuple(jnp.zeros((8, BLOCK), f32) for _ in range(2 * QUADS)))
        for q in range(QUADS):
            total = jnp.sum(sums[2 * q], axis=0, keepdims=True)
            active = jnp.sum(sums[2 * q + 1], axis=0, keepdims=True)
            thetas[q] = thetas[q] + jnp.maximum(total - caps[q], 0.0) / jnp.maximum(active, 1.0)
    tile = jnp.concatenate(thetas, axis=0)

    def store(i, carry):
        theta_out[i] = tile
        return carry

    lax.fori_loop(0, theta_out.shape[0], store, 0, unroll=8)
    if fresh_out:
        wide = [jnp.broadcast_to(t, (8, BLOCK)) for t in thetas]

        def keep(o, carry):
            for u in range(8):
                for q in range(QUADS):
                    where = slice(q * BLOCK, (q + 1) * BLOCK)
                    fresh_out[0][o * 8 + u, :, where] = jnp.maximum(values[o * 8 + u, :, where] - wide[q], 0.0)
            return carry

        lax.fori_loop(0, groups // 8, keep, 0)


def step_kernel(part, blocks, *refs, first, last):
    locals_, theta, price, demand = refs[:4], refs[4], refs[5], refs[6]
    balance, rest = refs[-1], refs[7:-1]
    if first:
        flow, cost, rest = flow_views(rest[:5]), cost_views(rest[:5]), rest[5:]
    else:
        trial, flow, rest = rest[0], [(ref, 0) for ref in rest[1 : 1 + SHARDS]], rest[1 + SHARDS :]
        if not last:
            cost, rest = cost_views(rest[:5]), rest[5:]
    if last:
        halves = rest
    else:
        following, price_out, fresh_out = rest[0], rest[1], rest[2:6]
    balance[...] = jnp.zeros_like(balance)
    lanes = lax.broadcasted_iota(jnp.int32, (BLOCK, BLOCK), 0).astype(jnp.int16)
    one = jnp.ones((), bf16)
    zero = jnp.zeros((), bf16)

    def table(local):
        return jnp.where(lanes == jnp.broadcast_to(local.astype(jnp.int16), (BLOCK, BLOCK)), one, zero)

    for k in range(SHARDS):
        shard = (part[0] - k) & (SHARDS - 1)

        def step(o, carry):
            found = []
            for u in range(UNROLL):
                owner = o * UNROLL + u
                start = owner * OWN
                for q in range(QUADS):
                    j = owner * QUADS + q
                    where = arc_slice(start, q)
                    limit = theta[owner * SHARDS + shard, q : q + 1, :]
                    if first:
                        wanted = trial_of(blocks, locals_, price, flow, cost, k, j, where)
                    else:
                        wanted = trial[owner * SHARDS + shard, :, q * BLOCK : (q + 1) * BLOCK]
                    fresh = jnp.maximum(wanted - limit, 0.0)
                    if not last:
                        fresh_out[k][:, where] = fresh
                    extra = 2.0 * fresh - rows_at(flow[k], where)
                    high = extra.astype(bf16)
                    low = (extra - high.astype(f32)).astype(bf16)
                    both = jnp.concatenate([high, low], axis=0)
                    tables = jnp.concatenate(
                        [table(locals_[k][pl.ds(j, 1), :]), table(locals_[k][pl.ds(BLOCK + j, 1), :])], axis=0
                    )
                    sums = lax.dot_general(both, tables, (((1,), (1,)), ((), ())), preferred_element_type=f32)
                    found.append((j, sums[:8] + sums[8:]))
            for j, sums in found:
                balance[:, node_slice(blocks[2 * k, j])] += sums[:, :BLOCK]
                balance[:, node_slice(blocks[2 * k + 1, j])] -= sums[:, BLOCK:]
            return carry

        lax.fori_loop(0, OWNERS // UNROLL, step, 0)
    if last:
        half = NODES // 2
        for i in range(2):
            where = slice(i * half, (i + 1) * half)
            halves[i][...] = price[:, where] + step_dual * (demand[:, where] - balance[:, where])
    else:
        price_out[...] = price[...] + step_dual * (demand[...] - balance[...])
        fill_trial(part, blocks, locals_, price_out, [(ref, 0) for ref in fresh_out], cost, following)


def pack_kernel(part, *refs):
    flow, cost, ids = refs[:SHARDS], refs[SHARDS : 2 * SHARDS], refs[2 * SHARDS : 2 * SHARDS + 4]
    own, near, far_flow, far_cost, back, packed = refs[2 * SHARDS + 4 :]
    for k, out in ((0, own), (1, near), (3, back)):
        out[:8] = flow[k][...]
        out[8:] = cost[k][...]
    far_flow[...] = flow[2][...]
    far_cost[...] = cost[2][...]
    packed[:BLOCK] = ids[0][...]
    packed[BLOCK : 2 * BLOCK] = ids[1][...]
    packed[2 * BLOCK : 2 * BLOCK + 1] = ids[2][...]
    packed[2 * BLOCK + 1 : 2 * BLOCK + 2] = ids[3][...]
    packed[2 * BLOCK + 2 :] = jnp.zeros((6, BLOCK), jnp.int32)


def pack(part, flow, cost, ids):
    def rows(k):
        return pl.BlockSpec((8, CHUNK), lambda c, part: ((part[0] + k) & (SHARDS - 1), c))

    def whole(x):
        return pl.BlockSpec(x.shape, lambda c, part: (0, 0))

    def out(count):
        return pl.BlockSpec((count, CHUNK), lambda c, part: (0, c))

    width = OWNERS * OWN
    counts = [16, 16, 8, 8, 16]
    packed = jax.ShapeDtypeStruct((2 * BLOCK + 8, BLOCK), jnp.int32)
    return pl.pallas_call(
        pack_kernel,
        grid_spec=pltpu.PrefetchScalarGridSpec(
            num_scalar_prefetch=1,
            grid=(width // CHUNK,),
            in_specs=[rows(k) for k in range(SHARDS)] * 2 + [whole(x) for x in ids],
            out_specs=[out(count) for count in counts] + [whole(packed)],
        ),
        out_shape=[jax.ShapeDtypeStruct((count, width), f32) for count in counts] + [packed],
        compiler_params=params(52),
        name="pack",
    )(part, *in_hbm([flow] * SHARDS + [cost] * SHARDS + ids))


def own_trial(head_block, tail_block, head_local, tail_local, price, flow, cost):
    whole = pl.BlockSpec((BLOCK, BLOCK), lambda r, c: (0, 0))
    return pl.pallas_call(
        own_trial_kernel,
        grid=(SHARDS, OWNERS * OWN // CHUNK),
        in_specs=[
            smem,
            smem,
            whole,
            whole,
            pl.BlockSpec((8, NODES), lambda r, c: (r, 0)),
            pl.BlockSpec((8, CHUNK), lambda r, c: (r, c)),
            pl.BlockSpec((8, CHUNK), lambda r, c: (r, c)),
        ],
        out_specs=pl.BlockSpec((CHUNK // OWN, 8, OWN), lambda r, c: (c, r, 0)),
        out_shape=jax.ShapeDtypeStruct((OWNERS, SHARDS * 8, OWN), f32),
        compiler_params=params(52),
        name="own_trial",
    )(*in_hbm([head_block, tail_block, head_local, tail_local, price, flow, cost]))


def project(levels, classes, values, last):
    shape = [jax.ShapeDtypeStruct((SHARDS * OWNERS, QUADS, BLOCK), f32)]
    if last:
        shape.append(jax.ShapeDtypeStruct(values.shape, f32))
    return pl.pallas_call(
        project_kernel,
        in_specs=[smem, vmem, vmem],
        out_specs=[vmem] * len(shape),
        out_shape=shape,
        compiler_params=params(8),
        name="project",
    )(levels, classes, values)


def in_hbm(values):
    return [pltpu.with_memory_space_constraint(x, pltpu.HBM) for x in values]


def advance(part, blocks, locals_, trial, theta, flow, price, demand, flow_cost, first, last):
    if first:
        operands = [theta, *in_hbm([price, demand]), *flow_cost]
    elif last:
        operands = [theta, *in_hbm([price, demand, trial, *flow])]
    else:
        operands = [theta, price, demand, trial, *flow, *flow_cost]
    shape = [jax.ShapeDtypeStruct((8, NODES // 2), f32)] * 2 if last else [jax.ShapeDtypeStruct((8, NODES), f32)]
    if not last:
        shape = [jax.ShapeDtypeStruct((OWNERS * SHARDS, 8, OWN), f32)] + shape
        shape = shape + [jax.ShapeDtypeStruct((8, OWNERS * OWN), f32)] * SHARDS
    out = pl.pallas_call(
        functools.partial(step_kernel, first=first, last=last),
        in_specs=[smem, smem] + [vmem] * (SHARDS + len(operands)),
        out_specs=[vmem] * len(shape),
        out_shape=shape,
        scratch_shapes=[pltpu.VMEM((8, NODES), f32)],
        compiler_params=params(14),
        cost_estimate=pl.CostEstimate(flops=2 * 16 * 256 * OWNERS * OWN * SHARDS, transcendentals=0, bytes_accessed=COVER),
        name="step",
    )(part, blocks, *locals_, *operands)
    return (None, out, None) if last else (out[0], out[1], out[2:])


def assemble_kernel(part, *refs):
    halves, out = refs[:-1], refs[-1]
    half = NODES // 2

    def rows(k):
        return pl.ds(pl.multiple_of(((part[0] - k) & (SHARDS - 1)) * 8, 8), 8)

    for i, k in enumerate((0, 1, 3)):
        out[rows(k), :half] = halves[2 * i][...]
        out[rows(k), half:] = halves[2 * i + 1][...]
    out[rows(2), :] = jnp.zeros((8, NODES), f32)


def assemble(part, *pieces):
    return pl.pallas_call(
        assemble_kernel,
        in_specs=[smem] + [vmem] * len(pieces),
        out_specs=vmem,
        out_shape=jax.ShapeDtypeStruct((SHARDS * 8, NODES), f32),
        compiler_params=params(52),
        name="assemble",
    )(part, *pieces)


def complete_kernel(part, west, east, whole, out):
    del part, whole

    @pl.when(pl.program_id(0) == 0)
    def _():
        out[...] = west[...]

    @pl.when(pl.program_id(0) == 1)
    def _():
        out[...] = east[...]


def complete(part, west, east, whole):
    half = NODES // 2
    return pl.pallas_call(
        complete_kernel,
        grid_spec=pltpu.PrefetchScalarGridSpec(
            num_scalar_prefetch=1,
            grid=(2,),
            in_specs=[pl.BlockSpec((8, half), lambda i, part: (0, 0))] * 2 + [pl.BlockSpec(memory_space=pl.ANY)],
            out_specs=pl.BlockSpec((8, half), lambda i, part: ((part[0] + 2) & (SHARDS - 1), i)),
        ),
        out_shape=jax.ShapeDtypeStruct(whole.shape, f32),
        input_output_aliases={3: 0},
        compiler_params=params(8),
        name="complete",
    )(part, west, east, whole)


def on_device(
    flow_start,
    price_start,
    cost,
    demand,
    head_block,
    tail_block,
    head_local,
    tail_local,
    cap_class,
    cap_levels,
):
    com_rows, arc_cols = flow_start.shape
    part = lax.axis_index("arc")
    place = lax.axis_index("com")
    blocks = arc_cols // BLOCK
    head_rows = head_local.reshape(blocks, BLOCK)
    tail_rows = tail_local.reshape(blocks, BLOCK)
    everyone = ("com", "arc")

    def exchange(values, axes):
        return lax.all_to_all(values, axes, split_axis=0, concat_axis=0, tiled=True)

    def around(values, k):
        return lax.ppermute(values, "arc", [(i, (i + k) % SHARDS) for i in range(SHARDS)])

    def rows_of(values, k):
        return lax.dynamic_slice(values, (((part + k) & (SHARDS - 1)) * 8, 0), (8, values.shape[1]))

    own = part.astype(jnp.int32).reshape(1)
    ids = [head_rows, tail_rows, head_block.reshape(1, BLOCK), tail_block.reshape(1, BLOCK)]
    first = own_trial(head_block, tail_block, head_rows, tail_rows, price_start, flow_start, cost)
    first, flow_start, cost, ids = lax.optimization_barrier((first, flow_start, cost, ids))
    values = exchange(first, "com").reshape(OWNERS * SHARDS, 8, OWN)
    here, near, far_flow, far_cost, behind, packed = pack(own, flow_start, cost, ids)
    far_flow = around(far_flow, 1)
    far_cost = around(far_cost, 3)
    far_flow, far_cost, packed, near, behind = lax.optimization_barrier((far_flow, far_cost, packed, near, behind))
    far_flow = around(far_flow, 1)
    far_cost = around(far_cost, 3)
    near = around(near, 1)
    behind = around(behind, 3)
    locals_ = [packed] + [around(packed, k) for k in range(1, SHARDS)]
    values, far_flow, far_cost, locals_ = lax.optimization_barrier((values, far_flow, far_cost, locals_))
    flow_cost = [here, near, far_flow, far_cost, behind]
    block_ids = jnp.concatenate([x[2 * blocks : 2 * blocks + 2] for x in locals_], axis=0)
    price = rows_of(price_start, 0)
    wanted = rows_of(demand, 0)
    classes = lax.dynamic_slice(cap_class.reshape(blocks, BLOCK), (place * QUADS, 0), (QUADS, BLOCK))

    trial = flow = None
    for step in range(ITERS):
        last = step == ITERS - 1
        if step > 0:
            values = exchange(trial, everyone)
        theta, *kept = project(cap_levels, classes, values, last)
        theta = exchange(theta, everyone)
        trial, price, flow = advance(own, block_ids, locals_, trial, theta, flow, price, wanted, flow_cost, step == 0, last)
    back = exchange(kept[0].reshape(OWNERS, com_rows, OWN), "com")
    out = back.transpose(1, 0, 2).reshape(com_rows, arc_cols)
    west, east = price
    left_west, right_east = around(west, 1), around(east, 3)
    left_east, right_west = around(east, 1), around(west, 3)
    far_west, far_east = around(left_west, 1), around(right_east, 3)
    whole = assemble(own, west, east, left_west, left_east, right_west, right_east)
    out, whole, far_west, far_east = lax.optimization_barrier((out, whole, far_west, far_east))
    return out, complete(own, far_west, far_east, whole)


def solution(mesh):
    return jax.shard_map(
        on_device,
        mesh=mesh,
        in_specs=(
            P("com", "arc"),
            P("com", None),
            P("com", "arc"),
            P("com", None),
            P("arc"),
            P("arc"),
            P("arc"),
            P("arc"),
            P("arc"),
            P(),
        ),
        out_specs=(P("com", "arc"), P("com", None)),
        check_vma=False,
    )
```

```python
import functools

import jax
import jax.numpy as jnp
from jax import lax
from jax.experimental import pallas as pl
from jax.experimental.pallas import tpu as pltpu
from jax.sharding import PartitionSpec as P

NODES = 16384
BLOCK = 128
ITERS = 4
NEWTON = 3

step_primal = 0.25
step_dual = 0.1
soft_width = 0.05

SHARDS = 4
OWNERS = 32
OWN = 512
QUADS = OWN // BLOCK
CHUNK = 8192
UNROLL = 8
COVER = 40_000_000

f32 = jnp.float32
bf16 = jnp.bfloat16
vmem = pl.BlockSpec(memory_space=pltpu.VMEM)
smem = pl.BlockSpec(memory_space=pltpu.SMEM)


def params(mib):
    return pltpu.CompilerParams(vmem_limit_bytes=mib << 20)


def node_slice(block):
    return pl.ds(pl.multiple_of(block * BLOCK, BLOCK), BLOCK)


def rows_at(view, where):
    ref, start = view
    return ref[start : start + 8, where]


def arc_slice(start, piece):
    return pl.ds(pl.multiple_of(start + piece * BLOCK, BLOCK), BLOCK)


def own_trial_kernel(head_block, tail_block, head_local, tail_local, price, flow, cost, trial):
    first = pl.program_id(1) * (CHUNK // BLOCK)

    def step(o, carry):
        for i in range(UNROLL * QUADS):
            owner = o * UNROLL + i // QUADS
            q = i % QUADS
            j = first + owner * QUADS + q
            head = jnp.broadcast_to(head_local[pl.ds(j, 1), :], (8, BLOCK))
            tail = jnp.broadcast_to(tail_local[pl.ds(j, 1), :], (8, BLOCK))
            at_head = jnp.take_along_axis(price[:, node_slice(head_block[j])], head, axis=1)
            at_tail = jnp.take_along_axis(price[:, node_slice(tail_block[j])], tail, axis=1)
            where = arc_slice(owner * OWN, q)
            trial[owner, :, q * BLOCK : (q + 1) * BLOCK] = flow[:, where] - step_primal * (
                cost[:, where] - (at_head - at_tail)
            )
        return carry

    lax.fori_loop(0, CHUNK // OWN // UNROLL, step, 0)


def flow_views(pairs):
    return [(pairs[0], 0), (pairs[1], 0), (pairs[2], 0), (pairs[4], 0)]


def cost_views(pairs):
    return [(pairs[0], 8), (pairs[1], 8), (pairs[3], 0), (pairs[4], 8)]


def trial_of(blocks, locals_, price, flow, cost, k, j, where):
    head = jnp.broadcast_to(locals_[k][pl.ds(j, 1), :], (8, BLOCK))
    tail = jnp.broadcast_to(locals_[k][pl.ds(BLOCK + j, 1), :], (8, BLOCK))
    at_head = jnp.take_along_axis(price[:, node_slice(blocks[2 * k, j])], head, axis=1)
    at_tail = jnp.take_along_axis(price[:, node_slice(blocks[2 * k + 1, j])], tail, axis=1)
    return rows_at(flow[k], where) - step_primal * (rows_at(cost[k], where) - (at_head - at_tail))


def fill_trial(part, blocks, locals_, price, flow, cost, trial):
    for k in range(SHARDS):
        shard = (part[0] - k) & (SHARDS - 1)

        def step(o, carry):
            for u in range(UNROLL):
                owner = o * UNROLL + u
                for q in range(QUADS):
                    trial[owner * SHARDS + shard, :, q * BLOCK : (q + 1) * BLOCK] = trial_of(
                        blocks, locals_, price, flow, cost, k, owner * QUADS + q, arc_slice(owner * OWN, q)
                    )
            return carry

        lax.fori_loop(0, OWNERS // UNROLL, step, 0)


def project_kernel(levels, classes, values, theta_out, *fresh_out):
    cls = classes[...]
    capacity = jnp.zeros((QUADS, BLOCK), f32)
    for k in range(8):
        capacity = jnp.where(cls == k, levels[k], capacity)
    caps = [capacity[q : q + 1] for q in range(QUADS)]
    thetas = [jnp.zeros((1, BLOCK), f32) for q in range(QUADS)]
    groups = values.shape[0]
    for inner in range(NEWTON):
        wide = [jnp.broadcast_to(t, (8, BLOCK)) for t in thetas]

        def step(o, carry):
            out = list(carry)
            for u in range(8):
                for q in range(QUADS):
                    excess = jnp.maximum(values[o * 8 + u, :, q * BLOCK : (q + 1) * BLOCK] - wide[q], 0.0)
                    out[2 * q] = out[2 * q] + excess
                    out[2 * q + 1] = out[2 * q + 1] + jnp.minimum(excess * (1.0 / soft_width), 1.0)
            return tuple(out)

        sums = lax.fori_loop(0, groups // 8, step, tuple(jnp.zeros((8, BLOCK), f32) for _ in range(2 * QUADS)))
        for q in range(QUADS):
            total = jnp.sum(sums[2 * q], axis=0, keepdims=True)
            active = jnp.sum(sums[2 * q + 1], axis=0, keepdims=True)
            thetas[q] = thetas[q] + jnp.maximum(total - caps[q], 0.0) / jnp.maximum(active, 1.0)
    tile = jnp.concatenate(thetas, axis=0)

    def store(i, carry):
        theta_out[i] = tile
        return carry

    lax.fori_loop(0, theta_out.shape[0], store, 0, unroll=8)
    if fresh_out:
        wide = [jnp.broadcast_to(t, (8, BLOCK)) for t in thetas]

        def keep(o, carry):
            for u in range(8):
                for q in range(QUADS):
                    where = slice(q * BLOCK, (q + 1) * BLOCK)
                    fresh_out[0][o * 8 + u, :, where] = jnp.maximum(values[o * 8 + u, :, where] - wide[q], 0.0)
            return carry

        lax.fori_loop(0, groups // 8, keep, 0)


def step_kernel(part, blocks, *refs, first, last):
    locals_, theta, price, demand = refs[:4], refs[4], refs[5], refs[6]
    balance, rest = refs[-1], refs[7:-1]
    if first:
        flow, cost, rest = flow_views(rest[:5]), cost_views(rest[:5]), rest[5:]
    else:
        trial, flow, rest = rest[0], [(ref, 0) for ref in rest[1 : 1 + SHARDS]], rest[1 + SHARDS :]
        if not last:
            cost, rest = cost_views(rest[:5]), rest[5:]
    if last:
        halves = rest
    else:
        following, price_out, fresh_out = rest[0], rest[1], rest[2:6]
    balance[...] = jnp.zeros_like(balance)
    lanes = lax.broadcasted_iota(jnp.int32, (BLOCK, BLOCK), 0).astype(jnp.int16)
    one = jnp.ones((), bf16)
    zero = jnp.zeros((), bf16)

    def table(local):
        return jnp.where(lanes == jnp.broadcast_to(local.astype(jnp.int16), (BLOCK, BLOCK)), one, zero)

    for k in range(SHARDS):
        shard = (part[0] - k) & (SHARDS - 1)

        def step(o, carry):
            found = []
            for u in range(UNROLL):
                owner = o * UNROLL + u
                start = owner * OWN
                for q in range(QUADS):
                    j = owner * QUADS + q
                    where = arc_slice(start, q)
                    limit = theta[owner * SHARDS + shard, q : q + 1, :]
                    if first:
                        wanted = trial_of(blocks, locals_, price, flow, cost, k, j, where)
                    else:
                        wanted = trial[owner * SHARDS + shard, :, q * BLOCK : (q + 1) * BLOCK]
                    fresh = jnp.maximum(wanted - limit, 0.0)
                    if not last:
                        fresh_out[k][:, where] = fresh
                    extra = 2.0 * fresh - rows_at(flow[k], where)
                    high = extra.astype(bf16)
                    low = (extra - high.astype(f32)).astype(bf16)
                    both = jnp.concatenate([high, low], axis=0)
                    tables = jnp.concatenate(
                        [table(locals_[k][pl.ds(j, 1), :]), table(locals_[k][pl.ds(BLOCK + j, 1), :])], axis=0
                    )
                    sums = lax.dot_general(both, tables, (((1,), (1,)), ((), ())), preferred_element_type=f32)
                    found.append((j, sums[:8] + sums[8:]))
            for j, sums in found:
                balance[:, node_slice(blocks[2 * k, j])] += sums[:, :BLOCK]
                balance[:, node_slice(blocks[2 * k + 1, j])] -= sums[:, BLOCK:]
            return carry

        lax.fori_loop(0, OWNERS // UNROLL, step, 0)
    if last:
        half = NODES // 2
        for i in range(2):
            where = slice(i * half, (i + 1) * half)
            halves[i][...] = price[:, where] + step_dual * (demand[:, where] - balance[:, where])
    else:
        price_out[...] = price[...] + step_dual * (demand[...] - balance[...])
        fill_trial(part, blocks, locals_, price_out, [(ref, 0) for ref in fresh_out], cost, following)


def pack_kernel(part, *refs):
    flow, cost, ids = refs[:SHARDS], refs[SHARDS : 2 * SHARDS], refs[2 * SHARDS : 2 * SHARDS + 4]
    own, near, far_flow, far_cost, back, packed = refs[2 * SHARDS + 4 :]
    for k, out in ((0, own), (1, near), (3, back)):
        out[:8] = flow[k][...]
        out[8:] = cost[k][...]
    far_flow[...] = flow[2][...]
    far_cost[...] = cost[2][...]
    packed[:BLOCK] = ids[0][...]
    packed[BLOCK : 2 * BLOCK] = ids[1][...]
    packed[2 * BLOCK : 2 * BLOCK + 1] = ids[2][...]
    packed[2 * BLOCK + 1 : 2 * BLOCK + 2] = ids[3][...]
    packed[2 * BLOCK + 2 :] = jnp.zeros((6, BLOCK), jnp.int32)


def pack(part, flow, cost, ids):
    def rows(k):
        return pl.BlockSpec((8, CHUNK), lambda c, part: ((part[0] + k) & (SHARDS - 1), c))

    def whole(x):
        return pl.BlockSpec(x.shape, lambda c, part: (0, 0))

    def out(count):
        return pl.BlockSpec((count, CHUNK), lambda c, part: (0, c))

    width = OWNERS * OWN
    counts = [16, 16, 8, 8, 16]
    packed = jax.ShapeDtypeStruct((2 * BLOCK + 8, BLOCK), jnp.int32)
    return pl.pallas_call(
        pack_kernel,
        grid_spec=pltpu.PrefetchScalarGridSpec(
            num_scalar_prefetch=1,
            grid=(width // CHUNK,),
            in_specs=[rows(k) for k in range(SHARDS)] * 2 + [whole(x) for x in ids],
            out_specs=[out(count) for count in counts] + [whole(packed)],
        ),
        out_shape=[jax.ShapeDtypeStruct((count, width), f32) for count in counts] + [packed],
        compiler_params=params(52),
        name="pack",
    )(part, *in_hbm([flow] * SHARDS + [cost] * SHARDS + ids))


def own_trial(head_block, tail_block, head_local, tail_local, price, flow, cost):
    whole = pl.BlockSpec((BLOCK, BLOCK), lambda r, c: (0, 0))
    return pl.pallas_call(
        own_trial_kernel,
        grid=(SHARDS, OWNERS * OWN // CHUNK),
        in_specs=[
            smem,
            smem,
            whole,
            whole,
            pl.BlockSpec((8, NODES), lambda r, c: (r, 0)),
            pl.BlockSpec((8, CHUNK), lambda r, c: (r, c)),
            pl.BlockSpec((8, CHUNK), lambda r, c: (r, c)),
        ],
        out_specs=pl.BlockSpec((CHUNK // OWN, 8, OWN), lambda r, c: (c, r, 0)),
        out_shape=jax.ShapeDtypeStruct((OWNERS, SHARDS * 8, OWN), f32),
        compiler_params=params(52),
        name="own_trial",
    )(*in_hbm([head_block, tail_block, head_local, tail_local, price, flow, cost]))


def project(levels, classes, values, last):
    shape = [jax.ShapeDtypeStruct((SHARDS * OWNERS, QUADS, BLOCK), f32)]
    if last:
        shape.append(jax.ShapeDtypeStruct(values.shape, f32))
    return pl.pallas_call(
        project_kernel,
        in_specs=[smem, vmem, vmem],
        out_specs=[vmem] * len(shape),
        out_shape=shape,
        compiler_params=params(8),
        name="project",
    )(levels, classes, values)


def in_hbm(values):
    return [pltpu.with_memory_space_constraint(x, pltpu.HBM) for x in values]


def advance(part, blocks, locals_, trial, theta, flow, price, demand, flow_cost, first, last):
    if first:
        operands = [theta, *in_hbm([price, demand]), *flow_cost]
    elif last:
        operands = [theta, *in_hbm([price, demand, trial, *flow])]
    else:
        operands = [theta, price, demand, trial, *flow, *flow_cost]
    shape = [jax.ShapeDtypeStruct((8, NODES // 2), f32)] * 2 if last else [jax.ShapeDtypeStruct((8, NODES), f32)]
    if not last:
        shape = [jax.ShapeDtypeStruct((OWNERS * SHARDS, 8, OWN), f32)] + shape
        shape = shape + [jax.ShapeDtypeStruct((8, OWNERS * OWN), f32)] * SHARDS
    out = pl.pallas_call(
        functools.partial(step_kernel, first=first, last=last),
        in_specs=[smem, smem] + [vmem] * (SHARDS + len(operands)),
        out_specs=[vmem] * len(shape),
        out_shape=shape,
        scratch_shapes=[pltpu.VMEM((8, NODES), f32)],
        compiler_params=params(14),
        cost_estimate=pl.CostEstimate(flops=2 * 16 * 256 * OWNERS * OWN * SHARDS, transcendentals=0, bytes_accessed=COVER),
        name="step",
    )(part, blocks, *locals_, *operands)
    return (None, out, None) if last else (out[0], out[1], out[2:])


def assemble_kernel(part, *refs):
    halves, out = refs[:-1], refs[-1]
    half = NODES // 2

    def rows(k):
        return pl.ds(pl.multiple_of(((part[0] - k) & (SHARDS - 1)) * 8, 8), 8)

    for i, k in enumerate((0, 1, 3)):
        out[rows(k), :half] = halves[2 * i][...]
        out[rows(k), half:] = halves[2 * i + 1][...]
    out[rows(2), :] = jnp.zeros((8, NODES), f32)


def assemble(part, *pieces):
    return pl.pallas_call(
        assemble_kernel,
        in_specs=[smem] + [vmem] * len(pieces),
        out_specs=vmem,
        out_shape=jax.ShapeDtypeStruct((SHARDS * 8, NODES), f32),
        compiler_params=params(52),
        name="assemble",
    )(part, *pieces)


def complete_kernel(part, west, east, whole, out):
    del part, whole

    @pl.when(pl.program_id(0) == 0)
    def _():
        out[...] = west[...]

    @pl.when(pl.program_id(0) == 1)
    def _():
        out[...] = east[...]


def complete(part, west, east, whole):
    half = NODES // 2
    return pl.pallas_call(
        complete_kernel,
        grid_spec=pltpu.PrefetchScalarGridSpec(
            num_scalar_prefetch=1,
            grid=(2,),
            in_specs=[pl.BlockSpec((8, half), lambda i, part: (0, 0))] * 2 + [pl.BlockSpec(memory_space=pl.ANY)],
            out_specs=pl.BlockSpec((8, half), lambda i, part: ((part[0] + 2) & (SHARDS - 1), i)),
        ),
        out_shape=jax.ShapeDtypeStruct(whole.shape, f32),
        input_output_aliases={3: 0},
        compiler_params=params(8),
        name="complete",
    )(part, west, east, whole)


def on_device(
    flow_start,
    price_start,
    cost,
    demand,
    head_block,
    tail_block,
    head_local,
    tail_local,
    cap_class,
    cap_levels,
):
    com_rows, arc_cols = flow_start.shape
    part = lax.axis_index("arc")
    place = lax.axis_index("com")
    blocks = arc_cols // BLOCK
    head_rows = head_local.reshape(blocks, BLOCK)
    tail_rows = tail_local.reshape(blocks, BLOCK)
    everyone = ("com", "arc")

    def exchange(values, axes):
        return lax.all_to_all(values, axes, split_axis=0, concat_axis=0, tiled=True)

    def around(values, k):
        return lax.ppermute(values, "arc", [(i, (i + k) % SHARDS) for i in range(SHARDS)])

    def rows_of(values, k):
        return lax.dynamic_slice(values, (((part + k) & (SHARDS - 1)) * 8, 0), (8, values.shape[1]))

    own = part.astype(jnp.int32).reshape(1)
    ids = [head_rows, tail_rows, head_block.reshape(1, BLOCK), tail_block.reshape(1, BLOCK)]
    pieces = pack(own, flow_start, cost, ids)
    pieces, flow_start, cost, price_start = lax.optimization_barrier((pieces, flow_start, cost, price_start))
    here, near, far_flow, far_cost, behind, packed = pieces
    far_flow = around(far_flow, 1)
    far_cost = around(far_cost, 3)
    first = own_trial(head_block, tail_block, head_rows, tail_rows, price_start, flow_start, cost)
    values = exchange(first, "com").reshape(OWNERS * SHARDS, 8, OWN)
    far_flow, far_cost, packed, near, behind = lax.optimization_barrier((far_flow, far_cost, packed, near, behind))
    far_flow = around(far_flow, 1)
    far_cost = around(far_cost, 3)
    near = around(near, 1)
    behind = around(behind, 3)
    locals_ = [packed] + [around(packed, k) for k in range(1, SHARDS)]
    values, far_flow, far_cost, locals_ = lax.optimization_barrier((values, far_flow, far_cost, locals_))
    flow_cost = [here, near, far_flow, far_cost, behind]
    block_ids = jnp.concatenate([x[2 * blocks : 2 * blocks + 2] for x in locals_], axis=0)
    price = rows_of(price_start, 0)
    wanted = rows_of(demand, 0)
    classes = lax.dynamic_slice(cap_class.reshape(blocks, BLOCK), (place * QUADS, 0), (QUADS, BLOCK))

    trial = flow = None
    for step in range(ITERS):
        last = step == ITERS - 1
        if step > 0:
            values = exchange(trial, everyone)
        theta, *kept = project(cap_levels, classes, values, last)
        theta = exchange(theta, everyone)
        trial, price, flow = advance(own, block_ids, locals_, trial, theta, flow, price, wanted, flow_cost, step == 0, last)
    back = exchange(kept[0].reshape(OWNERS, com_rows, OWN), "com")
    out = back.transpose(1, 0, 2).reshape(com_rows, arc_cols)
    west, east = price
    left_west, right_east = around(west, 1), around(east, 3)
    left_east, right_west = around(east, 1), around(west, 3)
    far_west, far_east = around(left_west, 1), around(right_east, 3)
    whole = assemble(own, west, east, left_west, left_east, right_west, right_east)
    out, whole, far_west, far_east = lax.optimization_barrier((out, whole, far_west, far_east))
    return out, complete(own, far_west, far_east, whole)


def solution(mesh):
    return jax.shard_map(
        on_device,
        mesh=mesh,
        in_specs=(
            P("com", "arc"),
            P("com", None),
            P("com", "arc"),
            P("com", None),
            P("arc"),
            P("arc"),
            P("arc"),
            P("arc"),
            P("arc"),
            P(),
        ),
        out_specs=(P("com", "arc"), P("com", None)),
        check_vma=False,
    )
```

```python
import functools

import jax
import jax.numpy as jnp
from jax import lax
from jax.experimental import pallas as pl
from jax.experimental.pallas import tpu as pltpu
from jax.sharding import PartitionSpec as P

NODES = 16384
BLOCK = 128
ITERS = 4
NEWTON = 3

step_primal = 0.25
step_dual = 0.1
soft_width = 0.05

SHARDS = 4
OWNERS = 32
OWN = 512
QUADS = OWN // BLOCK
CHUNK = 8192
UNROLL = 8
COVER = 40_000_000

f32 = jnp.float32
bf16 = jnp.bfloat16
narrow = jnp.float8_e4m3fn
PART = 32
PARTS = 16
vmem = pl.BlockSpec(memory_space=pltpu.VMEM)
smem = pl.BlockSpec(memory_space=pltpu.SMEM)


def params(mib):
    return pltpu.CompilerParams(vmem_limit_bytes=mib << 20)


def node_slice(block):
    return pl.ds(pl.multiple_of(block * BLOCK, BLOCK), BLOCK)


def rows_at(view, where):
    ref, start = view
    return ref[start : start + 8, where]


def arc_slice(start, piece):
    return pl.ds(pl.multiple_of(start + piece * BLOCK, BLOCK), BLOCK)


def own_trial_kernel(head_block, tail_block, head_local, tail_local, price, flow, cost, trial):
    first = pl.program_id(1) * (CHUNK // BLOCK)

    def step(o, carry):
        for i in range(UNROLL * QUADS):
            owner = o * UNROLL + i // QUADS
            q = i % QUADS
            j = first + owner * QUADS + q
            head = jnp.broadcast_to(head_local[pl.ds(j, 1), :], (8, BLOCK))
            tail = jnp.broadcast_to(tail_local[pl.ds(j, 1), :], (8, BLOCK))
            at_head = jnp.take_along_axis(price[:, node_slice(head_block[j])], head, axis=1)
            at_tail = jnp.take_along_axis(price[:, node_slice(tail_block[j])], tail, axis=1)
            where = arc_slice(owner * OWN, q)
            trial[owner, :, q * BLOCK : (q + 1) * BLOCK] = flow[:, where] - step_primal * (
                cost[:, where] - (at_head - at_tail)
            )
        return carry

    lax.fori_loop(0, CHUNK // OWN // UNROLL, step, 0)


def flow_views(pairs):
    return [(pairs[0], 0), (pairs[1], 0), (pairs[2], 0), (pairs[4], 0)]


def cost_views(pairs):
    return [(pairs[0], 8), (pairs[1], 8), (pairs[3], 0), (pairs[4], 8)]


def trial_of(blocks, locals_, price, flow, cost, k, j, where):
    head = jnp.broadcast_to(locals_[k][pl.ds(j, 1), :], (8, BLOCK))
    tail = jnp.broadcast_to(locals_[k][pl.ds(BLOCK + j, 1), :], (8, BLOCK))
    at_head = jnp.take_along_axis(price[:, node_slice(blocks[2 * k, j])], head, axis=1)
    at_tail = jnp.take_along_axis(price[:, node_slice(blocks[2 * k + 1, j])], tail, axis=1)
    return rows_at(flow[k], where) - step_primal * (rows_at(cost[k], where) - (at_head - at_tail))


def fill_trial(part, blocks, locals_, price, flow, cost, trial):
    for k in range(SHARDS):
        shard = (part[0] - k) & (SHARDS - 1)

        def step(o, carry):
            for u in range(UNROLL):
                owner = o * UNROLL + u
                for q in range(QUADS):
                    trial[owner * SHARDS + shard, :, q * BLOCK : (q + 1) * BLOCK] = trial_of(
                        blocks, locals_, price, flow, cost, k, owner * QUADS + q, arc_slice(owner * OWN, q)
                    )
            return carry

        lax.fori_loop(0, OWNERS // UNROLL, step, 0)


def project_kernel(levels, classes, values, theta_out, *fresh_out):
    cls = classes[...]
    capacity = jnp.zeros((QUADS, BLOCK), f32)
    for k in range(8):
        capacity = jnp.where(cls == k, levels[k], capacity)
    caps = [capacity[q : q + 1] for q in range(QUADS)]
    thetas = [jnp.zeros((1, BLOCK), f32) for q in range(QUADS)]
    groups = values.shape[0]
    for inner in range(NEWTON):
        wide = [jnp.broadcast_to(t, (8, BLOCK)) for t in thetas]

        def step(o, carry):
            out = list(carry)
            for u in range(8):
                for q in range(QUADS):
                    excess = jnp.maximum(values[o * 8 + u, :, q * BLOCK : (q + 1) * BLOCK] - wide[q], 0.0)
                    out[2 * q] = out[2 * q] + excess
                    out[2 * q + 1] = out[2 * q + 1] + jnp.minimum(excess * (1.0 / soft_width), 1.0)
            return tuple(out)

        sums = lax.fori_loop(0, groups // 8, step, tuple(jnp.zeros((8, BLOCK), f32) for _ in range(2 * QUADS)))
        for q in range(QUADS):
            total = jnp.sum(sums[2 * q], axis=0, keepdims=True)
            active = jnp.sum(sums[2 * q + 1], axis=0, keepdims=True)
            thetas[q] = thetas[q] + jnp.maximum(total - caps[q], 0.0) / jnp.maximum(active, 1.0)
    tile = jnp.concatenate(thetas, axis=0)

    def store(i, carry):
        theta_out[i] = tile
        return carry

    lax.fori_loop(0, theta_out.shape[0], store, 0, unroll=8)
    if fresh_out:
        wide = [jnp.broadcast_to(t, (8, BLOCK)) for t in thetas]

        def keep(o, carry):
            for u in range(8):
                for q in range(QUADS):
                    where = slice(q * BLOCK, (q + 1) * BLOCK)
                    fresh_out[0][o * 8 + u, :, where] = jnp.maximum(values[o * 8 + u, :, where] - wide[q], 0.0)
            return carry

        lax.fori_loop(0, groups // 8, keep, 0)


def ends_table(local, j):
    nodes = lax.broadcasted_iota(jnp.int32, (BLOCK, BLOCK), 0).astype(jnp.int16)
    one = jnp.ones((), bf16)
    zero = jnp.zeros((), bf16)

    def table(row):
        return jnp.where(nodes == jnp.broadcast_to(row.astype(jnp.int16), (BLOCK, BLOCK)), one, zero)

    return jnp.concatenate([table(local[pl.ds(j, 1), :]), table(local[pl.ds(BLOCK + j, 1), :])], axis=0)


def select_kernel(local, out):
    first = pl.program_id(1) * PART
    rows = lax.broadcasted_iota(jnp.int32, (BLOCK, BLOCK), 0)
    cols = lax.broadcasted_iota(jnp.int32, (BLOCK, BLOCK), 1)
    eye = jnp.where(rows == cols, 1.0, 0.0).astype(bf16)
    for i in range(PART):
        turned = lax.dot_general(
            eye, ends_table(local.at[0], first + i), (((1,), (1,)), ((), ())), preferred_element_type=f32
        )
        out[0, i] = turned.astype(narrow)


def select(local):
    steps = BLOCK // PART
    return pl.pallas_call(
        select_kernel,
        grid=(SHARDS, steps),
        in_specs=[pl.BlockSpec((1, 2 * BLOCK + 8, BLOCK), lambda k, c: (k, 0, 0))],
        out_specs=pl.BlockSpec((1, PART, BLOCK, 2 * BLOCK), lambda k, c: (k * steps + c, 0, 0, 0)),
        out_shape=jax.ShapeDtypeStruct((PARTS, PART, BLOCK, 2 * BLOCK), narrow),
        compiler_params=params(52),
        cost_estimate=pl.CostEstimate(flops=2 * PARTS * PART * BLOCK * BLOCK * 2 * BLOCK, transcendentals=0, bytes_accessed=COVER),
        name="select",
    )(local)


def step_kernel(part, blocks, *refs, first, last):
    locals_, theta, price, demand = refs[:4], refs[4], refs[5], refs[6]
    if first:
        balance, rest = refs[-1], refs[7:-1]
    else:
        stored, tables, arrived, balance, rest = refs[7], refs[-2], refs[-1], refs[-3], refs[8:-3]

        def piece(c):
            return pltpu.make_async_copy(stored.at[c], tables.at[c], arrived.at[c])

        for c in range(PARTS):
            piece(c).start()
    if first:
        flow, cost, rest = flow_views(rest[:5]), cost_views(rest[:5]), rest[5:]
    else:
        trial, flow, rest = rest[0], [(ref, 0) for ref in rest[1 : 1 + SHARDS]], rest[1 + SHARDS :]
        if not last:
            cost, rest = cost_views(rest[:5]), rest[5:]
    if last:
        halves = rest
    else:
        following, price_out, fresh_out = rest[0], rest[1], rest[2:6]
    balance[...] = jnp.zeros_like(balance)
    for k in range(SHARDS):
        shard = (part[0] - k) & (SHARDS - 1)

        def step(o, carry):
            if not first:
                piece(k * (OWNERS // UNROLL) + o).wait()
            found = []
            for u in range(UNROLL):
                owner = o * UNROLL + u
                start = owner * OWN
                for q in range(QUADS):
                    j = owner * QUADS + q
                    where = arc_slice(start, q)
                    limit = theta[owner * SHARDS + shard, q : q + 1, :]
                    if first:
                        wanted = trial_of(blocks, locals_, price, flow, cost, k, j, where)
                    else:
                        wanted = trial[owner * SHARDS + shard, :, q * BLOCK : (q + 1) * BLOCK]
                    fresh = jnp.maximum(wanted - limit, 0.0)
                    if not last:
                        fresh_out[k][:, where] = fresh
                    extra = 2.0 * fresh - rows_at(flow[k], where)
                    high = extra.astype(bf16)
                    low = (extra - high.astype(f32)).astype(bf16)
                    both = jnp.concatenate([high, low], axis=0)
                    if first:
                        sums = lax.dot_general(
                            both, ends_table(locals_[k], j), (((1,), (1,)), ((), ())), preferred_element_type=f32
                        )
                    else:
                        chosen = tables[k * (OWNERS // UNROLL) + o, u * QUADS + q].astype(bf16)
                        sums = lax.dot_general(both, chosen, (((1,), (0,)), ((), ())), preferred_element_type=f32)
                    found.append((j, sums[:8] + sums[8:]))
            for j, sums in found:
                balance[:, node_slice(blocks[2 * k, j])] += sums[:, :BLOCK]
                balance[:, node_slice(blocks[2 * k + 1, j])] -= sums[:, BLOCK:]
            return carry

        lax.fori_loop(0, OWNERS // UNROLL, step, 0)
    if last:
        half = NODES // 2
        for i in range(2):
            where = slice(i * half, (i + 1) * half)
            halves[i][...] = price[:, where] + step_dual * (demand[:, where] - balance[:, where])
    else:
        price_out[...] = price[...] + step_dual * (demand[...] - balance[...])
        fill_trial(part, blocks, locals_, price_out, [(ref, 0) for ref in fresh_out], cost, following)


def pack_kernel(part, *refs):
    flow, cost, ids = refs[:SHARDS], refs[SHARDS : 2 * SHARDS], refs[2 * SHARDS : 2 * SHARDS + 4]
    own, near, far_flow, far_cost, back, packed = refs[2 * SHARDS + 4 :]
    for k, out in ((0, own), (1, near), (3, back)):
        out[:8] = flow[k][...]
        out[8:] = cost[k][...]
    far_flow[...] = flow[2][...]
    far_cost[...] = cost[2][...]
    packed[:BLOCK] = ids[0][...]
    packed[BLOCK : 2 * BLOCK] = ids[1][...]
    packed[2 * BLOCK : 2 * BLOCK + 1] = ids[2][...]
    packed[2 * BLOCK + 1 : 2 * BLOCK + 2] = ids[3][...]
    packed[2 * BLOCK + 2 :] = jnp.zeros((6, BLOCK), jnp.int32)


def pack(part, flow, cost, ids):
    def rows(k):
        return pl.BlockSpec((8, CHUNK), lambda c, part: ((part[0] + k) & (SHARDS - 1), c))

    def whole(x):
        return pl.BlockSpec(x.shape, lambda c, part: (0, 0))

    def out(count):
        return pl.BlockSpec((count, CHUNK), lambda c, part: (0, c))

    width = OWNERS * OWN
    counts = [16, 16, 8, 8, 16]
    packed = jax.ShapeDtypeStruct((2 * BLOCK + 8, BLOCK), jnp.int32)
    return pl.pallas_call(
        pack_kernel,
        grid_spec=pltpu.PrefetchScalarGridSpec(
            num_scalar_prefetch=1,
            grid=(width // CHUNK,),
            in_specs=[rows(k) for k in range(SHARDS)] * 2 + [whole(x) for x in ids],
            out_specs=[out(count) for count in counts] + [whole(packed)],
        ),
        out_shape=[jax.ShapeDtypeStruct((count, width), f32) for count in counts] + [packed],
        compiler_params=params(52),
        name="pack",
    )(part, *in_hbm([flow] * SHARDS + [cost] * SHARDS + ids))


def own_rows_kernel(part, price, demand, price_out, demand_out):
    del part
    price_out[...] = price[...]
    demand_out[...] = demand[...]


def own_rows(part, price, demand):
    taken = pl.BlockSpec((8, CHUNK), lambda c, part: (part[0], c))
    kept = pl.BlockSpec((8, CHUNK), lambda c, part: (0, c))
    return pl.pallas_call(
        own_rows_kernel,
        grid_spec=pltpu.PrefetchScalarGridSpec(
            num_scalar_prefetch=1, grid=(NODES // CHUNK,), in_specs=[taken] * 2, out_specs=[kept] * 2
        ),
        out_shape=[jax.ShapeDtypeStruct((8, NODES), f32)] * 2,
        compiler_params=params(52),
        name="own_rows",
    )(part, *in_hbm([price, demand]))


def own_trial(head_block, tail_block, head_local, tail_local, price, flow, cost):
    whole = pl.BlockSpec((BLOCK, BLOCK), lambda r, c: (0, 0))
    return pl.pallas_call(
        own_trial_kernel,
        grid=(SHARDS, OWNERS * OWN // CHUNK),
        in_specs=[
            smem,
            smem,
            whole,
            whole,
            pl.BlockSpec((8, NODES), lambda r, c: (r, 0)),
            pl.BlockSpec((8, CHUNK), lambda r, c: (r, c)),
            pl.BlockSpec((8, CHUNK), lambda r, c: (r, c)),
        ],
        out_specs=pl.BlockSpec((CHUNK // OWN, 8, OWN), lambda r, c: (c, r, 0)),
        out_shape=jax.ShapeDtypeStruct((OWNERS, SHARDS * 8, OWN), f32),
        compiler_params=params(52),
        name="own_trial",
    )(*in_hbm([head_block, tail_block, head_local, tail_local, price, flow, cost]))


def project(levels, classes, values, last):
    shape = [jax.ShapeDtypeStruct((SHARDS * OWNERS, QUADS, BLOCK), f32)]
    if last:
        shape.append(jax.ShapeDtypeStruct(values.shape, f32))
    return pl.pallas_call(
        project_kernel,
        in_specs=[smem, vmem, vmem],
        out_specs=[vmem] * len(shape),
        out_shape=shape,
        compiler_params=params(8),
        name="project",
    )(levels, classes, values)


def in_hbm(values):
    return [pltpu.with_memory_space_constraint(x, pltpu.HBM) for x in values]


def advance(part, blocks, locals_, tables, trial, theta, flow, price, demand, flow_cost, step):
    first, last = step == 0, step == ITERS - 1
    if first:
        operands = [theta, *in_hbm([price, demand]), *flow_cost]
    elif last:
        operands = [theta, *in_hbm([price, demand, tables, trial, *flow])]
    elif step == 1:
        operands = [theta, *in_hbm([price, demand, tables, trial, *flow]), *flow_cost]
    else:
        operands = [theta, price, demand, *in_hbm([tables]), trial, *flow, *flow_cost]
    shape = [jax.ShapeDtypeStruct((8, NODES // 2), f32)] * 2 if last else [jax.ShapeDtypeStruct((8, NODES), f32)]
    if not last:
        shape = [jax.ShapeDtypeStruct((OWNERS * SHARDS, 8, OWN), f32)] + shape
        shape = shape + [jax.ShapeDtypeStruct((8, OWNERS * OWN), f32)] * SHARDS
    specs = [smem, smem] + [vmem] * (SHARDS + len(operands))
    scratch = [pltpu.VMEM((8, NODES), f32)]
    if not first:
        specs[2 + SHARDS + 3] = pl.BlockSpec(memory_space=pl.ANY)
        scratch += [pltpu.VMEM(tables.shape, narrow), pltpu.SemaphoreType.DMA((PARTS,))]
    out = pl.pallas_call(
        functools.partial(step_kernel, first=first, last=last),
        in_specs=specs,
        out_specs=[vmem] * len(shape),
        out_shape=shape,
        scratch_shapes=scratch,
        compiler_params=params(58 if first else 30),
        cost_estimate=pl.CostEstimate(flops=2 * 16 * 256 * OWNERS * OWN * SHARDS, transcendentals=0, bytes_accessed=COVER),
        name="step",
    )(part, blocks, *locals_, *operands)
    return (None, out, None) if last else (out[0], out[1], out[2:])


def assemble_kernel(part, *refs):
    halves, out = refs[:-1], refs[-1]
    half = NODES // 2

    def rows(k):
        return pl.ds(pl.multiple_of(((part[0] - k) & (SHARDS - 1)) * 8, 8), 8)

    for i, k in enumerate((0, 1, 3)):
        out[rows(k), :half] = halves[2 * i][...]
        out[rows(k), half:] = halves[2 * i + 1][...]
    out[rows(2), :] = jnp.zeros((8, NODES), f32)


def assemble(part, *pieces):
    return pl.pallas_call(
        assemble_kernel,
        in_specs=[smem] + [vmem] * len(pieces),
        out_specs=vmem,
        out_shape=jax.ShapeDtypeStruct((SHARDS * 8, NODES), f32),
        compiler_params=params(52),
        name="assemble",
    )(part, *pieces)


def complete_kernel(part, west, east, whole, out):
    del part, whole

    @pl.when(pl.program_id(0) == 0)
    def _():
        out[...] = west[...]

    @pl.when(pl.program_id(0) == 1)
    def _():
        out[...] = east[...]


def complete(part, west, east, whole):
    half = NODES // 2
    return pl.pallas_call(
        complete_kernel,
        grid_spec=pltpu.PrefetchScalarGridSpec(
            num_scalar_prefetch=1,
            grid=(2,),
            in_specs=[pl.BlockSpec((8, half), lambda i, part: (0, 0))] * 2 + [pl.BlockSpec(memory_space=pl.ANY)],
            out_specs=pl.BlockSpec((8, half), lambda i, part: ((part[0] + 2) & (SHARDS - 1), i)),
        ),
        out_shape=jax.ShapeDtypeStruct(whole.shape, f32),
        input_output_aliases={3: 0},
        compiler_params=params(8),
        name="complete",
    )(part, west, east, whole)


def on_device(
    flow_start,
    price_start,
    cost,
    demand,
    head_block,
    tail_block,
    head_local,
    tail_local,
    cap_class,
    cap_levels,
):
    com_rows, arc_cols = flow_start.shape
    part = lax.axis_index("arc")
    place = lax.axis_index("com")
    blocks = arc_cols // BLOCK
    head_rows = head_local.reshape(blocks, BLOCK)
    tail_rows = tail_local.reshape(blocks, BLOCK)
    everyone = ("com", "arc")

    def exchange(values, axes):
        return lax.all_to_all(values, axes, split_axis=0, concat_axis=0, tiled=True)

    def around(values, k):
        return lax.ppermute(values, "arc", [(i, (i + k) % SHARDS) for i in range(SHARDS)])

    own = part.astype(jnp.int32).reshape(1)
    ids = [head_rows, tail_rows, head_block.reshape(1, BLOCK), tail_block.reshape(1, BLOCK)]
    pieces = pack(own, flow_start, cost, ids)
    pieces, flow_start, cost, price_start = lax.optimization_barrier((pieces, flow_start, cost, price_start))
    here, near, far_flow, far_cost, behind, packed = pieces
    far_flow = around(far_flow, 1)
    far_cost = around(far_cost, 3)
    first = own_trial(head_block, tail_block, head_rows, tail_rows, price_start, flow_start, cost)
    first, far_flow, far_cost = lax.optimization_barrier((first, far_flow, far_cost))
    values = exchange(first, "com").reshape(OWNERS * SHARDS, 8, OWN)
    far_flow, far_cost, packed, near, behind = lax.optimization_barrier((far_flow, far_cost, packed, near, behind))
    far_flow = around(far_flow, 1)
    far_cost = around(far_cost, 3)
    locals_ = [packed] + [around(packed, k) for k in range(1, SHARDS)]
    locals_, far_flow, far_cost, near, behind = lax.optimization_barrier((locals_, far_flow, far_cost, near, behind))
    near = around(near, 1)
    behind = around(behind, 3)
    values, far_flow, far_cost, locals_ = lax.optimization_barrier((values, far_flow, far_cost, locals_))
    flow_cost = [here, near, far_flow, far_cost, behind]
    block_ids = jnp.concatenate([x[2 * blocks : 2 * blocks + 2] for x in locals_], axis=0)
    price, wanted = own_rows(own, price_start, demand)
    classes = lax.dynamic_slice(cap_class.reshape(blocks, BLOCK), (place * QUADS, 0), (QUADS, BLOCK))

    trial = flow = tables = None
    for step in range(ITERS):
        last = step == ITERS - 1
        if step > 0:
            values = exchange(trial, everyone)
        if step == 1:
            values, tables = lax.optimization_barrier((values, tables))
        theta, *kept = project(cap_levels, classes, values, last)
        theta = exchange(theta, everyone)
        trial, price, flow = advance(
            own, block_ids, locals_, tables, trial, theta, flow, price, wanted, flow_cost, step
        )
        if step == 0:
            trial, together = lax.optimization_barrier((trial, jnp.stack(locals_)))
            tables = select(together)
    back = exchange(kept[0].reshape(OWNERS, com_rows, OWN), "com")
    out = back.transpose(1, 0, 2).reshape(com_rows, arc_cols)
    west, east = price
    left_west, right_east = around(west, 1), around(east, 3)
    left_east, right_west = around(east, 1), around(west, 3)
    far_west, far_east = around(left_west, 1), around(right_east, 3)
    whole = assemble(own, west, east, left_west, left_east, right_west, right_east)
    out, whole, far_west, far_east = lax.optimization_barrier((out, whole, far_west, far_east))
    return out, complete(own, far_west, far_east, whole)


def solution(mesh):
    return jax.shard_map(
        on_device,
        mesh=mesh,
        in_specs=(
            P("com", "arc"),
            P("com", None),
            P("com", "arc"),
            P("com", None),
            P("arc"),
            P("arc"),
            P("arc"),
            P("arc"),
            P("arc"),
            P(),
        ),
        out_specs=(P("com", "arc"), P("com", None)),
        check_vma=False,
    )
```

```python
import functools

import jax
import jax.numpy as jnp
from jax import lax
from jax.experimental import pallas as pl
from jax.experimental.pallas import tpu as pltpu
from jax.sharding import PartitionSpec as P

NODES = 16384
BLOCK = 128
ITERS = 4
NEWTON = 3

step_primal = 0.25
step_dual = 0.1
soft_width = 0.05

SHARDS = 4
OWNERS = 32
OWN = 512
QUADS = OWN // BLOCK
CHUNK = 8192
UNROLL = 8
COVER = 40_000_000

f32 = jnp.float32
bf16 = jnp.bfloat16
narrow = jnp.float8_e4m3fn
PART = 32
PARTS = 16
vmem = pl.BlockSpec(memory_space=pltpu.VMEM)
smem = pl.BlockSpec(memory_space=pltpu.SMEM)


def params(mib):
    return pltpu.CompilerParams(vmem_limit_bytes=mib << 20)


def node_slice(block):
    return pl.ds(pl.multiple_of(block * BLOCK, BLOCK), BLOCK)


def rows_at(view, where):
    ref, start = view
    return ref[start : start + 8, where]


def arc_slice(start, piece):
    return pl.ds(pl.multiple_of(start + piece * BLOCK, BLOCK), BLOCK)


def own_trial_kernel(head_block, tail_block, head_local, tail_local, price, flow, cost, trial):
    first = pl.program_id(1) * (CHUNK // BLOCK)

    def step(o, carry):
        for i in range(UNROLL * QUADS):
            owner = o * UNROLL + i // QUADS
            q = i % QUADS
            j = first + owner * QUADS + q
            head = jnp.broadcast_to(head_local[pl.ds(j, 1), :], (8, BLOCK))
            tail = jnp.broadcast_to(tail_local[pl.ds(j, 1), :], (8, BLOCK))
            at_head = jnp.take_along_axis(price[:, node_slice(head_block[j])], head, axis=1)
            at_tail = jnp.take_along_axis(price[:, node_slice(tail_block[j])], tail, axis=1)
            where = arc_slice(owner * OWN, q)
            trial[owner, :, q * BLOCK : (q + 1) * BLOCK] = flow[:, where] - step_primal * (
                cost[:, where] - (at_head - at_tail)
            )
        return carry

    lax.fori_loop(0, CHUNK // OWN // UNROLL, step, 0)


def flow_views(pairs):
    return [(pairs[0], 0), (pairs[1], 0), (pairs[2], 0), (pairs[4], 0)]


def cost_views(pairs):
    return [(pairs[0], 8), (pairs[1], 8), (pairs[3], 0), (pairs[4], 8)]


def trial_of(blocks, locals_, price, flow, cost, k, j, where):
    head = jnp.broadcast_to(locals_[k][pl.ds(j, 1), :], (8, BLOCK))
    tail = jnp.broadcast_to(locals_[k][pl.ds(BLOCK + j, 1), :], (8, BLOCK))
    at_head = jnp.take_along_axis(price[:, node_slice(blocks[2 * k, j])], head, axis=1)
    at_tail = jnp.take_along_axis(price[:, node_slice(blocks[2 * k + 1, j])], tail, axis=1)
    return rows_at(flow[k], where) - step_primal * (rows_at(cost[k], where) - (at_head - at_tail))


def fill_trial(part, blocks, locals_, price, flow, cost, trial):
    for k in range(SHARDS):
        shard = (part[0] - k) & (SHARDS - 1)

        def step(o, carry):
            for u in range(UNROLL):
                owner = o * UNROLL + u
                for q in range(QUADS):
                    trial[owner * SHARDS + shard, :, q * BLOCK : (q + 1) * BLOCK] = trial_of(
                        blocks, locals_, price, flow, cost, k, owner * QUADS + q, arc_slice(owner * OWN, q)
                    )
            return carry

        lax.fori_loop(0, OWNERS // UNROLL, step, 0)


def project_kernel(levels, classes, values, theta_out, *fresh_out):
    cls = classes[...]
    capacity = jnp.zeros((QUADS, BLOCK), f32)
    for k in range(8):
        capacity = jnp.where(cls == k, levels[k], capacity)
    caps = [capacity[q : q + 1] for q in range(QUADS)]
    thetas = [jnp.zeros((1, BLOCK), f32) for q in range(QUADS)]
    groups = values.shape[0]
    for inner in range(NEWTON):
        wide = [jnp.broadcast_to(t, (8, BLOCK)) for t in thetas]

        def step(o, carry):
            out = list(carry)
            for u in range(8):
                for q in range(QUADS):
                    excess = jnp.maximum(values[o * 8 + u, :, q * BLOCK : (q + 1) * BLOCK] - wide[q], 0.0)
                    out[2 * q] = out[2 * q] + excess
                    out[2 * q + 1] = out[2 * q + 1] + jnp.minimum(excess * (1.0 / soft_width), 1.0)
            return tuple(out)

        sums = lax.fori_loop(0, groups // 8, step, tuple(jnp.zeros((8, BLOCK), f32) for _ in range(2 * QUADS)))
        for q in range(QUADS):
            total = jnp.sum(sums[2 * q], axis=0, keepdims=True)
            active = jnp.sum(sums[2 * q + 1], axis=0, keepdims=True)
            thetas[q] = thetas[q] + jnp.maximum(total - caps[q], 0.0) / jnp.maximum(active, 1.0)
    tile = jnp.concatenate(thetas, axis=0)

    def store(i, carry):
        theta_out[i] = tile
        return carry

    lax.fori_loop(0, theta_out.shape[0], store, 0, unroll=8)
    if fresh_out:
        wide = [jnp.broadcast_to(t, (8, BLOCK)) for t in thetas]

        def keep(o, carry):
            for u in range(8):
                for q in range(QUADS):
                    where = slice(q * BLOCK, (q + 1) * BLOCK)
                    fresh_out[0][o * 8 + u, :, where] = jnp.maximum(values[o * 8 + u, :, where] - wide[q], 0.0)
            return carry

        lax.fori_loop(0, groups // 8, keep, 0)


def ends_table(local, j):
    nodes = lax.broadcasted_iota(jnp.int32, (BLOCK, BLOCK), 0).astype(jnp.int16)
    one = jnp.ones((), bf16)
    zero = jnp.zeros((), bf16)

    def table(row):
        return jnp.where(nodes == jnp.broadcast_to(row.astype(jnp.int16), (BLOCK, BLOCK)), one, zero)

    return jnp.concatenate([table(local[pl.ds(j, 1), :]), table(local[pl.ds(BLOCK + j, 1), :])], axis=0)


def select_kernel(local, out):
    first = pl.program_id(1) * PART
    rows = lax.broadcasted_iota(jnp.int32, (BLOCK, BLOCK), 0)
    cols = lax.broadcasted_iota(jnp.int32, (BLOCK, BLOCK), 1)
    eye = jnp.where(rows == cols, 1.0, 0.0).astype(bf16)
    for i in range(PART):
        turned = lax.dot_general(
            eye, ends_table(local.at[0], first + i), (((1,), (1,)), ((), ())), preferred_element_type=f32
        )
        out[0, i] = turned.astype(narrow)


def select(local):
    steps = BLOCK // PART
    return pl.pallas_call(
        select_kernel,
        grid=(SHARDS, steps),
        in_specs=[pl.BlockSpec((1, 2 * BLOCK + 8, BLOCK), lambda k, c: (k, 0, 0))],
        out_specs=pl.BlockSpec((1, PART, BLOCK, 2 * BLOCK), lambda k, c: (k * steps + c, 0, 0, 0)),
        out_shape=jax.ShapeDtypeStruct((PARTS, PART, BLOCK, 2 * BLOCK), narrow),
        compiler_params=params(52),
        cost_estimate=pl.CostEstimate(flops=2 * PARTS * PART * BLOCK * BLOCK * 2 * BLOCK, transcendentals=0, bytes_accessed=COVER),
        name="select",
    )(local)


def step_kernel(part, blocks, *refs, first, last):
    locals_, theta, price, demand = refs[:4], refs[4], refs[5], refs[6]
    stored, tables, arrived, balance, rest = refs[7], refs[-2], refs[-1], refs[-3], refs[8:-3]

    def piece(c):
        return pltpu.make_async_copy(stored.at[c], tables.at[c], arrived.at[c])

    for c in range(PARTS):
        piece(c).start()
    if first:
        flow, cost, rest = flow_views(rest[:5]), cost_views(rest[:5]), rest[5:]
    else:
        trial, flow, rest = rest[0], [(ref, 0) for ref in rest[1 : 1 + SHARDS]], rest[1 + SHARDS :]
        if not last:
            cost, rest = cost_views(rest[:5]), rest[5:]
    if last:
        halves = rest
    else:
        following, price_out, fresh_out = rest[0], rest[1], rest[2:6]
    balance[...] = jnp.zeros_like(balance)
    for k in range(SHARDS):
        shard = (part[0] - k) & (SHARDS - 1)

        def step(o, carry):
            piece(k * (OWNERS // UNROLL) + o).wait()
            found = []
            for u in range(UNROLL):
                owner = o * UNROLL + u
                start = owner * OWN
                for q in range(QUADS):
                    j = owner * QUADS + q
                    where = arc_slice(start, q)
                    limit = theta[owner * SHARDS + shard, q : q + 1, :]
                    if first:
                        wanted = trial_of(blocks, locals_, price, flow, cost, k, j, where)
                    else:
                        wanted = trial[owner * SHARDS + shard, :, q * BLOCK : (q + 1) * BLOCK]
                    fresh = jnp.maximum(wanted - limit, 0.0)
                    if not last:
                        fresh_out[k][:, where] = fresh
                    extra = 2.0 * fresh - rows_at(flow[k], where)
                    high = extra.astype(bf16)
                    low = (extra - high.astype(f32)).astype(bf16)
                    both = jnp.concatenate([high, low], axis=0)
                    chosen = tables[k * (OWNERS // UNROLL) + o, u * QUADS + q].astype(bf16)
                    sums = lax.dot_general(both, chosen, (((1,), (0,)), ((), ())), preferred_element_type=f32)
                    found.append((j, sums[:8] + sums[8:]))
            for j, sums in found:
                balance[:, node_slice(blocks[2 * k, j])] += sums[:, :BLOCK]
                balance[:, node_slice(blocks[2 * k + 1, j])] -= sums[:, BLOCK:]
            return carry

        lax.fori_loop(0, OWNERS // UNROLL, step, 0)
    if last:
        half = NODES // 2
        for i in range(2):
            where = slice(i * half, (i + 1) * half)
            halves[i][...] = price[:, where] + step_dual * (demand[:, where] - balance[:, where])
    else:
        price_out[...] = price[...] + step_dual * (demand[...] - balance[...])
        fill_trial(part, blocks, locals_, price_out, [(ref, 0) for ref in fresh_out], cost, following)


def pack_kernel(part, *refs):
    flow, cost, ids = refs[:SHARDS], refs[SHARDS : 2 * SHARDS], refs[2 * SHARDS : 2 * SHARDS + 4]
    own, near, far_flow, far_cost, back, packed = refs[2 * SHARDS + 4 :]
    for k, out in ((0, own), (1, near), (3, back)):
        out[:8] = flow[k][...]
        out[8:] = cost[k][...]
    far_flow[...] = flow[2][...]
    far_cost[...] = cost[2][...]
    packed[:BLOCK] = ids[0][...]
    packed[BLOCK : 2 * BLOCK] = ids[1][...]
    packed[2 * BLOCK : 2 * BLOCK + 1] = ids[2][...]
    packed[2 * BLOCK + 1 : 2 * BLOCK + 2] = ids[3][...]
    packed[2 * BLOCK + 2 :] = jnp.zeros((6, BLOCK), jnp.int32)


def pack(part, flow, cost, ids):
    def rows(k):
        return pl.BlockSpec((8, CHUNK), lambda c, part: ((part[0] + k) & (SHARDS - 1), c))

    def whole(x):
        return pl.BlockSpec(x.shape, lambda c, part: (0, 0))

    def out(count):
        return pl.BlockSpec((count, CHUNK), lambda c, part: (0, c))

    width = OWNERS * OWN
    counts = [16, 16, 8, 8, 16]
    packed = jax.ShapeDtypeStruct((2 * BLOCK + 8, BLOCK), jnp.int32)
    return pl.pallas_call(
        pack_kernel,
        grid_spec=pltpu.PrefetchScalarGridSpec(
            num_scalar_prefetch=1,
            grid=(width // CHUNK,),
            in_specs=[rows(k) for k in range(SHARDS)] * 2 + [whole(x) for x in ids],
            out_specs=[out(count) for count in counts] + [whole(packed)],
        ),
        out_shape=[jax.ShapeDtypeStruct((count, width), f32) for count in counts] + [packed],
        compiler_params=params(52),
        name="pack",
    )(part, *in_hbm([flow] * SHARDS + [cost] * SHARDS + ids))


def own_trial(head_block, tail_block, head_local, tail_local, price, flow, cost):
    whole = pl.BlockSpec((BLOCK, BLOCK), lambda r, c: (0, 0))
    return pl.pallas_call(
        own_trial_kernel,
        grid=(SHARDS, OWNERS * OWN // CHUNK),
        in_specs=[
            smem,
            smem,
            whole,
            whole,
            pl.BlockSpec((8, NODES), lambda r, c: (r, 0)),
            pl.BlockSpec((8, CHUNK), lambda r, c: (r, c)),
            pl.BlockSpec((8, CHUNK), lambda r, c: (r, c)),
        ],
        out_specs=pl.BlockSpec((CHUNK // OWN, 8, OWN), lambda r, c: (c, r, 0)),
        out_shape=jax.ShapeDtypeStruct((OWNERS, SHARDS * 8, OWN), f32),
        compiler_params=params(52),
        name="own_trial",
    )(*in_hbm([head_block, tail_block, head_local, tail_local, price, flow, cost]))


def project(levels, classes, values, last):
    shape = [jax.ShapeDtypeStruct((SHARDS * OWNERS, QUADS, BLOCK), f32)]
    if last:
        shape.append(jax.ShapeDtypeStruct(values.shape, f32))
    return pl.pallas_call(
        project_kernel,
        in_specs=[smem, vmem, vmem],
        out_specs=[vmem] * len(shape),
        out_shape=shape,
        compiler_params=params(8),
        name="project",
    )(levels, classes, values)


def in_hbm(values):
    return [pltpu.with_memory_space_constraint(x, pltpu.HBM) for x in values]


def advance(part, blocks, locals_, tables, trial, theta, flow, price, demand, flow_cost, first, last):
    if first:
        operands = [theta, *in_hbm([price, demand, tables]), *flow_cost]
    elif last:
        operands = [theta, *in_hbm([price, demand, tables, trial, *flow])]
    else:
        operands = [theta, price, demand, *in_hbm([tables]), trial, *flow, *flow_cost]
    shape = [jax.ShapeDtypeStruct((8, NODES // 2), f32)] * 2 if last else [jax.ShapeDtypeStruct((8, NODES), f32)]
    if not last:
        shape = [jax.ShapeDtypeStruct((OWNERS * SHARDS, 8, OWN), f32)] + shape
        shape = shape + [jax.ShapeDtypeStruct((8, OWNERS * OWN), f32)] * SHARDS
    specs = [smem, smem] + [vmem] * (SHARDS + len(operands))
    specs[2 + SHARDS + 3] = pl.BlockSpec(memory_space=pl.ANY)
    scratch = [
        pltpu.VMEM((8, NODES), f32),
        pltpu.VMEM(tables.shape, narrow),
        pltpu.SemaphoreType.DMA((PARTS,)),
    ]
    out = pl.pallas_call(
        functools.partial(step_kernel, first=first, last=last),
        in_specs=specs,
        out_specs=[vmem] * len(shape),
        out_shape=shape,
        scratch_shapes=scratch,
        compiler_params=params(30),
        cost_estimate=pl.CostEstimate(flops=2 * 16 * 256 * OWNERS * OWN * SHARDS, transcendentals=0, bytes_accessed=COVER),
        name="step",
    )(part, blocks, *locals_, *operands)
    return (None, out, None) if last else (out[0], out[1], out[2:])


def assemble_kernel(part, *refs):
    halves, out = refs[:-1], refs[-1]
    half = NODES // 2

    def rows(k):
        return pl.ds(pl.multiple_of(((part[0] - k) & (SHARDS - 1)) * 8, 8), 8)

    for i, k in enumerate((0, 1, 3)):
        out[rows(k), :half] = halves[2 * i][...]
        out[rows(k), half:] = halves[2 * i + 1][...]
    out[rows(2), :] = jnp.zeros((8, NODES), f32)


def assemble(part, *pieces):
    return pl.pallas_call(
        assemble_kernel,
        in_specs=[smem] + [vmem] * len(pieces),
        out_specs=vmem,
        out_shape=jax.ShapeDtypeStruct((SHARDS * 8, NODES), f32),
        compiler_params=params(52),
        name="assemble",
    )(part, *pieces)


def complete_kernel(part, west, east, whole, out):
    del part, whole

    @pl.when(pl.program_id(0) == 0)
    def _():
        out[...] = west[...]

    @pl.when(pl.program_id(0) == 1)
    def _():
        out[...] = east[...]


def complete(part, west, east, whole):
    half = NODES // 2
    return pl.pallas_call(
        complete_kernel,
        grid_spec=pltpu.PrefetchScalarGridSpec(
            num_scalar_prefetch=1,
            grid=(2,),
            in_specs=[pl.BlockSpec((8, half), lambda i, part: (0, 0))] * 2 + [pl.BlockSpec(memory_space=pl.ANY)],
            out_specs=pl.BlockSpec((8, half), lambda i, part: ((part[0] + 2) & (SHARDS - 1), i)),
        ),
        out_shape=jax.ShapeDtypeStruct(whole.shape, f32),
        input_output_aliases={3: 0},
        compiler_params=params(8),
        name="complete",
    )(part, west, east, whole)


def on_device(
    flow_start,
    price_start,
    cost,
    demand,
    head_block,
    tail_block,
    head_local,
    tail_local,
    cap_class,
    cap_levels,
):
    com_rows, arc_cols = flow_start.shape
    part = lax.axis_index("arc")
    place = lax.axis_index("com")
    blocks = arc_cols // BLOCK
    head_rows = head_local.reshape(blocks, BLOCK)
    tail_rows = tail_local.reshape(blocks, BLOCK)
    everyone = ("com", "arc")

    def exchange(values, axes):
        return lax.all_to_all(values, axes, split_axis=0, concat_axis=0, tiled=True)

    def around(values, k):
        return lax.ppermute(values, "arc", [(i, (i + k) % SHARDS) for i in range(SHARDS)])

    def rows_of(values, k):
        return lax.dynamic_slice(values, (((part + k) & (SHARDS - 1)) * 8, 0), (8, values.shape[1]))

    own = part.astype(jnp.int32).reshape(1)
    ids = [head_rows, tail_rows, head_block.reshape(1, BLOCK), tail_block.reshape(1, BLOCK)]
    pieces = pack(own, flow_start, cost, ids)
    pieces, flow_start, cost, price_start = lax.optimization_barrier((pieces, flow_start, cost, price_start))
    here, near, far_flow, far_cost, behind, packed = pieces
    far_flow = around(far_flow, 1)
    far_cost = around(far_cost, 3)
    first = own_trial(head_block, tail_block, head_rows, tail_rows, price_start, flow_start, cost)
    values = exchange(first, "com").reshape(OWNERS * SHARDS, 8, OWN)
    far_flow, far_cost, packed, near, behind = lax.optimization_barrier((far_flow, far_cost, packed, near, behind))
    far_flow = around(far_flow, 1)
    far_cost = around(far_cost, 3)
    near = around(near, 1)
    behind = around(behind, 3)
    locals_ = [packed] + [around(packed, k) for k in range(1, SHARDS)]
    tables = select(jnp.stack(locals_))
    values, far_flow, far_cost, locals_, tables = lax.optimization_barrier((values, far_flow, far_cost, locals_, tables))
    flow_cost = [here, near, far_flow, far_cost, behind]
    block_ids = jnp.concatenate([x[2 * blocks : 2 * blocks + 2] for x in locals_], axis=0)
    price = rows_of(price_start, 0)
    wanted = rows_of(demand, 0)
    classes = lax.dynamic_slice(cap_class.reshape(blocks, BLOCK), (place * QUADS, 0), (QUADS, BLOCK))

    trial = flow = None
    for step in range(ITERS):
        last = step == ITERS - 1
        if step > 0:
            values = exchange(trial, everyone)
        theta, *kept = project(cap_levels, classes, values, last)
        theta = exchange(theta, everyone)
        trial, price, flow = advance(
            own, block_ids, locals_, tables, trial, theta, flow, price, wanted, flow_cost, step == 0, last
        )
    back = exchange(kept[0].reshape(OWNERS, com_rows, OWN), "com")
    out = back.transpose(1, 0, 2).reshape(com_rows, arc_cols)
    west, east = price
    left_west, right_east = around(west, 1), around(east, 3)
    left_east, right_west = around(east, 1), around(west, 3)
    far_west, far_east = around(left_west, 1), around(right_east, 3)
    whole = assemble(own, west, east, left_west, left_east, right_west, right_east)
    out, whole, far_west, far_east = lax.optimization_barrier((out, whole, far_west, far_east))
    return out, complete(own, far_west, far_east, whole)


def solution(mesh):
    return jax.shard_map(
        on_device,
        mesh=mesh,
        in_specs=(
            P("com", "arc"),
            P("com", None),
            P("com", "arc"),
            P("com", None),
            P("arc"),
            P("arc"),
            P("arc"),
            P("arc"),
            P("arc"),
            P(),
        ),
        out_specs=(P("com", "arc"), P("com", None)),
        check_vma=False,
    )
```

```python
import functools

import jax
import jax.numpy as jnp
from jax import lax
from jax.experimental import pallas as pl
from jax.experimental.pallas import tpu as pltpu
from jax.sharding import PartitionSpec as P

NODES = 16384
BLOCK = 128
ITERS = 4
NEWTON = 3

step_primal = 0.25
step_dual = 0.1
soft_width = 0.05

SHARDS = 4
OWNERS = 32
OWN = 512
QUADS = OWN // BLOCK
CHUNK = 8192
UNROLL = 8
COVER = 40_000_000

f32 = jnp.float32
bf16 = jnp.bfloat16
narrow = jnp.float8_e4m3fn
PART = 32
PARTS = 16
vmem = pl.BlockSpec(memory_space=pltpu.VMEM)
smem = pl.BlockSpec(memory_space=pltpu.SMEM)


def params(mib):
    return pltpu.CompilerParams(vmem_limit_bytes=mib << 20)


def node_slice(block):
    return pl.ds(pl.multiple_of(block * BLOCK, BLOCK), BLOCK)


def rows_at(view, where):
    ref, start = view
    return ref[start : start + 8, where]


def arc_slice(start, piece):
    return pl.ds(pl.multiple_of(start + piece * BLOCK, BLOCK), BLOCK)


def own_trial_kernel(head_block, tail_block, head_local, tail_local, price, flow, cost, trial):
    first = pl.program_id(1) * (CHUNK // BLOCK)

    def step(o, carry):
        for i in range(UNROLL * QUADS):
            owner = o * UNROLL + i // QUADS
            q = i % QUADS
            j = first + owner * QUADS + q
            head = jnp.broadcast_to(head_local[pl.ds(j, 1), :], (8, BLOCK))
            tail = jnp.broadcast_to(tail_local[pl.ds(j, 1), :], (8, BLOCK))
            at_head = jnp.take_along_axis(price[:, node_slice(head_block[j])], head, axis=1)
            at_tail = jnp.take_along_axis(price[:, node_slice(tail_block[j])], tail, axis=1)
            where = arc_slice(owner * OWN, q)
            trial[owner, :, q * BLOCK : (q + 1) * BLOCK] = flow[:, where] - step_primal * (
                cost[:, where] - (at_head - at_tail)
            )
        return carry

    lax.fori_loop(0, CHUNK // OWN // UNROLL, step, 0)


def flow_views(pairs):
    return [(pairs[0], 0), (pairs[1], 0), (pairs[2], 0), (pairs[4], 0)]


def cost_views(pairs):
    return [(pairs[0], 8), (pairs[1], 8), (pairs[3], 0), (pairs[4], 8)]


def trial_of(blocks, locals_, price, flow, cost, k, j, where):
    head = jnp.broadcast_to(locals_[k][pl.ds(j, 1), :], (8, BLOCK))
    tail = jnp.broadcast_to(locals_[k][pl.ds(BLOCK + j, 1), :], (8, BLOCK))
    at_head = jnp.take_along_axis(price[:, node_slice(blocks[2 * k, j])], head, axis=1)
    at_tail = jnp.take_along_axis(price[:, node_slice(blocks[2 * k + 1, j])], tail, axis=1)
    return rows_at(flow[k], where) - step_primal * (rows_at(cost[k], where) - (at_head - at_tail))


def fill_trial(part, blocks, locals_, price, flow, cost, trial):
    for k in range(SHARDS):
        shard = (part[0] - k) & (SHARDS - 1)

        def step(o, carry):
            for u in range(UNROLL):
                owner = o * UNROLL + u
                for q in range(QUADS):
                    trial[owner * SHARDS + shard, :, q * BLOCK : (q + 1) * BLOCK] = trial_of(
                        blocks, locals_, price, flow, cost, k, owner * QUADS + q, arc_slice(owner * OWN, q)
                    )
            return carry

        lax.fori_loop(0, OWNERS // UNROLL, step, 0)


def project_kernel(levels, classes, values, theta_out, *fresh_out):
    cls = classes[...]
    capacity = jnp.zeros((QUADS, BLOCK), f32)
    for k in range(8):
        capacity = jnp.where(cls == k, levels[k], capacity)
    caps = [capacity[q : q + 1] for q in range(QUADS)]
    thetas = [jnp.zeros((1, BLOCK), f32) for q in range(QUADS)]
    groups = values.shape[0]
    for inner in range(NEWTON):
        wide = [jnp.broadcast_to(t, (8, BLOCK)) for t in thetas]

        def step(o, carry):
            out = list(carry)
            for u in range(8):
                for q in range(QUADS):
                    excess = jnp.maximum(values[o * 8 + u, :, q * BLOCK : (q + 1) * BLOCK] - wide[q], 0.0)
                    out[2 * q] = out[2 * q] + excess
                    out[2 * q + 1] = out[2 * q + 1] + jnp.minimum(excess * (1.0 / soft_width), 1.0)
            return tuple(out)

        sums = lax.fori_loop(0, groups // 8, step, tuple(jnp.zeros((8, BLOCK), f32) for _ in range(2 * QUADS)))
        for q in range(QUADS):
            total = jnp.sum(sums[2 * q], axis=0, keepdims=True)
            active = jnp.sum(sums[2 * q + 1], axis=0, keepdims=True)
            thetas[q] = thetas[q] + jnp.maximum(total - caps[q], 0.0) / jnp.maximum(active, 1.0)
    tile = jnp.concatenate(thetas, axis=0)

    def store(i, carry):
        theta_out[i] = tile
        return carry

    lax.fori_loop(0, theta_out.shape[0], store, 0, unroll=8)
    if fresh_out:
        wide = [jnp.broadcast_to(t, (8, BLOCK)) for t in thetas]

        def keep(o, carry):
            for u in range(8):
                for q in range(QUADS):
                    where = slice(q * BLOCK, (q + 1) * BLOCK)
                    fresh_out[0][o * 8 + u, :, where] = jnp.maximum(values[o * 8 + u, :, where] - wide[q], 0.0)
            return carry

        lax.fori_loop(0, groups // 8, keep, 0)


def ends_table(local, j):
    nodes = lax.broadcasted_iota(jnp.int32, (BLOCK, BLOCK), 0).astype(jnp.int16)
    one = jnp.ones((), bf16)
    zero = jnp.zeros((), bf16)

    def table(row):
        return jnp.where(nodes == jnp.broadcast_to(row.astype(jnp.int16), (BLOCK, BLOCK)), one, zero)

    return jnp.concatenate([table(local[pl.ds(j, 1), :]), table(local[pl.ds(BLOCK + j, 1), :])], axis=0)


def select_kernel(local, out):
    first = pl.program_id(1) * PART
    rows = lax.broadcasted_iota(jnp.int32, (BLOCK, BLOCK), 0)
    cols = lax.broadcasted_iota(jnp.int32, (BLOCK, BLOCK), 1)
    eye = jnp.where(rows == cols, 1.0, 0.0).astype(bf16)
    for i in range(PART):
        turned = lax.dot_general(
            eye, ends_table(local.at[0], first + i), (((1,), (1,)), ((), ())), preferred_element_type=f32
        )
        out[0, i] = turned.astype(narrow)


def select(local):
    steps = BLOCK // PART
    return pl.pallas_call(
        select_kernel,
        grid=(SHARDS, steps),
        in_specs=[pl.BlockSpec((1, 2 * BLOCK + 8, BLOCK), lambda k, c: (k, 0, 0))],
        out_specs=pl.BlockSpec((1, PART, BLOCK, 2 * BLOCK), lambda k, c: (k * steps + c, 0, 0, 0)),
        out_shape=jax.ShapeDtypeStruct((PARTS, PART, BLOCK, 2 * BLOCK), narrow),
        compiler_params=params(52),
        cost_estimate=pl.CostEstimate(flops=2 * PARTS * PART * BLOCK * BLOCK * 2 * BLOCK, transcendentals=0, bytes_accessed=COVER),
        name="select",
    )(local)


def step_kernel(part, blocks, *refs, first, last):
    locals_, theta, price, demand = refs[:4], refs[4], refs[5], refs[6]
    stored, tables, arrived, balance, rest = refs[7], refs[-2], refs[-1], refs[-3], refs[8:-3]

    def piece(c):
        return pltpu.make_async_copy(stored.at[c], tables.at[c], arrived.at[c])

    for c in range(PARTS):
        piece(c).start()
    if first:
        flow, cost, rest = flow_views(rest[:5]), cost_views(rest[:5]), rest[5:]
    else:
        trial, flow, rest = rest[0], [(ref, 0) for ref in rest[1 : 1 + SHARDS]], rest[1 + SHARDS :]
        if not last:
            cost, rest = cost_views(rest[:5]), rest[5:]
    if last:
        halves = rest
    else:
        following, price_out, fresh_out = rest[0], rest[1], rest[2:6]
    balance[...] = jnp.zeros_like(balance)
    for k in range(SHARDS):
        shard = (part[0] - k) & (SHARDS - 1)

        def step(o, carry):
            piece(k * (OWNERS // UNROLL) + o).wait()
            found = []
            for u in range(UNROLL):
                owner = o * UNROLL + u
                start = owner * OWN
                for q in range(QUADS):
                    j = owner * QUADS + q
                    where = arc_slice(start, q)
                    limit = theta[owner * SHARDS + shard, q : q + 1, :]
                    if first:
                        wanted = trial_of(blocks, locals_, price, flow, cost, k, j, where)
                    else:
                        wanted = trial[owner * SHARDS + shard, :, q * BLOCK : (q + 1) * BLOCK]
                    fresh = jnp.maximum(wanted - limit, 0.0)
                    if not last:
                        fresh_out[k][:, where] = fresh
                    extra = 2.0 * fresh - rows_at(flow[k], where)
                    high = extra.astype(bf16)
                    low = (extra - high.astype(f32)).astype(bf16)
                    both = jnp.concatenate([high, low], axis=0)
                    chosen = tables[k * (OWNERS // UNROLL) + o, u * QUADS + q].astype(bf16)
                    sums = lax.dot_general(both, chosen, (((1,), (0,)), ((), ())), preferred_element_type=f32)
                    found.append((j, sums[:8] + sums[8:]))
            for j, sums in found:
                balance[:, node_slice(blocks[2 * k, j])] += sums[:, :BLOCK]
                balance[:, node_slice(blocks[2 * k + 1, j])] -= sums[:, BLOCK:]
            return carry

        lax.fori_loop(0, OWNERS // UNROLL, step, 0)
    if last:
        half = NODES // 2
        for i in range(2):
            where = slice(i * half, (i + 1) * half)
            halves[i][...] = price[:, where] + step_dual * (demand[:, where] - balance[:, where])
    else:
        price_out[...] = price[...] + step_dual * (demand[...] - balance[...])
        fill_trial(part, blocks, locals_, price_out, [(ref, 0) for ref in fresh_out], cost, following)


def pack_kernel(part, *refs):
    flow, cost, ids = refs[:SHARDS], refs[SHARDS : 2 * SHARDS], refs[2 * SHARDS : 2 * SHARDS + 4]
    own, near, far_flow, far_cost, back, packed = refs[2 * SHARDS + 4 :]
    for k, out in ((0, own), (1, near), (3, back)):
        out[:8] = flow[k][...]
        out[8:] = cost[k][...]
    far_flow[...] = flow[2][...]
    far_cost[...] = cost[2][...]
    packed[:BLOCK] = ids[0][...]
    packed[BLOCK : 2 * BLOCK] = ids[1][...]
    packed[2 * BLOCK : 2 * BLOCK + 1] = ids[2][...]
    packed[2 * BLOCK + 1 : 2 * BLOCK + 2] = ids[3][...]
    packed[2 * BLOCK + 2 :] = jnp.zeros((6, BLOCK), jnp.int32)


def pack(part, flow, cost, ids):
    def rows(k):
        return pl.BlockSpec((8, CHUNK), lambda c, part: ((part[0] + k) & (SHARDS - 1), c))

    def whole(x):
        return pl.BlockSpec(x.shape, lambda c, part: (0, 0))

    def out(count):
        return pl.BlockSpec((count, CHUNK), lambda c, part: (0, c))

    width = OWNERS * OWN
    counts = [16, 16, 8, 8, 16]
    packed = jax.ShapeDtypeStruct((2 * BLOCK + 8, BLOCK), jnp.int32)
    return pl.pallas_call(
        pack_kernel,
        grid_spec=pltpu.PrefetchScalarGridSpec(
            num_scalar_prefetch=1,
            grid=(width // CHUNK,),
            in_specs=[rows(k) for k in range(SHARDS)] * 2 + [whole(x) for x in ids],
            out_specs=[out(count) for count in counts] + [whole(packed)],
        ),
        out_shape=[jax.ShapeDtypeStruct((count, width), f32) for count in counts] + [packed],
        compiler_params=params(52),
        name="pack",
    )(part, *in_hbm([flow] * SHARDS + [cost] * SHARDS + ids))


def own_trial(head_block, tail_block, head_local, tail_local, price, flow, cost):
    whole = pl.BlockSpec((BLOCK, BLOCK), lambda r, c: (0, 0))
    return pl.pallas_call(
        own_trial_kernel,
        grid=(SHARDS, OWNERS * OWN // CHUNK),
        in_specs=[
            smem,
            smem,
            whole,
            whole,
            pl.BlockSpec((8, NODES), lambda r, c: (r, 0)),
            pl.BlockSpec((8, CHUNK), lambda r, c: (r, c)),
            pl.BlockSpec((8, CHUNK), lambda r, c: (r, c)),
        ],
        out_specs=pl.BlockSpec((CHUNK // OWN, 8, OWN), lambda r, c: (c, r, 0)),
        out_shape=jax.ShapeDtypeStruct((OWNERS, SHARDS * 8, OWN), f32),
        compiler_params=params(52),
        name="own_trial",
    )(*in_hbm([head_block, tail_block, head_local, tail_local, price, flow, cost]))


def project(levels, classes, values, last):
    shape = [jax.ShapeDtypeStruct((SHARDS * OWNERS, QUADS, BLOCK), f32)]
    if last:
        shape.append(jax.ShapeDtypeStruct(values.shape, f32))
    return pl.pallas_call(
        project_kernel,
        in_specs=[smem, vmem, vmem],
        out_specs=[vmem] * len(shape),
        out_shape=shape,
        compiler_params=params(8),
        name="project",
    )(levels, classes, values)


def in_hbm(values):
    return [pltpu.with_memory_space_constraint(x, pltpu.HBM) for x in values]


def advance(part, blocks, locals_, tables, trial, theta, flow, price, demand, flow_cost, first, last):
    if first:
        operands = [theta, *in_hbm([price, demand, tables, *flow_cost])]
    elif last:
        operands = [theta, *in_hbm([price, demand, tables, trial, *flow])]
    else:
        operands = [theta, price, demand, *in_hbm([tables]), trial, *flow, *flow_cost]
    shape = [jax.ShapeDtypeStruct((8, NODES // 2), f32)] * 2 if last else [jax.ShapeDtypeStruct((8, NODES), f32)]
    if not last:
        shape = [jax.ShapeDtypeStruct((OWNERS * SHARDS, 8, OWN), f32)] + shape
        shape = shape + [jax.ShapeDtypeStruct((8, OWNERS * OWN), f32)] * SHARDS
    specs = [smem, smem] + [vmem] * (SHARDS + len(operands))
    specs[2 + SHARDS + 3] = pl.BlockSpec(memory_space=pl.ANY)
    scratch = [
        pltpu.VMEM((8, NODES), f32),
        pltpu.VMEM(tables.shape, narrow),
        pltpu.SemaphoreType.DMA((PARTS,)),
    ]
    out = pl.pallas_call(
        functools.partial(step_kernel, first=first, last=last),
        in_specs=specs,
        out_specs=[vmem] * len(shape),
        out_shape=shape,
        scratch_shapes=scratch,
        compiler_params=params(30),
        cost_estimate=pl.CostEstimate(flops=2 * 16 * 256 * OWNERS * OWN * SHARDS, transcendentals=0, bytes_accessed=COVER),
        name="step",
    )(part, blocks, *locals_, *operands)
    return (None, out, None) if last else (out[0], out[1], out[2:])


def assemble_kernel(part, *refs):
    halves, out = refs[:-1], refs[-1]
    half = NODES // 2

    def rows(k):
        return pl.ds(pl.multiple_of(((part[0] - k) & (SHARDS - 1)) * 8, 8), 8)

    for i, k in enumerate((0, 1, 3)):
        out[rows(k), :half] = halves[2 * i][...]
        out[rows(k), half:] = halves[2 * i + 1][...]
    out[rows(2), :] = jnp.zeros((8, NODES), f32)


def assemble(part, *pieces):
    return pl.pallas_call(
        assemble_kernel,
        in_specs=[smem] + [vmem] * len(pieces),
        out_specs=vmem,
        out_shape=jax.ShapeDtypeStruct((SHARDS * 8, NODES), f32),
        compiler_params=params(52),
        name="assemble",
    )(part, *pieces)


def complete_kernel(part, west, east, whole, out):
    del part, whole

    @pl.when(pl.program_id(0) == 0)
    def _():
        out[...] = west[...]

    @pl.when(pl.program_id(0) == 1)
    def _():
        out[...] = east[...]


def complete(part, west, east, whole):
    half = NODES // 2
    return pl.pallas_call(
        complete_kernel,
        grid_spec=pltpu.PrefetchScalarGridSpec(
            num_scalar_prefetch=1,
            grid=(2,),
            in_specs=[pl.BlockSpec((8, half), lambda i, part: (0, 0))] * 2 + [pl.BlockSpec(memory_space=pl.ANY)],
            out_specs=pl.BlockSpec((8, half), lambda i, part: ((part[0] + 2) & (SHARDS - 1), i)),
        ),
        out_shape=jax.ShapeDtypeStruct(whole.shape, f32),
        input_output_aliases={3: 0},
        compiler_params=params(8),
        name="complete",
    )(part, west, east, whole)


def on_device(
    flow_start,
    price_start,
    cost,
    demand,
    head_block,
    tail_block,
    head_local,
    tail_local,
    cap_class,
    cap_levels,
):
    com_rows, arc_cols = flow_start.shape
    part = lax.axis_index("arc")
    place = lax.axis_index("com")
    blocks = arc_cols // BLOCK
    head_rows = head_local.reshape(blocks, BLOCK)
    tail_rows = tail_local.reshape(blocks, BLOCK)
    everyone = ("com", "arc")

    def exchange(values, axes):
        return lax.all_to_all(values, axes, split_axis=0, concat_axis=0, tiled=True)

    def around(values, k):
        return lax.ppermute(values, "arc", [(i, (i + k) % SHARDS) for i in range(SHARDS)])

    def rows_of(values, k):
        return lax.dynamic_slice(values, (((part + k) & (SHARDS - 1)) * 8, 0), (8, values.shape[1]))

    own = part.astype(jnp.int32).reshape(1)
    ids = [head_rows, tail_rows, head_block.reshape(1, BLOCK), tail_block.reshape(1, BLOCK)]
    pieces = pack(own, flow_start, cost, ids)
    pieces, flow_start, cost, price_start = lax.optimization_barrier((pieces, flow_start, cost, price_start))
    here, near, far_flow, far_cost, behind, packed = pieces
    far_flow = around(far_flow, 1)
    far_cost = around(far_cost, 3)
    first = own_trial(head_block, tail_block, head_rows, tail_rows, price_start, flow_start, cost)
    values = exchange(first, "com").reshape(OWNERS * SHARDS, 8, OWN)
    far_flow, far_cost, packed, near, behind = lax.optimization_barrier((far_flow, far_cost, packed, near, behind))
    far_flow = around(far_flow, 1)
    far_cost = around(far_cost, 3)
    near = around(near, 1)
    behind = around(behind, 3)
    locals_ = [packed] + [around(packed, k) for k in range(1, SHARDS)]
    tables = select(jnp.stack(locals_))
    values, far_flow, far_cost, locals_, tables = lax.optimization_barrier((values, far_flow, far_cost, locals_, tables))
    flow_cost = [here, near, far_flow, far_cost, behind]
    block_ids = jnp.concatenate([x[2 * blocks : 2 * blocks + 2] for x in locals_], axis=0)
    price = rows_of(price_start, 0)
    wanted = rows_of(demand, 0)
    classes = lax.dynamic_slice(cap_class.reshape(blocks, BLOCK), (place * QUADS, 0), (QUADS, BLOCK))

    trial = flow = None
    for step in range(ITERS):
        last = step == ITERS - 1
        if step > 0:
            values = exchange(trial, everyone)
        theta, *kept = project(cap_levels, classes, values, last)
        theta = exchange(theta, everyone)
        trial, price, flow = advance(
            own, block_ids, locals_, tables, trial, theta, flow, price, wanted, flow_cost, step == 0, last
        )
    back = exchange(kept[0].reshape(OWNERS, com_rows, OWN), "com")
    out = back.transpose(1, 0, 2).reshape(com_rows, arc_cols)
    west, east = price
    left_west, right_east = around(west, 1), around(east, 3)
    left_east, right_west = around(east, 1), around(west, 3)
    far_west, far_east = around(left_west, 1), around(right_east, 3)
    whole = assemble(own, west, east, left_west, left_east, right_west, right_east)
    out, whole, far_west, far_east = lax.optimization_barrier((out, whole, far_west, far_east))
    return out, complete(own, far_west, far_east, whole)


def solution(mesh):
    return jax.shard_map(
        on_device,
        mesh=mesh,
        in_specs=(
            P("com", "arc"),
            P("com", None),
            P("com", "arc"),
            P("com", None),
            P("arc"),
            P("arc"),
            P("arc"),
            P("arc"),
            P("arc"),
            P(),
        ),
        out_specs=(P("com", "arc"), P("com", None)),
        check_vma=False,
    )
```
